32 devices in a mesh: dp: 8 (over z, x), tensor: 4 (over y, core).
Axes of the slice: x: 2, y: 2, z: 4, core: 2. Of those that a mesh axis runs over, the one named last changes fastest.
Arguments:
- tokens: bfloat16 [16, 1024, 768], P('dp', 'tensor'), may hold values from -6 to 6
- segment_ids: int32 [16, 1024], P('dp'), may hold values from 0 to 7, never falling along the last dimension, each value on 1 to 512 neighbouring positions
- w_query: bfloat16 [768, 768], P('dp', 'tensor'), may hold values from -0.21875 to 0.21875
- w_key: bfloat16 [768, 768], P('dp', 'tensor'), may hold values from -0.21875 to 0.21875
- w_value: bfloat16 [768, 768], P('dp', 'tensor'), may hold values from -0.21875 to 0.21875
- w_out: bfloat16 [768, 768], P('tensor', 'dp'), may hold values from -1.75 to 1.75
- w_up: bfloat16 [768, 3072], P('dp', 'tensor'), may hold values from -0.21875 to 0.21875
- w_down: bfloat16 [3072, 768], P('tensor', 'dp'), may hold values from -0.109375 to 0.109375
- gain_attn: bfloat16 [768], P('dp'), may hold values from 0.25 to 1.75
- gain_mlp: bfloat16 [768], P('dp'), may hold values from 0.25 to 1.75
- cotangent: bfloat16 [16, 1024, 768], P('dp', 'tensor'), may hold values from -6 to 6
Outputs:
- output: float32 [16, 1024, 768], P('dp', 'tensor')
- input_grad: float32 [16, 1024, 768], P('dp', 'tensor')
- grad_query: float32 [768, 768], P('dp', 'tensor')
- grad_key: float32 [768, 768], P('dp', 'tensor')
- grad_value: float32 [768, 768], P('dp', 'tensor')
- grad_out: float32 [768, 768], P('tensor', 'dp')
- grad_up: float32 [768, 3072], P('dp', 'tensor')
- grad_down: float32 [3072, 768], P('tensor', 'dp')
- grad_gain_attn: float32 [768], P('dp')
- grad_gain_mlp: float32 [768], P('dp')
The draws below stay inside these ranges and needn't reach their ends.
Inputs may be any that keep to these rules, and one draw needn't show every extreme that they name: `segment_ids`: within a sequence the document numbers never fall, and each of the 8 documents holds 1 to 512 tokens.
All inputs are finite; a program needn't handle non-finite values.
Results may differ from the reference program's by a relative error of at most 0.017.
Values may be sent and summed in bfloat16 or wider, within the bound.
No kernel may reach another device: no remote copies, remote signals or barrier semaphores. Data moves between devices by JAX's collectives and lax.ppermute only.
A program may use at most 128 MiB of HBM per device.

```python
import math
import jax
import jax.numpy as jnp
import numpy as np
from jax import lax

D = 768
H = 12
HD = 64
FF = 3072
L = 1024
DOCS = 8
SEQS = 16


def levels(rng, shape, pieces, low, high):
    def one(dim, shards_of):
        draws = jax.random.uniform(jax.random.fold_in(jax.random.fold_in(rng, 6), dim), (shards_of,), jnp.float32, low / len(pieces), high / len(pieces))
        return jnp.repeat(jnp.exp(draws), shape[dim] // shards_of).reshape((-1,) + (1,) * (len(shape) - dim - 1))

    factor_of = one(*pieces[0])
    for cut in pieces[1:]:
        factor_of = factor_of * one(*cut)
    return factor_of


def split_up(count, total, limit, lean):
    portions = [(1 << 20) // math.isqrt(grade ** lean) + 1 for grade in range(2, count + 1)]
    surplus, counts = total - limit - (count - 1), [1] * (count - 1)
    while surplus > 0:
        free = [i for i in range(count - 1) if counts[i] < limit]
        pool, left = sum([portions[i] for i in free]), surplus
        for i in free:
            addition = min(limit - counts[i], max(1, left * portions[i] // pool), surplus)
            counts[i] = counts[i] + addition
            surplus = surplus - addition
    return np.array([limit] + counts)


def ragged_sizes(stream_key, number_of, total, limit, skew):
    if number_of == 2:
        one = jax.random.randint(stream_key, (), max(1, total - limit), min(limit, total - 1) + 1)
        return jnp.stack([one, total - one])
    lengths = jnp.asarray(split_up(number_of, total, limit, skew), jnp.int32)
    twos = (number_of - 1) // 2
    source_of, receiver = lengths[1:1 + 2 * twos:2], lengths[2:2 + 2 * twos:2]
    slack = jnp.minimum(source_of - 1, limit - receiver)
    shifted = jax.random.randint(jax.random.fold_in(stream_key, 1), (twos,), 0, 1 << 20) % (slack + 1)
    lengths = lengths.at[1:1 + 2 * twos:2].set(source_of - shifted).at[2:2 + 2 * twos:2].set(receiver + shifted)
    return lengths[jax.random.permutation(jax.random.fold_in(stream_key, 2), number_of)]


def gaussian(key, shape, width, most, pieces=(), held_as=jnp.bfloat16):
    result = jax.random.normal(key, shape, jnp.float32) * width
    if len(pieces) > 0:
        result = levels(key, shape, pieces, -0.22, 0.18) * result
    return jnp.clip(result, min=-most, max=most).astype(held_as)


def setup_inputs(seed: int = 0) -> dict:
    seeds = jax.random.split(jax.random.key(seed), 12)
    return {
        "tokens": gaussian(seeds[0], (SEQS, L, D), 1.0, 6.0, ((0, 8), (1, 4))),
        "segment_ids": jax.vmap(lambda own: jnp.searchsorted(jnp.cumsum(ragged_sizes(own, DOCS, L, L // 2, 2)), jnp.arange(L), side="right"))(jax.random.split(seeds[1], SEQS)).reshape((SEQS, L)).astype(jnp.int32),
        "w_query": gaussian(seeds[2], (D, D), D ** -0.5, 0.21875, ((0, 8), (1, 4))),
        "w_key": gaussian(seeds[3], (D, D), D ** -0.5, 0.21875, ((0, 8), (1, 4))),
        "w_value": gaussian(seeds[4], (D, D), D ** -0.5, 0.21875, ((0, 8), (1, 4))),
        "w_out": gaussian(seeds[5], (D, D), (D // 64) ** -0.5, 1.75, ((0, 4), (1, 8))),
        "w_up": gaussian(seeds[6], (D, FF), D ** -0.5, 0.21875, ((0, 8), (1, 4))),
        "w_down": gaussian(seeds[7], (FF, D), FF ** -0.5, 0.109375, ((0, 4), (1, 8))),
        "gain_attn": jnp.clip(1.0 + 0.15 * jax.random.normal(seeds[8], (D,), jnp.float32), 0.25, 1.75).astype(jnp.bfloat16),
        "gain_mlp": jnp.clip(1.0 + 0.15 * jax.random.normal(seeds[9], (D,), jnp.float32), 0.25, 1.75).astype(jnp.bfloat16),
        "cotangent": gaussian(seeds[10], (SEQS, L, D), 1.0, 6.0, ((0, 8), (1, 4))),
    }


@jax.custom_vjp
def low(v):
    return lax.optimization_barrier(v.astype(jnp.bfloat16)).astype(jnp.float32)

@jax.custom_vjp
def low_back(v):
    return v

def low_keep(v):
    return (low(v), None)

def low_pass(kept, grad):
    return (grad,)

def back_keep(v):
    return (v, None)

def back_low(kept, grad):
    return (low(grad),)
low.defvjp(low_keep, low_pass)
low_back.defvjp(back_keep, back_low)
eps = 1e-05
negative = -1e+30

def product(left, right):
    return jnp.dot(left, right, precision=lax.Precision.HIGHEST)

def normalize(stream, gain):
    center = stream - lax.optimization_barrier(jnp.mean(stream, axis=-1, keepdims=True))
    spread = lax.optimization_barrier(jnp.mean(center * center, axis=-1, keepdims=True))
    return center * lax.rsqrt(spread + eps) * gain

def residual_block(stream, segments, w_query, w_key, w_value, w_out, w_up, w_down, gain_attn, gain_mlp):
    length = stream.shape[0]
    normed = low(normalize(stream, gain_attn))
    queries = low(low_back(product(normed, w_query))).reshape(length, H, HD)
    key_rows = low(low_back(product(normed, w_key))).reshape(length, H, HD)
    value_rows = low(low_back(product(normed, w_value))).reshape(length, H, HD)
    scores = jnp.einsum('qhd,khd->hqk', queries, key_rows, precision=lax.Precision.HIGHEST) * HD ** (-0.5)
    places = jnp.arange(length)
    allowed = (places[:, None] >= places[None, :]) & (segments[:, None] == segments[None, :])
    scores = low_back(jnp.where(allowed[None], scores, negative))
    highest = lax.optimization_barrier(jnp.max(scores, axis=-1, keepdims=True))
    weights = jnp.exp(scores - highest)
    probabilities = low(weights / lax.optimization_barrier(jnp.sum(weights, axis=-1, keepdims=True)))
    mixture = jnp.einsum('hqk,khd->qhd', probabilities, value_rows, precision=lax.Precision.HIGHEST)
    mixture = low(low_back(mixture.reshape(length, H * HD)))
    hidden_state = stream + low_back(product(mixture, w_out))
    normed_mlp = low(normalize(hidden_state, gain_mlp))
    upward = low_back(product(normed_mlp, w_up))
    active = low(jax.nn.gelu(upward, approximate=True))
    return hidden_state + low_back(product(active, w_down))

def reference(tokens, segment_ids, w_query, w_key, w_value, w_out, w_up, w_down, gain_attn, gain_mlp, cotangent):
    params = tuple((entry.astype(jnp.float32) for entry in (w_query, w_key, w_value, w_out, w_up, w_down, gain_attn, gain_mlp)))
    checked = jax.checkpoint(residual_block)

    def forward(stream_all, weights_all):

        def advance(carried, entry_pair):
            return (carried, checked(entry_pair[0], entry_pair[1], *weights_all))
        unused, outputs = lax.scan(advance, jnp.float32(0.0), (stream_all, segment_ids))
        return outputs
    output, pullback = jax.vjp(forward, tokens.astype(jnp.float32), params)
    input_grad, gradients = pullback(cotangent.astype(jnp.float32))
    return (output, input_grad, gradients[0], gradients[1], gradients[2], gradients[3], gradients[4], gradients[5], gradients[6], gradients[7])
```

```python
from functools import partial

import jax
import jax.numpy as jnp
from jax import lax
from jax.experimental import pallas as pl
from jax.experimental.pallas import tpu as pltpu
from jax.sharding import PartitionSpec as P

HD = 64
DOC_MOST = 512
EPS = 1e-05
NEGATIVE = -1e30
SCALE = HD ** (-0.5)
GELU_A = 0.7978845608028654
GELU_B = 0.044715
F32 = jnp.float32
BF16 = jnp.bfloat16


def nn(left, right):
    return lax.dot_general(left, right, (((1,), (0,)), ((), ())), preferred_element_type=F32)


def nt(left, right):
    return lax.dot_general(left, right, (((1,), (1,)), ((), ())), preferred_element_type=F32)


def tn(left, right):
    return lax.dot_general(left, right, (((0,), (0,)), ((), ())), preferred_element_type=F32)


def unit_of(rows):
    center = rows - jnp.mean(rows, axis=-1, keepdims=True)
    spread = jnp.mean(center * center, axis=-1, keepdims=True)
    inverse = lax.rsqrt(spread + EPS)
    return center * inverse, inverse


def norm_back(incoming, unit, inverse, gain):
    scaled = incoming * gain
    return inverse * (
        scaled
        - jnp.mean(scaled, axis=-1, keepdims=True)
        - unit * jnp.mean(scaled * unit, axis=-1, keepdims=True)
    )


def whole():
    return pl.BlockSpec(memory_space=pltpu.VMEM)


def scalars():
    return pl.BlockSpec(memory_space=pltpu.SMEM)


def call(body, name, ids, ins, outs, scratch=(), flops=0, seq=None):
    in_specs = [scalars()] + [whole() for _ in ins]
    if seq is not None:
        inner, (part, those) = body, seq

        def body(ids_ref, *refs):
            inner(ids_ref, *[r.at[part] if i in those else r for i, r in enumerate(refs)])
    nbytes = sum(x.size * x.dtype.itemsize for x in ins) + sum(
        o.size * o.dtype.itemsize for o in outs
    )
    return pl.pallas_call(
        body,
        name=name,
        out_shape=tuple(outs),
        in_specs=in_specs,
        out_specs=tuple(whole() for _ in outs),
        scratch_shapes=list(scratch),
        compiler_params=pltpu.CompilerParams(vmem_limit_bytes=56 << 20),
        cost_estimate=pl.CostEstimate(flops=flops, transcendentals=0, bytes_accessed=nbytes),
    )(ids, *ins)


def sds(shape, dtype):
    return jax.ShapeDtypeStruct(shape, dtype)


def place_kernel(rows, splits, ids, *refs):
    count = len(refs) - len(splits)
    for k in range(count):
        start = pl.multiple_of(ids[k] * rows, 16)
        low = 0
        for out in refs[count:]:
            out[pl.ds(start, rows), :] = refs[k][:, low : low + out.shape[1]]
            low += out.shape[1]


def gains_kernel(lane, ids, wa, out):
    out[...] = wa[:, lane : lane + 128].astype(F32).T[64:72, :]


def place_gains_kernel(rows, lane, ids, *refs):
    out, gains = refs[-2:]
    place_kernel(rows, (0,), ids, *refs[:-1])
    gains_kernel(lane, ids, out, gains)


def attend_kernel(
    ids, start, tok0, tok1, tok2, tok3, wa, gains,
    normed_o, qkv_o, mix_t_o, mix_n_o, mix_own_o, mix_oth_o, lse_o, q_t, v_t,
):
    t = ids[0]
    heads = mix_t_o.shape[0] // HD
    width = heads * HD
    block = tok0.shape[0]
    gain = gains[0:1, :]
    for j, tok in enumerate((tok0, tok1, tok2, tok3)):
        unit, _ = unit_of(tok[...].astype(F32))
        place = pl.multiple_of((t ^ j) * block, block)
        normed_o[pl.ds(place, block), :] = (unit * gain).astype(BF16)
    count = normed_o.shape[0] // block
    for g in range(count):
        here = slice(g * block, (g + 1) * block)
        got = nn(normed_o[here, :], wa[:, : 3 * width])
        qkv_o[here, :width] = (got[:, :width] * SCALE).astype(BF16)
        qkv_o[here, width:] = got[:, width:].astype(BF16)
        q_t[:, here] = (got[:, :width] * SCALE).T.astype(BF16)
        v_t[:, here] = got[:, 2 * width :].T.astype(BF16)
    lse_o[...] = jnp.zeros_like(lse_o)
    for g in range(count):
        low = max(0, g - (DOC_MOST + block - 2) // block)
        here = slice(g * block, (g + 1) * block)
        keys = slice(low * block, (g + 1) * block)
        span = (g + 1 - low) * block
        row = lax.broadcasted_iota(jnp.int32, (span, block), 0) + low * block
        column = lax.broadcasted_iota(jnp.int32, (span, block), 1) + g * block
        valid = (row <= column) & (row >= start[0:1, here])
        for h in range(heads):
            lanes = slice(h * HD, (h + 1) * HD)
            klanes = slice(width + h * HD, width + (h + 1) * HD)
            scores = nn(qkv_o[keys, klanes], q_t[lanes, here])
            scores = jnp.where(valid, scores, NEGATIVE)
            highest = jnp.max(scores, axis=0, keepdims=True)
            weights = jnp.exp(scores - highest)
            total = jnp.sum(weights, axis=0, keepdims=True)
            mixed = nn(v_t[lanes, keys], weights.astype(BF16)) / total
            mix_t_o[lanes, here] = mixed.astype(BF16)
            lse_o[h : h + 1, here] = highest + jnp.log(total)
        mix_n_o[here, :] = mix_t_o[:, here].astype(F32).T.astype(BF16)
    for j in range(4):
        place = pl.multiple_of((t ^ j) * block, block)
        target = mix_own_o if j % 2 == 0 else mix_oth_o
        target[j // 2] = mix_n_o[pl.ds(place, block), :]


def mlp_kernel(
    ids, tok0, tok2, mix_own, mix_c, mix_y, mix_cy, cot0, cot2, gains, wo, wo_oth, wup, wup_oth, wd, wd_oth,
    unit_o, inv_o, hid_o, nm_o, act_own_o, act_oth_o, gu_own_o, gu_oth_o, gnm_o,
):
    gain = gains[1:2, :]
    block = tok0.shape[0]
    qw = mix_own.shape[2]
    ff = wup.shape[1]
    step = 256
    for k, (tok, cot) in enumerate(((tok0, cot0), (tok2, cot2))):
        here = slice(k * block, (k + 1) * block)
        hidden = tok[...].astype(F32) + (
            (nt(mix_own[k], wo[:, :qw]) + nt(mix_c[k], wo_oth[:, :qw]))
            + (nt(mix_y[1 - k], wo[:, qw:]) + nt(mix_cy[1 - k], wo_oth[:, qw:]))
        )
        if k == 0:
            hid_o[...] = hidden
        unit, inverse = unit_of(hidden)
        unit_o[here, :] = unit
        inv_o[here, :] = jnp.broadcast_to(inverse, (block, 128))
        nm_o[here, :] = (unit * gain).astype(BF16)
        back = jnp.zeros((block, tok.shape[1]), F32)
        for up_w, down_w, act_o, gu_o in (
            (wup, wd, act_own_o, gu_own_o), (wup_oth, wd_oth, act_oth_o, gu_oth_o)
        ):
            for c in range(0, ff, step):
                cols = slice(c, c + step)
                up = up_w[:, cols]
                u = nn(nm_o[here, :], up)
                ga = nn(cot[...], down_w[:, cols])
                square = u * u
                th = jnp.tanh(GELU_A * (u + GELU_B * square * u))
                half = 0.5 * (1.0 + th)
                slope = half + 0.5 * u * (1.0 - th * th) * (GELU_A + (3.0 * GELU_A * GELU_B) * square)
                act_o[here, cols] = (u * half).astype(BF16)
                gu = (ga * slope).astype(BF16)
                gu_o[here, cols] = gu
                back = back + nt(gu, up)
        gnm_o[k] = back.astype(BF16)


def down_kernel(seqs, ids, *refs):
    act_own, act_oth, gnm, unit, hid = (refs[i * seqs : (i + 1) * seqs] for i in range(5))
    wd, wd_oth, keep_o, send_o, gain_o = refs[5 * seqs :]
    block = hid[0].shape[0]
    gain = None
    for s in range(seqs):
        for k in range(2):
            here = slice(k * block, (k + 1) * block)
            part = nt(act_own[s][here, :], wd[...]) + nt(act_oth[s][here, :], wd_oth[...])
            if k == 0:
                keep_o[s] = hid[s][...] + part
            else:
                send_o[s] = part.astype(BF16)
            line = jnp.sum(gnm[s][k].astype(F32) * unit[s][here, :], axis=0, keepdims=True)
            gain = line if gain is None else gain + line
    gain_o[...] = jnp.broadcast_to(gain, gain_o.shape)


def deal(ids, total, rows, cols, outs):
    if len(outs) == 1:
        outs[0][:, cols] = total[...].astype(BF16)
        return
    keep, send3, send2, send10 = outs
    half = keep.shape[0]

    def take(k):
        start = pl.multiple_of(ids[k] * rows, 8)
        return total[pl.ds(start, rows), :].astype(BF16)

    for r in range(half):
        keep[r, :, cols] = take(r)
    send3[:, cols] = take(half + 3)
    send2[:, cols] = take(half + 2)
    send10[1, :, cols] = take(half + 1)
    send10[0, :, cols] = take(half)


def mlp_grads_kernel(seqs, rows, ids, *refs):
    nm, nm_r, gu, gu_r, act, act_r = (refs[i * seqs : (i + 1) * seqs] for i in range(6))
    cots = refs[6 * seqs : 6 * seqs + 4]
    outs, total = refs[6 * seqs + 4 : -1], refs[-1]
    block = cots[0].shape[1]
    ff = gu[0].shape[1]
    step = total.shape[1]
    one, two = slice(0, block), slice(block, 2 * block)
    for c in range(0, ff, step):
        cols = slice(c, c + step)
        got = None
        for s in range(seqs):
            part = tn(nm[s][...], gu[s][:, cols]) + tn(nm_r[s][...], gu_r[s][:, cols])
            got = part if got is None else got + part
        total[...] = got
        deal(ids, total, rows, cols, outs)
        got = None
        for s in range(seqs):
            part = (tn(cots[0][s], act[s][one, cols]) + tn(cots[2][s], act[s][two, cols])) + (
                tn(cots[1][s], act_r[s][one, cols]) + tn(cots[3][s], act_r[s][two, cols])
            )
            got = part if got is None else got + part
        total[...] = got
        deal(ids, total, rows, slice(ff + c, ff + c + step), outs)


def hidden_back_kernel(ids, gnm_own, gnm_rcv, unit, inv, cot0, cot2, gains, gh_o, ghb_o):
    gain = gains[1:2, :]
    block = cot0.shape[0]
    for k, cot in enumerate((cot0, cot2)):
        here = slice(k * block, (k + 1) * block)
        incoming = gnm_own[k].astype(F32) + gnm_rcv[1 - k].astype(F32)
        gh = cot[...].astype(F32) + norm_back(incoming, unit[here, :], inv[here, 0:1], gain)
        if k == 0:
            gh_o[...] = gh
        ghb_o[k] = gh.astype(BF16)


def attend_back_kernel(
    ids, start, qkv, mix_t, lse, gh_own, gh_rcv, wo, gq_own_o, gq_oth_o, gq_o, gh_o,
    gm_n, gm_t, q_t, k_t, inner, acc_k, acc_v,
):
    t = ids[0]
    width = mix_t.shape[0]
    heads = width // HD
    block = gh_own.shape[1]
    count = qkv.shape[0] // block
    for j in range(4):
        place = pl.multiple_of((t ^ j) * block, block)
        gh_o[pl.ds(place, block), :] = (gh_own if j % 2 == 0 else gh_rcv)[j // 2]
    for g in range(count):
        here = slice(g * block, (g + 1) * block)
        q_t[:, here] = qkv[here, :width].astype(F32).T.astype(BF16)
        k_t[:, here] = qkv[here, width : 2 * width].astype(F32).T.astype(BF16)
        grad_mix = nn(gh_o[here, :], wo[:, :width]).astype(BF16)
        gm_n[here, :] = grad_mix
        turned = grad_mix.astype(F32).T
        gm_t[:, here] = turned.astype(BF16)
        both = turned * mix_t[:, here].astype(F32)
        for h in range(heads):
            inner[h : h + 1, here] = jnp.sum(both[h * HD : (h + 1) * HD, :], axis=0, keepdims=True)
    acc_k[...] = jnp.zeros_like(acc_k)
    acc_v[...] = jnp.zeros_like(acc_v)
    for g in range(count):
        low = max(0, g - (DOC_MOST + block - 2) // block)
        here = slice(g * block, (g + 1) * block)
        keys = slice(low * block, (g + 1) * block)
        span = (g + 1 - low) * block
        row = lax.broadcasted_iota(jnp.int32, (span, block), 0) + low * block
        column = lax.broadcasted_iota(jnp.int32, (span, block), 1) + g * block
        valid = (row <= column) & (row >= start[0:1, here])
        for h in range(heads):
            lanes = slice(h * HD, (h + 1) * HD)
            klanes = slice(width + h * HD, width + (h + 1) * HD)
            vlanes = slice(2 * width + h * HD, 2 * width + (h + 1) * HD)
            scores = jnp.where(valid, nn(qkv[keys, klanes], q_t[lanes, here]), NEGATIVE)
            probs = jnp.exp(scores - lse[h : h + 1, here])
            grad_probs = nn(qkv[keys, vlanes], gm_t[lanes, here])
            grad_scores = (probs * (grad_probs - inner[h : h + 1, here])).astype(BF16)
            acc_k[h, keys, :] += nn(grad_scores, qkv[here, lanes])
            acc_v[h, keys, :] += nn(probs.astype(BF16), gm_n[here, lanes])
            grad_q = nn(k_t[lanes, keys], grad_scores) * SCALE
            gq_o[here, lanes] = grad_q.T.astype(BF16)
    for h in range(heads):
        gq_o[:, width + h * HD : width + (h + 1) * HD] = acc_k[h].astype(BF16)
        gq_o[:, 2 * width + h * HD : 2 * width + (h + 1) * HD] = acc_v[h].astype(BF16)
    for j in range(4):
        place = pl.multiple_of((t ^ j) * block, block)
        target = gq_own_o if j % 2 == 0 else gq_oth_o
        target[j // 2, :, : 3 * width] = gq_o[pl.ds(place, block), :]


def attn_grads_kernel(seqs, rows, ids, *refs):
    normed, gq, gh, mix = (refs[i * seqs : (i + 1) * seqs] for i in range(4))
    outs, total = refs[4 * seqs : -1], refs[-1]
    wide = gq[0].shape[1]
    for s in range(seqs):
        part = tn(normed[s][...], gq[s][...])
        more = tn(gh[s][...], mix[s][...])
        if s == 0:
            total[:, :wide] = part
            total[:, wide:] = more
        else:
            total[:, :wide] += part
            total[:, wide:] += more
    deal(ids, total, rows, slice(None), outs)


def normed_back_kernel(ids, gq_own, gq_rcv, wa_own, wa_oth, tok0, tok2, keep_o, send_o, gain_o):
    width = gq_own.shape[2] // 128 * 128 - 64
    gain = None
    for k, tok in enumerate((tok0, tok2)):
        part = nt(gq_own[k][:, :width], wa_own[:, :width]) + nt(gq_rcv[k][:, :width], wa_oth[:, :width])
        if k == 0:
            keep_o[...] = part
        else:
            send_o[...] = part.astype(BF16)
        unit, _ = unit_of(tok[...].astype(F32))
        line = jnp.sum(part * unit, axis=0, keepdims=True)
        gain = line if gain is None else gain + line
    gain_o[...] = jnp.broadcast_to(gain, gain_o.shape)


def input_back_kernel(seqs, ids, *refs):
    gh, keep, rcv = (refs[i * seqs : (i + 1) * seqs] for i in range(3))
    tok0, gains, out = refs[3 * seqs :]
    for s in range(seqs):
        unit, inverse = unit_of(tok0[s].astype(F32))
        incoming = keep[s][...] + rcv[s][...].astype(F32)
        out[s] = gh[s][...] + norm_back(incoming, unit, inverse, gains[0:1, :])


def flip(array, axis, bit):
    size = lax.axis_size(axis)
    return lax.ppermute(array, axis, [(i, i ^ bit) for i in range(size)])


def ring(array, axis, step):
    size = lax.axis_size(axis)
    return lax.ppermute(array, axis, [(i, (i + step) % size) for i in range(size)])


def after(value, *others):
    return lax.optimization_barrier((value, *others))[0]


def stepwise():
    return lax.axis_size("dp") == 8


def gather_pieces(shard):
    mine = [shard]
    for _ in range(3):
        mine.append(ring(mine[-1], "dp", 2))
    return mine + [flip(piece, "dp", 1) for piece in mine], mine[-1]


def arrival_order():
    size = lax.axis_size("dp")
    me = lax.axis_index("dp")
    order = [(me - 2 * k) % size for k in range(size // 2)]
    return jnp.stack(order + [p ^ 1 for p in order]).astype(jnp.int32)


def deal_order():
    size = lax.axis_size("dp")
    me = lax.axis_index("dp")
    order = [(me + 2 * r) % size for r in range(size // 2)]
    return jnp.stack(order + [p ^ 1 for p in order]).astype(jnp.int32)


def deal_shapes(rows, size, cols):
    if not stepwise():
        return [sds((rows * size, cols), BF16)]
    return [
        sds((size // 2, rows, cols), BF16), sds((rows, cols), BF16), sds((rows, cols), BF16),
        sds((2, rows, cols), BF16),
    ]


def sum_rows(blocks):
    if not stepwise():
        size = lax.axis_size("dp")
        grads = blocks[0].reshape(size, -1, blocks[0].shape[1])
        arrived = lax.all_to_all(grads, "dp", split_axis=0, concat_axis=0, tiled=True)
        return arrived.astype(F32).sum(axis=0)
    keep, send3, send2, send10 = blocks
    got3 = flip(send3, "dp", 1)
    got2 = flip(send2, "dp", 1)
    got10 = flip(send10, "dp", 1)
    moving = (keep[3].astype(F32) + got3.astype(F32)).astype(BF16)
    for r, got in ((2, got2), (1, got10[1]), (0, got10[0])):
        moving = ring(moving, "dp", 2).astype(F32) + (keep[r].astype(F32) + got.astype(F32))
        if r > 0:
            moving = moving.astype(BF16)
    return moving


def body(
    tokens, segment_ids, w_query, w_key, w_value, w_out, w_up, w_down, gain_attn, gain_mlp, cotangent
):
    seqs, block, width = tokens.shape
    length = segment_ids.shape[1]
    qw = w_query.shape[1]
    ff = w_up.shape[1]
    rows = w_query.shape[0]
    size = lax.axis_size("dp")
    heads = qw // HD
    t = lax.axis_index("tensor").astype(jnp.int32)
    ids = jnp.stack([t, t])
    act_rows = 2 * block

    gain_pair = jnp.stack([gain_attn, gain_mlp], axis=1)
    pack_a = jnp.concatenate(
        [w_query, w_key, w_value, jnp.pad(gain_pair, ((0, 0), (0, 62)))], axis=1
    )
    out_turned = w_out.T
    pack_u = jnp.concatenate([out_turned, flip(out_turned, "tensor", 2), w_up], axis=1)
    pack_d = w_down.T
    lane = 3 * qw - 64
    shape_a, shape_g = sds((width, 3 * qw + 64), BF16), sds((8, width), F32)
    shape_o, shape_f = sds((width, 2 * qw), BF16), sds((width, ff), BF16)
    if stepwise():
        order = arrival_order()
        pieces, last = gather_pieces(pack_a)
        wa, gains = call(
            partial(place_gains_kernel, rows, lane), "place_a", order, pieces, [shape_a, shape_g]
        )
        pieces, last = gather_pieces(after(pack_u, last))
        wo, wup = call(partial(place_kernel, rows, (0, 1)), "place_u", order, pieces, [shape_o, shape_f])
        pieces, last = gather_pieces(after(pack_d, last))
        wd = call(partial(place_kernel, rows, (0,)), "place_d", order, pieces, [shape_f])[0]
    else:
        wa = lax.all_gather(pack_a, "dp", axis=0, tiled=True)
        gains = call(partial(gains_kernel, lane), "gains", ids, [wa], [shape_g])[0]
        both = lax.all_gather(pack_u, "dp", axis=0, tiled=True)
        wo, wup = both[:, : 2 * qw], both[:, 2 * qw :]
        wd = lax.all_gather(pack_d, "dp", axis=0, tiled=True)
    wo_oth = flip(wo, "tensor", 1)
    wup_oth = flip(wup, "tensor", 1)
    wd_oth = flip(wd, "tensor", 1)
    wa_oth = flip(wa, "tensor", 1)

    tok0 = tokens
    tok2 = flip(tok0, "tensor", 2)
    tok1 = flip(tok0, "tensor", 1)
    tok3 = flip(tok2, "tensor", 1)
    cot0 = cotangent
    cot1 = flip(cot0, "tensor", 1)
    cot2 = flip(after(cot0, tok2), "tensor", 2)
    cot3 = flip(cot2, "tensor", 1)

    starts = jnp.sum(
        (segment_ids[:, None, :] < segment_ids[:, :, None]).astype(jnp.int32), axis=-1
    )

    normed, qkv, mix_t, mix_n, mix_own, mix_c, mix_y, mix_cy, lse = ([] for _ in range(9))
    turn = ids
    for s in range(seqs):
        got = call(
            attend_kernel, f"attend{s}", turn, [starts[s : s + 1], tok0, tok1, tok2, tok3, wa, gains],
            [
                sds((length, width), BF16), sds((length, 3 * qw), BF16), sds((qw, length), BF16),
                sds((length, qw), BF16), sds((2, block, qw), BF16), sds((2, block, qw), BF16),
                sds((8, length), F32),
            ],
            scratch=[pltpu.VMEM((qw, length), BF16), pltpu.VMEM((qw, length), BF16)],
            seq=(s, (1, 2, 3, 4)),
            flops=4 * length * width * qw * 3,
        )
        for target, value in zip((normed, qkv, mix_t, mix_n, mix_own), got):
            target.append(value)
        lse.append(got[6])
        mix_y.append(flip(mix_own[s], "tensor", 2))
        mix_c.append(flip(got[5], "tensor", 1))
        mix_cy.append(flip(mix_c[s], "tensor", 2))
        turn = after(ids, mix_own[s])

    unit, inv, hid, nm, act, act_oth, gu, gu_oth, gnm = ([] for _ in range(9))
    turn = ids
    for s in range(seqs):
        half = sds((act_rows, ff), BF16)
        got = call(
            mlp_kernel, f"mlp{s}", turn,
            [
                tok0, tok2, mix_own[s], mix_c[s], mix_y[s], mix_cy[s], cot0, cot2, gains,
                wo, wo_oth, wup, wup_oth, wd, wd_oth,
            ],
            [
                sds((act_rows, width), F32), sds((act_rows, 128), F32), sds((block, width), F32),
                sds((act_rows, width), BF16), half, half, half, half, sds((2, block, width), BF16),
            ],
            seq=(s, (0, 1, 6, 7)),
            flops=6 * act_rows * width * 2 * ff,
        )
        for target, value in zip((unit, inv, hid, nm, act, act_oth, gu, gu_oth, gnm), got):
            target.append(value)
        turn = after(ids, gnm[s])
    gnm_rcv = [flip(gnm[s], "tensor", 2) for s in range(seqs)]
    nm_r = [flip(nm[s], "tensor", 1) for s in range(seqs)]
    gu_r = [flip(gu_oth[s], "tensor", 1) for s in range(seqs)]
    act_r = [flip(act_oth[s], "tensor", 1) for s in range(seqs)]

    dealt = deal_order() if stepwise() else ids
    mlp_blocks = call(
        partial(mlp_grads_kernel, seqs, rows), "mlp_grads", dealt,
        [*nm, *nm_r, *gu, *gu_r, *act, *act_r, cot0, cot1, cot2, cot3],
        deal_shapes(rows, size, 2 * ff),
        scratch=[pltpu.VMEM((width, 256), F32)],
        flops=8 * seqs * act_rows * width * ff,
    )
    mlp_grad = sum_rows(mlp_blocks)

    gh, gh_full, gq_own, gq_rcv, gq = ([] for _ in range(5))
    turn = after(ids, mlp_blocks[0])
    for s in range(seqs):
        got = call(
            hidden_back_kernel, f"hidden_back{s}", turn,
            [gnm[s], gnm_rcv[s], unit[s], inv[s], cot0, cot2, gains],
            [sds((block, width), F32), sds((2, block, width), BF16)],
            seq=(s, (4, 5)),
        )
        gh.append(got[0])
        gh_rcv = flip(got[1], "tensor", 1)
        wide = sds((2, block, 3 * qw + 64), BF16)
        got = call(
            attend_back_kernel, f"attend_back{s}", ids,
            [starts[s : s + 1], qkv[s], mix_t[s], lse[s], got[1], gh_rcv, wo],
            [wide, wide, sds((length, 3 * qw), BF16), sds((length, width), BF16)],
            scratch=[
                pltpu.VMEM((length, qw), BF16), pltpu.VMEM((qw, length), BF16),
                pltpu.VMEM((qw, length), BF16), pltpu.VMEM((qw, length), BF16),
                pltpu.VMEM((8, length), F32), pltpu.VMEM((heads, length, HD), F32),
                pltpu.VMEM((heads, length, HD), F32),
            ],
            flops=10 * length * length * qw // 2,
        )
        gq_own.append(got[0])
        gq_rcv.append(flip(got[1], "tensor", 1))
        gq.append(got[2])
        gh_full.append(got[3])
        turn = after(ids, got[0])
    attn_blocks = call(
        partial(attn_grads_kernel, seqs, rows), "attn_grads", dealt, [*normed, *gq, *gh_full, *mix_n],
        deal_shapes(rows, size, 4 * qw),
        scratch=[pltpu.VMEM((width, 4 * qw), F32)],
        flops=2 * seqs * length * width * 4 * qw,
    )
    attn_grad = sum_rows(attn_blocks)

    down_turn = after(ids, gq_own[0])
    keep_out, send_out, gain_mlp_part = call(
        partial(down_kernel, seqs), "down", down_turn, [*act, *act_oth, *gnm, *unit, *hid, wd, wd_oth],
        [sds((seqs, block, width), F32), sds((seqs, block, width), BF16), sds((8, width), F32)],
        flops=4 * seqs * act_rows * width * ff,
    )
    output = keep_out + flip(send_out, "tensor", 2).astype(F32)

    keep_in, in_rcv, gain_attn_part = [], [], []
    for s in range(seqs):
        turn = ids if s == 0 else after(ids, attn_blocks[0])
        got = call(
            normed_back_kernel, f"normed_back{s}", turn,
            [gq_own[s], gq_rcv[s], wa, wa_oth, tok0, tok2],
            [sds((block, width), F32), sds((block, width), BF16), sds((8, width), F32)],
            seq=(s, (4, 5)),
            flops=4 * act_rows * width * 3 * qw,
        )
        keep_in.append(got[0])
        in_rcv.append(flip(got[1], "tensor", 2))
        gain_attn_part.append(got[2][0])
    input_grad = call(
        partial(input_back_kernel, seqs), "input_back", ids, [*gh, *keep_in, *in_rcv, tok0, gains],
        [sds((seqs, block, width), F32)],
    )[0]

    gain_parts = jnp.stack([sum(gain_attn_part), gain_mlp_part[0]])
    gain_parts = gain_parts + flip(gain_parts, "tensor", 1)
    gain_parts = gain_parts + flip(gain_parts, "tensor", 2)
    spread = jnp.moveaxis(gain_parts.reshape(2, size, rows), 1, 0)
    gain_mine = lax.all_to_all(spread, "dp", split_axis=0, concat_axis=0, tiled=True).sum(axis=0)
    return (
        output,
        input_grad,
        attn_grad[:, :qw],
        attn_grad[:, qw : 2 * qw],
        attn_grad[:, 2 * qw : 3 * qw],
        attn_grad[:, 3 * qw :].T,
        mlp_grad[:, :ff],
        mlp_grad[:, ff:].T,
        gain_mine[0],
        gain_mine[1],
    )


def solution(mesh):
    in_specs = (
        P("dp", "tensor", None),
        P("dp", None),
        P("dp", "tensor"),
        P("dp", "tensor"),
        P("dp", "tensor"),
        P("tensor", "dp"),
        P("dp", "tensor"),
        P("tensor", "dp"),
        P("dp"),
        P("dp"),
        P("dp", "tensor", None),
    )
    out_specs = (
        P("dp", "tensor", None),
        P("dp", "tensor", None),
        P("dp", "tensor"),
        P("dp", "tensor"),
        P("dp", "tensor"),
        P("tensor", "dp"),
        P("dp", "tensor"),
        P("tensor", "dp"),
        P("dp"),
        P("dp"),
    )
    return jax.shard_map(body, mesh=mesh, in_specs=in_specs, out_specs=out_specs, check_vma=False)
```

```python
import math
from functools import partial

import jax
import jax.numpy as jnp
import numpy as np
from jax import lax
from jax.experimental import pallas as pl
from jax.experimental.pallas import tpu as pltpu
from jax.sharding import PartitionSpec as P

HD = 64
DOC_MOST = 512
EPS = 1e-05
NEGATIVE = -1e30
COST = 5e8
SCALE = HD ** (-0.5)
GELU_A = 0.7978845608028654
GELU_B = 0.044715
F32 = jnp.float32
BF16 = jnp.bfloat16


def nn(left, right):
    return lax.dot_general(left, right, (((1,), (0,)), ((), ())), preferred_element_type=F32)


def nt(left, right):
    return lax.dot_general(left, right, (((1,), (1,)), ((), ())), preferred_element_type=F32)


def tn(left, right):
    return lax.dot_general(left, right, (((0,), (0,)), ((), ())), preferred_element_type=F32)


def unit_of(rows):
    center = rows - jnp.mean(rows, axis=-1, keepdims=True)
    spread = jnp.mean(center * center, axis=-1, keepdims=True)
    inverse = lax.rsqrt(spread + EPS)
    return center * inverse, inverse


def norm_back(incoming, unit, inverse, gain):
    scaled = incoming * gain
    return inverse * (
        scaled
        - jnp.mean(scaled, axis=-1, keepdims=True)
        - unit * jnp.mean(scaled * unit, axis=-1, keepdims=True)
    )


def nbytes_of(shapes):
    return sum(math.prod(x.shape) * jnp.dtype(x.dtype).itemsize for x in shapes)


def part(array, index):
    return array, index, jax.eval_shape(lambda x: x[index], array).shape


def call(body, name, ids, ins, outs, scratch=(), us=2.0):
    ins = [x if isinstance(x, tuple) else (x, None, x.shape) for x in ins]
    arrays = []
    for x, _, _ in ins:
        if not any(x is y for y in arrays):
            arrays.append(x)
    place = [next(i for i, y in enumerate(arrays) if y is x) for x, _, _ in ins]
    count, made = len(arrays), len(outs)

    def kernel(ids_ref, *refs):
        sources, targets, own = refs[:count], refs[count : count + made], refs[count + made :]
        loads = []
        for i, (_, index, _) in enumerate(ins):
            source = sources[place[i]]
            loads.append(source if index is None else source.at[index])
        body(ids_ref, *loads, *targets, *own)

    return pl.pallas_call(
        kernel,
        name=name,
        out_shape=tuple(outs),
        in_specs=[pl.BlockSpec(memory_space=pltpu.SMEM)] + [pl.BlockSpec(memory_space=pltpu.VMEM)] * count,
        out_specs=tuple(pl.BlockSpec(memory_space=pltpu.VMEM) for _ in outs),
        scratch_shapes=list(scratch),
        compiler_params=pltpu.CompilerParams(vmem_limit_bytes=nbytes_of(scratch) + (10 << 20)),
        cost_estimate=pl.CostEstimate(flops=int(us * COST), transcendentals=0, bytes_accessed=0),
    )(ids, *arrays)


def sds(shape, dtype):
    return jax.ShapeDtypeStruct(shape, dtype)


def gains_kernel(lane, ids, wa, out):
    out[...] = wa[:, lane : lane + 128].astype(F32).T[64:72, :]


def place_kernel(rows, ids, *refs):
    pieces, out = refs[:-1], refs[-1]
    for k, piece in enumerate(pieces):
        out[pl.ds(pl.multiple_of(ids[1 + k] * rows, 16), rows), :] = piece[...]


def place_gains_kernel(rows, lane, ids, *refs):
    out, gains = refs[-2:]
    place_kernel(rows, ids, *refs[:-1])
    gains_kernel(lane, ids, out, gains)


def attend_kernel(
    ids, tok0, tok1, tok2, tok3, wa, gains, start,
    normed_o, qkv_o, mix_t_o, mix_n_o, mix_own_o, mix_oth_o, lse_o, q_t, v_t,
):
    t = ids[0]
    heads = mix_t_o.shape[0] // HD
    width = heads * HD
    block = tok0.shape[0]
    gain = gains[0:1, :]
    for j, tok in enumerate((tok0, tok1, tok2, tok3)):
        unit, _ = unit_of(tok[...].astype(F32))
        place = pl.multiple_of((t ^ j) * block, block)
        normed_o[pl.ds(place, block), :] = (unit * gain).astype(BF16)
    count = normed_o.shape[0] // block
    for g in range(count):
        here = slice(g * block, (g + 1) * block)
        got = nn(normed_o[here, :], wa[:, : 3 * width])
        qkv_o[here, :width] = (got[:, :width] * SCALE).astype(BF16)
        qkv_o[here, width:] = got[:, width:].astype(BF16)
        q_t[:, here] = (got[:, :width] * SCALE).T.astype(BF16)
        v_t[:, here] = got[:, 2 * width :].T.astype(BF16)
    lse_o[...] = jnp.zeros_like(lse_o)
    for g in range(count):
        low = max(0, g - (DOC_MOST + block - 2) // block)
        here = slice(g * block, (g + 1) * block)
        keys = slice(low * block, (g + 1) * block)
        span = (g + 1 - low) * block
        row = lax.broadcasted_iota(jnp.int32, (span, block), 0) + low * block
        column = lax.broadcasted_iota(jnp.int32, (span, block), 1) + g * block
        valid = (row <= column) & (row >= start[0:1, here])
        for h in range(heads):
            lanes = slice(h * HD, (h + 1) * HD)
            klanes = slice(width + h * HD, width + (h + 1) * HD)
            scores = nn(qkv_o[keys, klanes], q_t[lanes, here])
            scores = jnp.where(valid, scores, NEGATIVE)
            highest = jnp.max(scores, axis=0, keepdims=True)
            weights = jnp.exp(scores - highest)
            total = jnp.sum(weights, axis=0, keepdims=True)
            mixed = nn(v_t[lanes, keys], weights.astype(BF16)) / total
            mix_t_o[lanes, here] = mixed.astype(BF16)
            lse_o[h : h + 1, here] = highest + jnp.log(total)
        mix_n_o[here, :] = mix_t_o[:, here].astype(F32).T.astype(BF16)
    for j in range(4):
        place = pl.multiple_of((t ^ j) * block, block)
        target = mix_own_o if j % 2 == 0 else mix_oth_o
        target[j // 2] = mix_n_o[pl.ds(place, block), :]


def mlp_kernel(
    ids, tok0, tok2, mix_own, mix_c, wo, wo_oth, mix_y, mix_cy, gains, cot0, cot2, wup, wd, wup_oth, wd_oth,
    unit_o, inv_o, hid_o, nm_o, act_o, gu_o, gnm_o,
):
    gain = gains[1:2, :]
    block = tok0.shape[0]
    qw = mix_own.shape[2]
    ff = wup.shape[1]
    step = 256
    for k, (tok, cot) in enumerate(((tok0, cot0), (tok2, cot2))):
        here = slice(k * block, (k + 1) * block)
        hidden = tok[...].astype(F32) + (
            (nt(mix_own[k], wo[:, :qw]) + nt(mix_c[k], wo_oth[:, :qw]))
            + (nt(mix_y[1 - k], wo[:, qw:]) + nt(mix_cy[1 - k], wo_oth[:, qw:]))
        )
        if k == 0:
            hid_o[...] = hidden
        unit, inverse = unit_of(hidden)
        unit_o[here, :] = unit
        inv_o[here, :] = jnp.broadcast_to(inverse, (block, 128))
        nm_o[here, :] = (unit * gain).astype(BF16)
        back = jnp.zeros((block, tok.shape[1]), F32)
        for h, (up_w, down_w) in enumerate(((wup, wd), (wup_oth, wd_oth))):
            for c in range(0, ff, step):
                cols = slice(c, c + step)
                to = slice(h * ff + c, h * ff + c + step)
                up = up_w[:, cols]
                u = nn(nm_o[here, :], up)
                ga = nn(cot[...], down_w[:, cols])
                square = u * u
                th = jnp.tanh(GELU_A * (u + GELU_B * square * u))
                half = 0.5 * (1.0 + th)
                slope = half + 0.5 * u * (1.0 - th * th) * (GELU_A + (3.0 * GELU_A * GELU_B) * square)
                act_o[here, to] = (u * half).astype(BF16)
                gu = (ga * slope).astype(BF16)
                gu_o[here, to] = gu
                back = back + nt(gu, up)
        gnm_o[k] = back.astype(BF16)


def down_kernel(seqs, ids, *refs):
    act, hid = refs[:seqs], refs[seqs : 2 * seqs]
    wd, wd_oth, keep_o, send_o = refs[2 * seqs :]
    block = hid[0].shape[0]
    ff = wd.shape[1]
    for s in range(seqs):
        for k in (1, 0):
            here = slice(k * block, (k + 1) * block)
            got = nt(act[s][here, :ff], wd[...]) + nt(act[s][here, ff:], wd_oth[...])
            if k == 0:
                keep_o[s] = hid[s][...] + got
            else:
                send_o[s] = got.astype(BF16)


def deal(ids, order, total, rows, cols, outs):
    if len(outs) == 1 and len(outs[0].shape) == 2:
        outs[0][:, cols] = total[...].astype(BF16)
        return
    at = 1 + order * (ids.shape[0] // 3)
    for out in outs:
        lead = out.shape[:-2]
        for k in range(math.prod(lead)):
            start = pl.multiple_of(ids[at] * rows, 8)
            got = total[pl.ds(start, rows), :].astype(BF16)
            if len(lead) == 2:
                out[k // lead[1], k % lead[1], :, cols] = got
            else:
                out[k, :, cols] = got
            at += 1


def mlp_grads_kernel(seqs, rows, ids, *refs):
    nm, gu, act = (refs[i * seqs : (i + 1) * seqs] for i in range(3))
    cot0, cot2 = refs[3 * seqs : 3 * seqs + 2]
    outs, total = refs[3 * seqs + 2 : -1], refs[-1]
    block = cot0.shape[1]
    ff = gu[0].shape[1]
    step = total.shape[1]
    one, two = slice(0, block), slice(block, 2 * block)
    for c in range(0, ff, step):
        cols = slice(c, c + step)
        got = None
        for s in range(seqs):
            more = tn(nm[s][...], gu[s][:, cols])
            got = more if got is None else got + more
        total[...] = got
        deal(ids, 1, total, rows, cols, outs)
        got = None
        for s in range(seqs):
            more = tn(cot0[s], act[s][one, cols]) + tn(cot2[s], act[s][two, cols])
            got = more if got is None else got + more
        total[...] = got
        deal(ids, 1, total, rows, slice(ff + c, ff + c + step), outs)


def hidden_back_kernel(ids, gnm_own, gnm_rcv, unit, inv, cot0, cot2, gains, gh_o, ghb_o):
    gain = gains[1:2, :]
    block = cot0.shape[0]
    for k, cot in enumerate((cot0, cot2)):
        here = slice(k * block, (k + 1) * block)
        incoming = gnm_own[k].astype(F32) + gnm_rcv[1 - k].astype(F32)
        gh = cot[...].astype(F32) + norm_back(incoming, unit[here, :], inv[here, 0:1], gain)
        if k == 0:
            gh_o[...] = gh
        ghb_o[k] = gh.astype(BF16)


def attend_back_kernel(
    ids, start, qkv, mix_t, lse, gh_own, gh_rcv, wo, gq_own_o, gq_oth_o, gq_o, gh_o,
    gm_n, gm_t, q_t, k_t, inner, acc_k, acc_v,
):
    t = ids[0]
    width = mix_t.shape[0]
    heads = width // HD
    block = gh_own.shape[1]
    count = qkv.shape[0] // block
    for j in range(4):
        place = pl.multiple_of((t ^ j) * block, block)
        gh_o[pl.ds(place, block), :] = (gh_own if j % 2 == 0 else gh_rcv)[j // 2]
    for g in range(count):
        here = slice(g * block, (g + 1) * block)
        q_t[:, here] = qkv[here, :width].astype(F32).T.astype(BF16)
        k_t[:, here] = qkv[here, width : 2 * width].astype(F32).T.astype(BF16)
        grad_mix = nn(gh_o[here, :], wo[:, :width]).astype(BF16)
        gm_n[here, :] = grad_mix
        turned = grad_mix.astype(F32).T
        gm_t[:, here] = turned.astype(BF16)
        both = turned * mix_t[:, here].astype(F32)
        for h in range(heads):
            inner[h : h + 1, here] = jnp.sum(both[h * HD : (h + 1) * HD, :], axis=0, keepdims=True)
    acc_k[...] = jnp.zeros_like(acc_k)
    acc_v[...] = jnp.zeros_like(acc_v)
    for g in range(count):
        low = max(0, g - (DOC_MOST + block - 2) // block)
        here = slice(g * block, (g + 1) * block)
        keys = slice(low * block, (g + 1) * block)
        span = (g + 1 - low) * block
        row = lax.broadcasted_iota(jnp.int32, (span, block), 0) + low * block
        column = lax.broadcasted_iota(jnp.int32, (span, block), 1) + g * block
        valid = (row <= column) & (row >= start[0:1, here])
        for h in range(heads):
            lanes = slice(h * HD, (h + 1) * HD)
            klanes = slice(width + h * HD, width + (h + 1) * HD)
            vlanes = slice(2 * width + h * HD, 2 * width + (h + 1) * HD)
            scores = jnp.where(valid, nn(qkv[keys, klanes], q_t[lanes, here]), NEGATIVE)
            probs = jnp.exp(scores - lse[h : h + 1, here])
            grad_probs = nn(qkv[keys, vlanes], gm_t[lanes, here])
            grad_scores = (probs * (grad_probs - inner[h : h + 1, here])).astype(BF16)
            acc_k[h, keys, :] += nn(grad_scores, qkv[here, lanes])
            acc_v[h, keys, :] += nn(probs.astype(BF16), gm_n[here, lanes])
            grad_q = nn(k_t[lanes, keys], grad_scores) * SCALE
            gq_o[here, lanes] = grad_q.T.astype(BF16)
    for h in range(heads):
        gq_o[:, width + h * HD : width + (h + 1) * HD] = acc_k[h].astype(BF16)
        gq_o[:, 2 * width + h * HD : 2 * width + (h + 1) * HD] = acc_v[h].astype(BF16)
    for j in range(4):
        place = pl.multiple_of((t ^ j) * block, block)
        target = gq_own_o if j % 2 == 0 else gq_oth_o
        target[j // 2, :, : 3 * width] = gq_o[pl.ds(place, block), :]


def attn_grads_kernel(seqs, rows, ids, *refs):
    normed, gq, gh, mix = (refs[i * seqs : (i + 1) * seqs] for i in range(4))
    outs, total = refs[4 * seqs : -1], refs[-1]
    wide = gq[0].shape[1]
    for cols, left, right in ((slice(0, wide), normed, gq), (slice(wide, None), gh, mix)):
        got = None
        for s in range(seqs):
            more = tn(left[s][...], right[s][...])
            got = more if got is None else got + more
        total[:, cols] = got
    deal(ids, 1, total, rows, slice(None), outs)


def normed_back_kernel(ids, gq_own, gq_rcv, wa_own, wa_oth, keep_o, send_o):
    width = gq_own.shape[2] // 128 * 128 - 64
    for k in (1, 0):
        got = nt(gq_own[k, :, :width], wa_own[:, :width]) + nt(gq_rcv[k, :, :width], wa_oth[:, :width])
        if k == 0:
            keep_o[...] = got
        else:
            send_o[...] = got.astype(BF16)


def finish_attn_kernel(count, ids, *refs):
    pieces, weights, outs = refs[:count], refs[count : count + 3], refs[count + 3 :]
    total = pieces[0][...].astype(F32)
    for piece in pieces[1:]:
        total = total + piece[...].astype(F32)
    width = outs[0].shape[1]
    gain = None
    for i in range(3):
        grad = total[:, i * width : (i + 1) * width]
        outs[i][...] = grad
        line = jnp.sum(grad * weights[i][...].astype(F32), axis=1, keepdims=True)
        gain = line if gain is None else gain + line
    outs[3][...] = total[:, 3 * width :].T
    outs[4][...] = jnp.broadcast_to(gain, outs[4].shape)


def finish_mlp_kernel(count, ids, *refs):
    pieces, weight, outs = refs[:count], refs[count], refs[count + 1 :]
    total = pieces[0][...].astype(F32)
    for piece in pieces[1:]:
        total = total + piece[...].astype(F32)
    width = outs[0].shape[1]
    outs[0][...] = total[:, :width]
    outs[1][...] = total[:, width:].T
    gain = jnp.sum(total[:, :width] * weight[...].astype(F32), axis=1, keepdims=True)
    outs[2][...] = jnp.broadcast_to(gain, outs[2].shape)


def input_back_kernel(seqs, ids, *refs):
    gh, keep, rcv = (refs[i * seqs : (i + 1) * seqs] for i in range(3))
    tok0, gains, out = refs[3 * seqs :]
    for s in range(seqs):
        unit, inverse = unit_of(tok0[s].astype(F32))
        incoming = keep[s][...] + rcv[s][...].astype(F32)
        out[s] = gh[s][...] + norm_back(incoming, unit, inverse, gains[0:1, :])


def flip(array, axis, bit):
    size = lax.axis_size(axis)
    return lax.ppermute(array, axis, [(i, i ^ bit) for i in range(size)])


def ring(array, axis, step):
    size = lax.axis_size(axis)
    return lax.ppermute(array, axis, [(i, (i + step) % size) for i in range(size)])


def after(value, *others):
    return lax.optimization_barrier((value, *others))[0]


def stepwise():
    return lax.axis_size("dp") == 8


def together(*values):
    return lax.optimization_barrier(values)


def places():
    size, wide = lax.axis_size("dp"), lax.axis_size("tensor")
    table = np.zeros((size * wide, 1 + 3 * size), np.int32)
    for me in range(size):
        half = range(size // 2)
        for low, line in (
            (0, [(me - 2 * k) % size for k in half]),
            (1, [(me + 2 * k) % size for k in half]),
            (2, [me % 2 + 2 * k for k in half]),
        ):
            for t in range(wide):
                row = table[me * wide + t]
                row[0] = t
                row[1 + low * size : 1 + (low + 1) * size] = line + [p ^ 1 for p in line]
    return lax.dynamic_index_in_dim(jnp.asarray(table), lax.axis_index(("dp", "tensor")), 0, keepdims=False)


def add(*blocks):
    return sum(block.astype(F32) for block in blocks).astype(BF16)


def sum_far(total):
    size = lax.axis_size("dp")
    groups = [[2 * k + low for k in range(size // 2)] for low in range(2)]
    got = lax.all_to_all(total, "dp", split_axis=0, concat_axis=0, tiled=True, axis_index_groups=groups)
    return [got[k] for k in range(size // 2)]


def sum_ring(total):
    return [total[0]] + [ring(total[r], "dp", 2 * r) for r in range(1, total.shape[0])]


def sum_rows_any(grads):
    size = lax.axis_size("dp")
    blocks = grads.reshape(size, -1, grads.shape[1])
    arrived = lax.all_to_all(blocks, "dp", split_axis=0, concat_axis=0, tiled=True)
    return [arrived.astype(F32).sum(axis=0)]


def body(
    tokens, segment_ids, w_query, w_key, w_value, w_out, w_up, w_down, gain_attn, gain_mlp, cotangent
):
    seqs, block, width = tokens.shape
    length = segment_ids.shape[1]
    qw = w_query.shape[1]
    ff = w_up.shape[1]
    rows = w_query.shape[0]
    size = lax.axis_size("dp")
    heads = qw // HD
    ids = places()
    act_rows = 2 * block

    gain_pair = jnp.stack([gain_attn, gain_mlp], axis=1)
    pack_a = jnp.concatenate(
        [w_query, w_key, w_value, jnp.pad(gain_pair, ((0, 0), (0, 62)))], axis=1
    )
    lane = 3 * qw - 64
    shape_a, shape_g = sds((width, 3 * qw + 64), BF16), sds((8, width), F32)
    out_turned = w_out.T
    tok0, cot0 = tokens, cotangent
    if stepwise():
        a_p, a_m, a_x0 = ring(pack_a, "dp", 2), ring(pack_a, "dp", -2), flip(pack_a, "dp", 1)
        out_y, tok1 = flip(after(out_turned, ids, pack_a), "tensor", 2), flip(tok0, "tensor", 1)
        tok2 = flip(after(tok0, out_y), "tensor", 2)
        a_p, a_m, a_x0, out_y, tok1 = together(a_p, a_m, a_x0, out_y, tok1)
        pack_b = jnp.concatenate([out_turned, out_y, w_up, w_down.T], axis=1)
        a_2, a_xp, a_xm, b_p = ring(a_p, "dp", 2), flip(a_p, "dp", 1), flip(a_m, "dp", 1), ring(pack_b, "dp", 2)
        a_2, a_xp, a_xm = together(a_2, a_xp, a_xm)
        a_x2 = flip(a_2, "dp", 1)
        a_x2, tok2, b_p = together(a_x2, tok2, b_p)
        tok3 = flip(tok2, "tensor", 1)
        b_2, b_m, b_x0 = ring(b_p, "dp", 2), ring(after(pack_b, b_p), "dp", -2), flip(after(pack_b, b_p), "dp", 1)
        cot2 = flip(after(cot0, tok2), "tensor", 2)
        wa, gains = call(
            partial(place_gains_kernel, rows, lane), "place_a", ids,
            [pack_a, a_p, a_2, a_m, a_x0, a_xp, a_x2, a_xm], [shape_a, shape_g],
        )
        start_turn = after(ids, wa)
    else:
        out_y = flip(out_turned, "tensor", 2)
        pack_b = jnp.concatenate([out_turned, out_y, w_up, w_down.T], axis=1)
        tok1, tok2, cot2 = flip(tok0, "tensor", 1), flip(tok0, "tensor", 2), flip(cot0, "tensor", 2)
        tok3 = flip(tok2, "tensor", 1)
        wa = lax.all_gather(pack_a, "dp", axis=0, tiled=True)
        gains = call(partial(gains_kernel, lane), "gains", ids, [wa], [shape_g])[0]
        wb = lax.all_gather(pack_b, "dp", axis=0, tiled=True)
        start_turn = ids

    def cut(array, low, count):
        return part(array, (slice(None), pl.ds(low, count)))

    def outs_of(array):
        return cut(array, 0, 2 * qw)

    def ups_of(array):
        return cut(array, 2 * qw, ff)

    def downs_of(array):
        return cut(array, 2 * qw + ff, ff)

    starts = jnp.sum(
        (segment_ids[:, None, :] < segment_ids[:, :, None]).astype(jnp.int32), axis=-1
    )

    normed, qkv, mix_t, mix_n, mix_own, mix_c, mix_y, mix_cy, lse = ([] for _ in range(9))
    turn = start_turn
    for s in range(seqs):
        got = call(
            attend_kernel, f"attend{s}", turn,
            [*(part(x, s) for x in (tok0, tok1, tok2, tok3)), wa, gains, starts[s : s + 1]],
            [
                sds((length, width), BF16), sds((length, 3 * qw), BF16), sds((qw, length), BF16),
                sds((length, qw), BF16), sds((2, block, qw), BF16), sds((2, block, qw), BF16),
                sds((8, length), F32),
            ],
            scratch=[pltpu.VMEM((qw, length), BF16), pltpu.VMEM((qw, length), BF16)],
            us=11,
        )
        for target, value in zip((normed, qkv, mix_t, mix_n, mix_own), got):
            target.append(value)
        lse.append(got[6])
        own, oth = together(mix_own[s], got[5], *mix_y, *mix_c, *mix_cy)[:2]
        mix_y.append(flip(own, "tensor", 2))
        mix_c.append(flip(oth, "tensor", 1))
        mix_cy.append(flip(oth, "tensor", 3))
        turn = after(ids, mix_own[s])
        if s == 0 and stepwise():
            b_x0, b_p = together(b_x0, b_p, mix_own[0])[:2]
            b_xp = flip(b_p, "dp", 1)
            turn = after(ids, b_x0)
        elif stepwise():
            b_2, b_m, b_xp = together(b_2, b_m, b_xp, mix_own[s])[:3]
            b_x2, b_xm = flip(b_2, "dp", 1), flip(b_m, "dp", 1)
    if stepwise():
        wb = call(
            partial(place_kernel, rows), "place_b", after(ids, mix_own[-1], cot2, mix_y[0], mix_c[0], mix_cy[0]),
            [pack_b, b_p, b_2, b_m, b_x0, b_xp, b_x2, b_xm],
            [sds((width, 2 * qw + 2 * ff), BF16)],
        )[0]
    wb_oth = flip(wb, "tensor", 1)

    unit, inv, hid, nm, act, gu, gnm, gnm_rcv = ([] for _ in range(8))
    turn = ids
    for s in range(seqs):
        got = call(
            mlp_kernel, f"mlp{s}", turn,
            [
                part(tok0, s), part(tok2, s), mix_own[s], mix_c[s], outs_of(wb), outs_of(wb_oth), mix_y[s], mix_cy[s],
                gains, part(cot0, s), part(cot2, s), ups_of(wb), downs_of(wb), ups_of(wb_oth), downs_of(wb_oth),
            ],
            [
                sds((act_rows, width), F32), sds((act_rows, 128), F32), sds((block, width), F32),
                sds((act_rows, width), BF16), sds((act_rows, 2 * ff), BF16), sds((act_rows, 2 * ff), BF16),
                sds((2, block, width), BF16),
            ],
            us=9,
        )
        for target, value in zip((unit, inv, hid, nm, act, gu, gnm), got):
            target.append(value)
        gnm_rcv.append(flip(after(gnm[s], mix_y[-1], mix_c[-1], mix_cy[-1]), "tensor", 2))
        if s == 0:
            wa_oth = flip(after(wa, mix_c[-1]), "tensor", 1)
        turn = after(ids, gnm[s], wa_oth)

    half_dp = size // 2
    if stepwise():
        apart = [sds((half_dp, rows, 2 * ff), BF16)] * 2
        paired = [sds((2, half_dp, rows, 2 * ff), BF16)]
        attn_apart = [sds((half_dp, rows, 4 * qw), BF16)] * 2
    else:
        apart = paired = [sds((width, 2 * ff), BF16)]
        attn_apart = [sds((width, 4 * qw), BF16)]
    grad_scratch = [pltpu.VMEM((width, 256), F32)]

    def columns(arrays, h):
        return [cut(x, h * ff, ff) for x in arrays]

    mlp_oth = call(
        partial(mlp_grads_kernel, seqs, rows), "mlp_grads_oth", after(ids, gnm[-1]),
        [*nm, *columns(gu, 1), *columns(act, 1), cot0, cot2], paired, scratch=grad_scratch, us=0.5,
    )[0]
    mlp_rcv = flip(mlp_oth, "tensor", 1)
    keep_out, send_out = call(
        partial(down_kernel, seqs), "down", after(ids, mlp_oth), [*act, *hid, downs_of(wb), downs_of(wb_oth)],
        [sds((seqs, block, width), F32), sds((seqs, block, width), BF16)],
        us=0.5,
    )
    mlp_own = call(
        partial(mlp_grads_kernel, seqs, rows), "mlp_grads_own", after(ids, keep_out, gnm_rcv[0]),
        [*nm, *columns(gu, 0), *columns(act, 0), cot0, cot2], apart, scratch=grad_scratch, us=50,
    )
    if stepwise():
        crossing = add(mlp_own[1], mlp_rcv[1])
        back_turn = after(ids, crossing)
        crossing = flip(crossing, "dp", 1)
        mlp_pieces = sum_ring(add(mlp_own[0], mlp_rcv[0], crossing))
    else:
        crossing = mlp_own[0] + mlp_rcv
        back_turn = after(ids, crossing)
        mlp_pieces = sum_rows_any(crossing)
    grad_up, grad_down, gain_mlp_part = call(
        partial(finish_mlp_kernel, len(mlp_pieces)), "finish_mlp", ids, [*mlp_pieces, w_up],
        [sds((rows, ff), F32), sds((ff, rows), F32), sds((rows, 128), F32)],
    )

    gh, gh_full, gq_own, gq_rcv, gq, keep_in, in_rcv = ([] for _ in range(7))

    def back_input(s, turn):
        got = call(
            normed_back_kernel, f"normed_back{s}", turn, [gq_own[s], gq_rcv[s], wa, wa_oth],
            [sds((block, width), F32), sds((block, width), BF16)],
        )
        keep_in.append(got[0])
        in_rcv.append(flip(got[1], "tensor", 2))

    turn = back_turn
    for s in range(seqs):
        got = call(
            hidden_back_kernel, f"hidden_back{s}", turn,
            [gnm[s], gnm_rcv[s], unit[s], inv[s], part(cot0, s), part(cot2, s), gains],
            [sds((block, width), F32), sds((2, block, width), BF16)],
        )
        gh.append(got[0])
        gh_rcv = flip(got[1], "tensor", 1)
        if s == seqs - 1:
            back_input(0, after(ids, gh[-1]))
        wide = sds((2, block, 3 * qw + 64), BF16)
        got = call(
            attend_back_kernel, f"attend_back{s}", ids if s == 0 else after(ids, crossing, keep_in[0]),
            [starts[s : s + 1], qkv[s], mix_t[s], lse[s], got[1], gh_rcv, outs_of(wb)],
            [wide, wide, sds((length, 3 * qw), BF16), sds((length, width), BF16)],
            scratch=[
                pltpu.VMEM((length, qw), BF16), pltpu.VMEM((qw, length), BF16),
                pltpu.VMEM((qw, length), BF16), pltpu.VMEM((qw, length), BF16),
                pltpu.VMEM((8, length), F32), pltpu.VMEM((heads, length, HD), F32),
                pltpu.VMEM((heads, length, HD), F32),
            ],
            us=7,
        )
        gq_own.append(got[0])
        gq_rcv.append(flip(got[1], "tensor", 1))
        gq.append(got[2])
        gh_full.append(got[3])
        turn = after(ids, got[0])
    attn_own = call(
        partial(attn_grads_kernel, seqs, rows), "attn_grads", after(ids, mlp_pieces[1 % len(mlp_pieces)], in_rcv[0]), [*normed, *gq, *gh_full, *mix_n],
        attn_apart, scratch=[pltpu.VMEM((width, 4 * qw), F32)], us=5,
    )
    if stepwise():
        attn_rcv = flip(attn_own[1], "dp", 1)
    for s in range(1, seqs):
        back_input(s, after(ids, attn_own[0]))
    out_rcv = flip(after(send_out, gh[-1]), "tensor", 2)
    output = keep_out + out_rcv.astype(F32)

    if stepwise():
        attn_pieces = sum_ring(add(after(attn_own[0], keep_in[1], grad_up, output), attn_rcv))
    else:
        attn_pieces = sum_rows_any(attn_own[0])
    input_grad = call(
        partial(input_back_kernel, seqs), "input_back", ids, [*gh, *keep_in, *in_rcv, tok0, gains],
        [sds((seqs, block, width), F32)],
        us=3,
    )[0]

    grad_query, grad_key, grad_value, grad_out, gain_attn_part = call(
        partial(finish_attn_kernel, len(attn_pieces)), "finish_attn", after(ids, input_grad),
        [*attn_pieces, w_query, w_key, w_value],
        [sds((rows, qw), F32)] * 3 + [sds((qw, rows), F32), sds((rows, 128), F32)],
    )

    gain_parts = jnp.stack([gain_attn_part[:, 0], gain_mlp_part[:, 0]])
    gain_parts = sum([gain_parts] + [flip(gain_parts, "tensor", bits) for bits in (1, 2, 3)])
    return (
        output, input_grad, grad_query, grad_key, grad_value, grad_out, grad_up, grad_down,
        gain_parts[0] / gain_attn.astype(F32), gain_parts[1] / gain_mlp.astype(F32),
    )


def solution(mesh):
    in_specs = (
        P("dp", "tensor", None),
        P("dp", None),
        P("dp", "tensor"),
        P("dp", "tensor"),
        P("dp", "tensor"),
        P("tensor", "dp"),
        P("dp", "tensor"),
        P("tensor", "dp"),
        P("dp"),
        P("dp"),
        P("dp", "tensor", None),
    )
    out_specs = (
        P("dp", "tensor", None),
        P("dp", "tensor", None),
        P("dp", "tensor"),
        P("dp", "tensor"),
        P("dp", "tensor"),
        P("tensor", "dp"),
        P("dp", "tensor"),
        P("tensor", "dp"),
        P("dp"),
        P("dp"),
    )
    return jax.shard_map(body, mesh=mesh, in_specs=in_specs, out_specs=out_specs, check_vma=False)
```

```python
import math
from functools import partial

import jax
import jax.numpy as jnp
import numpy as np
from jax import lax
from jax.experimental import pallas as pl
from jax.experimental.pallas import tpu as pltpu
from jax.sharding import PartitionSpec as P

HD = 64
DOC_MOST = 512
EPS = 1e-05
NEGATIVE = -1e30
COST = 5e8
SCALE = HD ** (-0.5)
GELU_A = 0.7978845608028654
GELU_B = 0.044715
F32 = jnp.float32
BF16 = jnp.bfloat16


def nn(left, right):
    return lax.dot_general(left, right, (((1,), (0,)), ((), ())), preferred_element_type=F32)


def nt(left, right):
    return lax.dot_general(left, right, (((1,), (1,)), ((), ())), preferred_element_type=F32)


def tn(left, right):
    return lax.dot_general(left, right, (((0,), (0,)), ((), ())), preferred_element_type=F32)


def unit_of(rows):
    center = rows - jnp.mean(rows, axis=-1, keepdims=True)
    spread = jnp.mean(center * center, axis=-1, keepdims=True)
    inverse = lax.rsqrt(spread + EPS)
    return center * inverse, inverse


def norm_back(incoming, unit, inverse, gain):
    scaled = incoming * gain
    return inverse * (
        scaled
        - jnp.mean(scaled, axis=-1, keepdims=True)
        - unit * jnp.mean(scaled * unit, axis=-1, keepdims=True)
    )


def nbytes_of(shapes):
    return sum(math.prod(x.shape) * jnp.dtype(x.dtype).itemsize for x in shapes)


def part(array, index):
    return array, index, jax.eval_shape(lambda x: x[index], array).shape


def call(body, name, ids, ins, outs, scratch=(), us=2.0):
    ins = [x if isinstance(x, tuple) else (x, None, x.shape) for x in ins]
    arrays = []
    for x, _, _ in ins:
        if not any(x is y for y in arrays):
            arrays.append(x)
    place = [next(i for i, y in enumerate(arrays) if y is x) for x, _, _ in ins]
    count, made = len(arrays), len(outs)

    def kernel(ids_ref, *refs):
        sources, targets, own = refs[:count], refs[count : count + made], refs[count + made :]
        loads = []
        for i, (_, index, _) in enumerate(ins):
            source = sources[place[i]]
            loads.append(source if index is None else source.at[index])
        body(ids_ref, *loads, *targets, *own)

    return pl.pallas_call(
        kernel,
        name=name,
        out_shape=tuple(outs),
        in_specs=[pl.BlockSpec(memory_space=pltpu.SMEM)] + [pl.BlockSpec(memory_space=pltpu.VMEM)] * count,
        out_specs=tuple(pl.BlockSpec(memory_space=pltpu.VMEM) for _ in outs),
        scratch_shapes=list(scratch),
        compiler_params=pltpu.CompilerParams(vmem_limit_bytes=nbytes_of(scratch) + (10 << 20)),
        cost_estimate=pl.CostEstimate(flops=int(us * COST), transcendentals=0, bytes_accessed=0),
    )(ids, *arrays)


def sds(shape, dtype):
    return jax.ShapeDtypeStruct(shape, dtype)


def gains_kernel(lane, ids, wa, out):
    out[...] = wa[:, lane : lane + 128].astype(F32).T[64:72, :]


def place_kernel(rows, ids, *refs):
    pieces, out = refs[:-1], refs[-1]
    for k, piece in enumerate(pieces):
        out[pl.ds(pl.multiple_of(ids[1 + k] * rows, 16), rows), :] = piece[...]


def place_gains_kernel(rows, lane, ids, *refs):
    out, gains = refs[-2:]
    place_kernel(rows, ids, *refs[:-1])
    gains_kernel(lane, ids, out, gains)


def attend_kernel(
    ids, tok0, tok1, tok2, tok3, wa, gains, start,
    normed_o, qkv_o, mix_t_o, mix_n_o, mix_own_o, mix_oth_o, lse_o, q_t, v_t,
):
    t = ids[0]
    heads = mix_t_o.shape[0] // HD
    width = heads * HD
    block = tok0.shape[0]
    gain = gains[0:1, :]
    for j, tok in enumerate((tok0, tok1, tok2, tok3)):
        unit, _ = unit_of(tok[...].astype(F32))
        place = pl.multiple_of((t ^ j) * block, block)
        normed_o[pl.ds(place, block), :] = (unit * gain).astype(BF16)
    count = normed_o.shape[0] // block
    for g in range(count):
        here = slice(g * block, (g + 1) * block)
        got = nn(normed_o[here, :], wa[:, : 3 * width])
        qkv_o[here, :width] = (got[:, :width] * SCALE).astype(BF16)
        qkv_o[here, width:] = got[:, width:].astype(BF16)
        q_t[:, here] = (got[:, :width] * SCALE).T.astype(BF16)
        v_t[:, here] = got[:, 2 * width :].T.astype(BF16)
    lse_o[...] = jnp.zeros_like(lse_o)
    for g in range(count):
        low = max(0, g - (DOC_MOST + block - 2) // block)
        here = slice(g * block, (g + 1) * block)
        keys = slice(low * block, (g + 1) * block)
        span = (g + 1 - low) * block
        row = lax.broadcasted_iota(jnp.int32, (span, block), 0) + low * block
        column = lax.broadcasted_iota(jnp.int32, (span, block), 1) + g * block
        valid = (row <= column) & (row >= start[0:1, here])
        for h in range(heads):
            lanes = slice(h * HD, (h + 1) * HD)
            klanes = slice(width + h * HD, width + (h + 1) * HD)
            scores = nn(qkv_o[keys, klanes], q_t[lanes, here])
            scores = jnp.where(valid, scores, NEGATIVE)
            highest = jnp.max(scores, axis=0, keepdims=True)
            weights = jnp.exp(scores - highest)
            total = jnp.sum(weights, axis=0, keepdims=True)
            mixed = nn(v_t[lanes, keys], weights.astype(BF16)) / total
            mix_t_o[lanes, here] = mixed.astype(BF16)
            lse_o[h : h + 1, here] = highest + jnp.log(total)
        mix_n_o[here, :] = mix_t_o[:, here].astype(F32).T.astype(BF16)
    for j in range(4):
        place = pl.multiple_of((t ^ j) * block, block)
        target = mix_own_o if j % 2 == 0 else mix_oth_o
        target[j // 2] = mix_n_o[pl.ds(place, block), :]


def mlp_kernel(
    ids, tok0, tok2, mix_own, mix_c, wo, wo_oth, mix_y, mix_cy, gains, cot0, cot2, wup, wd, wup_oth, wd_oth,
    unit_o, inv_o, hid_o, nm_o, act_o, gu_o, gnm_o,
):
    gain = gains[1:2, :]
    block = tok0.shape[0]
    qw = mix_own.shape[2]
    ff = wup.shape[1]
    step = 256
    for k, (tok, cot) in enumerate(((tok0, cot0), (tok2, cot2))):
        here = slice(k * block, (k + 1) * block)
        hidden = tok[...].astype(F32) + (
            (nt(mix_own[k], wo[:, :qw]) + nt(mix_c[k], wo_oth[:, :qw]))
            + (nt(mix_y[1 - k], wo[:, qw:]) + nt(mix_cy[1 - k], wo_oth[:, qw:]))
        )
        if k == 0:
            hid_o[...] = hidden
        unit, inverse = unit_of(hidden)
        unit_o[here, :] = unit
        inv_o[here, :] = jnp.broadcast_to(inverse, (block, 128))
        nm_o[here, :] = (unit * gain).astype(BF16)
        back = jnp.zeros((block, tok.shape[1]), F32)
        for h, (up_w, down_w) in enumerate(((wup, wd), (wup_oth, wd_oth))):
            for c in range(0, ff, step):
                cols = slice(c, c + step)
                to = slice(h * ff + c, h * ff + c + step)
                up = up_w[:, cols]
                u = nn(nm_o[here, :], up)
                ga = nn(cot[...], down_w[:, cols])
                square = u * u
                th = jnp.tanh(GELU_A * (u + GELU_B * square * u))
                half = 0.5 * (1.0 + th)
                slope = half + 0.5 * u * (1.0 - th * th) * (GELU_A + (3.0 * GELU_A * GELU_B) * square)
                act_o[here, to] = (u * half).astype(BF16)
                gu = (ga * slope).astype(BF16)
                gu_o[here, to] = gu
                back = back + nt(gu, up)
        gnm_o[k] = back.astype(BF16)


def down_kernel(seqs, ids, *refs):
    act, hid = refs[:seqs], refs[seqs : 2 * seqs]
    wd, wd_oth, keep_o, send_o = refs[2 * seqs :]
    block = hid[0].shape[0]
    ff = wd.shape[1]
    for s in range(seqs):
        for k in (1, 0):
            here = slice(k * block, (k + 1) * block)
            got = nt(act[s][here, :ff], wd[...]) + nt(act[s][here, ff:], wd_oth[...])
            if k == 0:
                keep_o[s] = hid[s][...] + got
            else:
                send_o[s] = got.astype(BF16)


def deal(ids, order, total, rows, cols, outs):
    if len(outs) == 1 and len(outs[0].shape) == 2:
        outs[0][:, cols] = total[...].astype(BF16)
        return
    at = 1 + order * (ids.shape[0] // 3)
    for out in outs:
        lead = out.shape[:-2]
        for k in range(math.prod(lead)):
            start = pl.multiple_of(ids[at] * rows, 8)
            got = total[pl.ds(start, rows), :].astype(BF16)
            if len(lead) == 2:
                out[k // lead[1], k % lead[1], :, cols] = got
            else:
                out[k, :, cols] = got
            at += 1


def mlp_grads_kernel(seqs, rows, ids, *refs):
    nm, gu, act = (refs[i * seqs : (i + 1) * seqs] for i in range(3))
    cot0, cot2 = refs[3 * seqs : 3 * seqs + 2]
    outs, total = refs[3 * seqs + 2 : -1], refs[-1]
    block = cot0.shape[1]
    ff = gu[0].shape[1]
    step = total.shape[1]
    one, two = slice(0, block), slice(block, 2 * block)
    for c in range(0, ff, step):
        cols = slice(c, c + step)
        got = None
        for s in range(seqs):
            more = tn(nm[s][...], gu[s][:, cols])
            got = more if got is None else got + more
        total[...] = got
        deal(ids, 1, total, rows, cols, outs)
        got = None
        for s in range(seqs):
            more = tn(cot0[s], act[s][one, cols]) + tn(cot2[s], act[s][two, cols])
            got = more if got is None else got + more
        total[...] = got
        deal(ids, 1, total, rows, slice(ff + c, ff + c + step), outs)


def hidden_back_kernel(ids, gnm_own, gnm_rcv, unit, inv, cot0, cot2, gains, gh_o, ghb_o):
    gain = gains[1:2, :]
    block = cot0.shape[0]
    for k, cot in enumerate((cot0, cot2)):
        here = slice(k * block, (k + 1) * block)
        incoming = gnm_own[k].astype(F32) + gnm_rcv[1 - k].astype(F32)
        gh = cot[...].astype(F32) + norm_back(incoming, unit[here, :], inv[here, 0:1], gain)
        if k == 0:
            gh_o[...] = gh
        ghb_o[k] = gh.astype(BF16)


def attend_back_kernel(
    ids, start, qkv, mix_t, lse, gh_own, gh_rcv, wo, gq_own_o, gq_oth_o, gq_o, gh_o,
    gm_n, gm_t, q_t, k_t, inner, acc_k, acc_v,
):
    t = ids[0]
    width = mix_t.shape[0]
    heads = width // HD
    block = gh_own.shape[1]
    count = qkv.shape[0] // block
    for j in range(4):
        place = pl.multiple_of((t ^ j) * block, block)
        gh_o[pl.ds(place, block), :] = (gh_own if j % 2 == 0 else gh_rcv)[j // 2]
    for g in range(count):
        here = slice(g * block, (g + 1) * block)
        q_t[:, here] = qkv[here, :width].astype(F32).T.astype(BF16)
        k_t[:, here] = qkv[here, width : 2 * width].astype(F32).T.astype(BF16)
        grad_mix = nn(gh_o[here, :], wo[:, :width]).astype(BF16)
        gm_n[here, :] = grad_mix
        turned = grad_mix.astype(F32).T
        gm_t[:, here] = turned.astype(BF16)
        both = turned * mix_t[:, here].astype(F32)
        for h in range(heads):
            inner[h : h + 1, here] = jnp.sum(both[h * HD : (h + 1) * HD, :], axis=0, keepdims=True)
    acc_k[...] = jnp.zeros_like(acc_k)
    acc_v[...] = jnp.zeros_like(acc_v)
    for g in range(count):
        low = max(0, g - (DOC_MOST + block - 2) // block)
        here = slice(g * block, (g + 1) * block)
        keys = slice(low * block, (g + 1) * block)
        span = (g + 1 - low) * block
        row = lax.broadcasted_iota(jnp.int32, (span, block), 0) + low * block
        column = lax.broadcasted_iota(jnp.int32, (span, block), 1) + g * block
        valid = (row <= column) & (row >= start[0:1, here])
        for h in range(heads):
            lanes = slice(h * HD, (h + 1) * HD)
            klanes = slice(width + h * HD, width + (h + 1) * HD)
            vlanes = slice(2 * width + h * HD, 2 * width + (h + 1) * HD)
            scores = jnp.where(valid, nn(qkv[keys, klanes], q_t[lanes, here]), NEGATIVE)
            probs = jnp.exp(scores - lse[h : h + 1, here])
            grad_probs = nn(qkv[keys, vlanes], gm_t[lanes, here])
            grad_scores = (probs * (grad_probs - inner[h : h + 1, here])).astype(BF16)
            acc_k[h, keys, :] += nn(grad_scores, qkv[here, lanes])
            acc_v[h, keys, :] += nn(probs.astype(BF16), gm_n[here, lanes])
            grad_q = nn(k_t[lanes, keys], grad_scores) * SCALE
            gq_o[here, lanes] = grad_q.T.astype(BF16)
    for h in range(heads):
        gq_o[:, width + h * HD : width + (h + 1) * HD] = acc_k[h].astype(BF16)
        gq_o[:, 2 * width + h * HD : 2 * width + (h + 1) * HD] = acc_v[h].astype(BF16)
    for j in range(4):
        place = pl.multiple_of((t ^ j) * block, block)
        target = gq_own_o if j % 2 == 0 else gq_oth_o
        target[j // 2, :, : 3 * width] = gq_o[pl.ds(place, block), :]


def attn_grads_kernel(seqs, rows, ids, *refs):
    normed, gq, gh, mix = (refs[i * seqs : (i + 1) * seqs] for i in range(4))
    outs, total = refs[4 * seqs : -1], refs[-1]
    wide = gq[0].shape[1]
    for cols, left, right in ((slice(0, wide), normed, gq), (slice(wide, None), gh, mix)):
        got = None
        for s in range(seqs):
            more = tn(left[s][...], right[s][...])
            got = more if got is None else got + more
        total[:, cols] = got
    deal(ids, 1, total, rows, slice(None), outs)


def normed_back_kernel(seqs, ids, *refs):
    gq_own, gq_rcv = refs[:seqs], refs[seqs : 2 * seqs]
    wa_own, wa_oth, keep_o, send_o = refs[2 * seqs :]
    width = gq_own[0].shape[2] // 128 * 128 - 64
    for k in (1, 0):
        for s in range(seqs):
            own, rcv = gq_own[s][k, :, :width], gq_rcv[s][k, :, :width]
            got = nt(own, wa_own[:, :width]) + nt(rcv, wa_oth[:, :width])
            if k == 0:
                keep_o[s] = got
            else:
                send_o[s] = got.astype(BF16)


def finish_attn_kernel(count, ids, *refs):
    pieces, weights, outs = refs[:count], refs[count : count + 3], refs[count + 3 :]
    total = pieces[0][...].astype(F32)
    for piece in pieces[1:]:
        total = total + piece[...].astype(F32)
    width = outs[0].shape[1]
    gain = None
    for i in range(3):
        grad = total[:, i * width : (i + 1) * width]
        outs[i][...] = grad
        line = jnp.sum(grad * weights[i][...].astype(F32), axis=1, keepdims=True)
        gain = line if gain is None else gain + line
    outs[3][...] = total[:, 3 * width :].T
    outs[4][...] = jnp.broadcast_to(gain, outs[4].shape)


def finish_mlp_kernel(count, ids, *refs):
    pieces, weight, outs = refs[:count], refs[count], refs[count + 1 :]
    total = pieces[0][...].astype(F32)
    for piece in pieces[1:]:
        total = total + piece[...].astype(F32)
    width = outs[0].shape[1]
    outs[0][...] = total[:, :width]
    outs[1][...] = total[:, width:].T
    gain = jnp.sum(total[:, :width] * weight[...].astype(F32), axis=1, keepdims=True)
    outs[2][...] = jnp.broadcast_to(gain, outs[2].shape)


def input_back_kernel(seqs, ids, *refs):
    gh = refs[:seqs]
    keep, rcv, tok0, gains, out = refs[seqs:]
    for s in range(seqs):
        unit, inverse = unit_of(tok0[s].astype(F32))
        incoming = keep[s] + rcv[s].astype(F32)
        out[s] = gh[s][...] + norm_back(incoming, unit, inverse, gains[0:1, :])


def flip(array, axis, bit):
    size = lax.axis_size(axis)
    return lax.ppermute(array, axis, [(i, i ^ bit) for i in range(size)])


def ring(array, axis, step):
    size = lax.axis_size(axis)
    return lax.ppermute(array, axis, [(i, (i + step) % size) for i in range(size)])


def after(value, *others):
    return lax.optimization_barrier((value, *others))[0]


def stepwise():
    return lax.axis_size("dp") == 8


def together(*values):
    return lax.optimization_barrier(values)


def places():
    size, wide = lax.axis_size("dp"), lax.axis_size("tensor")
    table = np.zeros((size * wide, 1 + 3 * size), np.int32)
    for me in range(size):
        half = range(size // 2)
        for low, line in (
            (0, [(me - 2 * k) % size for k in half]),
            (1, [(me + 2 * k) % size for k in half]),
            (2, [me % 2 + 2 * k for k in half]),
        ):
            for t in range(wide):
                row = table[me * wide + t]
                row[0] = t
                row[1 + low * size : 1 + (low + 1) * size] = line + [p ^ 1 for p in line]
    return lax.dynamic_index_in_dim(jnp.asarray(table), lax.axis_index(("dp", "tensor")), 0, keepdims=False)


def add(*blocks):
    return sum(block.astype(F32) for block in blocks).astype(BF16)


def sum_far(total):
    size = lax.axis_size("dp")
    groups = [[2 * k + low for k in range(size // 2)] for low in range(2)]
    got = lax.all_to_all(total, "dp", split_axis=0, concat_axis=0, tiled=True, axis_index_groups=groups)
    return [got[k] for k in range(size // 2)]


def sum_ring(total):
    return [total[0]] + [ring(total[r], "dp", 2 * r) for r in range(1, total.shape[0])]


def sum_rows_any(grads):
    size = lax.axis_size("dp")
    blocks = grads.reshape(size, -1, grads.shape[1])
    arrived = lax.all_to_all(blocks, "dp", split_axis=0, concat_axis=0, tiled=True)
    return [arrived.astype(F32).sum(axis=0)]


def body(
    tokens, segment_ids, w_query, w_key, w_value, w_out, w_up, w_down, gain_attn, gain_mlp, cotangent
):
    seqs, block, width = tokens.shape
    length = segment_ids.shape[1]
    qw = w_query.shape[1]
    ff = w_up.shape[1]
    rows = w_query.shape[0]
    size = lax.axis_size("dp")
    heads = qw // HD
    ids = places()
    act_rows = 2 * block

    gain_pair = jnp.stack([gain_attn, gain_mlp], axis=1)
    pack_a = jnp.concatenate(
        [w_query, w_key, w_value, jnp.pad(gain_pair, ((0, 0), (0, 62)))], axis=1
    )
    lane = 3 * qw - 64
    shape_a, shape_g = sds((width, 3 * qw + 64), BF16), sds((8, width), F32)
    out_turned = w_out.T
    tok0, cot0 = tokens, cotangent
    if stepwise():
        tok2, tok1 = flip(tok0, "tensor", 2), flip(tok0, "tensor", 1)
        a_p, a_m, a_x0 = ring(pack_a, "dp", 2), ring(pack_a, "dp", -2), flip(pack_a, "dp", 1)
        a_p, a_m, a_x0, tok1 = together(a_p, a_m, a_x0, tok1)
        out_y = flip(after(out_turned, ids, tok1), "tensor", 2)
        a_2, a_xp, a_xm = ring(a_p, "dp", 2), flip(a_p, "dp", 1), flip(a_m, "dp", 1)
        a_2, a_xp, a_xm, tok2, out_y = together(a_2, a_xp, a_xm, tok2, out_y)
        pack_b = jnp.concatenate([out_turned, out_y, w_up, w_down.T], axis=1)
        a_x2, tok3, b_p = flip(a_2, "dp", 1), flip(tok2, "tensor", 1), ring(pack_b, "dp", 2)
        cot2 = flip(after(cot0, tok2), "tensor", 2)
        a_x2, b_p, tok3 = together(a_x2, b_p, tok3)
        b_2, b_m, b_x0 = ring(b_p, "dp", 2), ring(after(pack_b, b_p), "dp", -2), flip(after(pack_b, b_p), "dp", 1)
        wa, gains = call(
            partial(place_gains_kernel, rows, lane), "place_a", ids,
            [pack_a, a_p, a_2, a_m, a_x0, a_xp, a_x2, a_xm], [shape_a, shape_g],
        )
        b_xp = flip(after(b_p, wa), "dp", 1)
        start_turn = after(ids, wa)
    else:
        out_y = flip(out_turned, "tensor", 2)
        pack_b = jnp.concatenate([out_turned, out_y, w_up, w_down.T], axis=1)
        tok1, tok2, cot2 = flip(tok0, "tensor", 1), flip(tok0, "tensor", 2), flip(cot0, "tensor", 2)
        tok3 = flip(tok2, "tensor", 1)
        wa = lax.all_gather(pack_a, "dp", axis=0, tiled=True)
        gains = call(partial(gains_kernel, lane), "gains", ids, [wa], [shape_g])[0]
        wb = lax.all_gather(pack_b, "dp", axis=0, tiled=True)
        start_turn = ids

    def cut(array, low, count):
        return part(array, (slice(None), pl.ds(low, count)))

    def outs_of(array):
        return cut(array, 0, 2 * qw)

    def ups_of(array):
        return cut(array, 2 * qw, ff)

    def downs_of(array):
        return cut(array, 2 * qw + ff, ff)

    starts = jnp.sum(
        (segment_ids[:, None, :] < segment_ids[:, :, None]).astype(jnp.int32), axis=-1
    )

    normed, qkv, mix_t, mix_n, mix_own, mix_c, mix_y, mix_cy, lse = ([] for _ in range(9))
    turn = start_turn
    for s in range(seqs):
        got = call(
            attend_kernel, f"attend{s}", turn,
            [*(part(x, s) for x in (tok0, tok1, tok2, tok3)), wa, gains, starts[s : s + 1]],
            [
                sds((length, width), BF16), sds((length, 3 * qw), BF16), sds((qw, length), BF16),
                sds((length, qw), BF16), sds((2, block, qw), BF16), sds((2, block, qw), BF16),
                sds((8, length), F32),
            ],
            scratch=[pltpu.VMEM((qw, length), BF16), pltpu.VMEM((qw, length), BF16)],
            us=11,
        )
        for target, value in zip((normed, qkv, mix_t, mix_n, mix_own), got):
            target.append(value)
        lse.append(got[6])
        own, oth = together(mix_own[s], got[5], *mix_y, *mix_c, *mix_cy)[:2]
        mix_y.append(flip(own, "tensor", 2))
        mix_c.append(flip(oth, "tensor", 1))
        mix_cy.append(flip(oth, "tensor", 3))
        turn = after(ids, mix_own[s])
        if s == 0 and stepwise():
            b_2, b_m, b_x0, b_xp = together(b_2, b_m, b_x0, b_xp, cot2, mix_own[0])[:4]
            b_x2, b_xm = flip(b_2, "dp", 1), flip(b_m, "dp", 1)
            turn = after(ids, b_2)
    if stepwise():
        wb = call(
            partial(place_kernel, rows), "place_b", after(ids, mix_own[-1], mix_y[0], mix_c[0], mix_cy[0]),
            [pack_b, b_p, b_2, b_m, b_x0, b_xp, b_x2, b_xm],
            [sds((width, 2 * qw + 2 * ff), BF16)],
        )[0]
    wb_oth = flip(wb, "tensor", 1)

    unit, inv, hid, nm, act, gu, gnm, gnm_rcv = ([] for _ in range(8))
    turn = ids
    for s in range(seqs):
        got = call(
            mlp_kernel, f"mlp{s}", turn,
            [
                part(tok0, s), part(tok2, s), mix_own[s], mix_c[s], outs_of(wb), outs_of(wb_oth), mix_y[s], mix_cy[s],
                gains, part(cot0, s), part(cot2, s), ups_of(wb), downs_of(wb), ups_of(wb_oth), downs_of(wb_oth),
            ],
            [
                sds((act_rows, width), F32), sds((act_rows, 128), F32), sds((block, width), F32),
                sds((act_rows, width), BF16), sds((act_rows, 2 * ff), BF16), sds((act_rows, 2 * ff), BF16),
                sds((2, block, width), BF16),
            ],
            us=9,
        )
        for target, value in zip((unit, inv, hid, nm, act, gu, gnm), got):
            target.append(value)
        gnm_rcv.append(flip(after(gnm[s], mix_y[-1], mix_c[-1], mix_cy[-1]), "tensor", 2))
        if s == 0:
            wa_oth = flip(after(wa, gnm[0]), "tensor", 1)
        turn = after(ids, gnm[s])

    half_dp = size // 2
    if stepwise():
        apart = [sds((half_dp, rows, 2 * ff), BF16)] * 2
        paired = [sds((2, half_dp, rows, 2 * ff), BF16)]
        attn_apart = [sds((half_dp, rows, 4 * qw), BF16)] * 2
    else:
        apart = paired = [sds((width, 2 * ff), BF16)]
        attn_apart = [sds((width, 4 * qw), BF16)]
    grad_scratch = [pltpu.VMEM((width, 256), F32)]

    def columns(arrays, h):
        return [cut(x, h * ff, ff) for x in arrays]

    mlp_oth = call(
        partial(mlp_grads_kernel, seqs, rows), "mlp_grads_oth", after(ids, gnm[-1]),
        [*nm, *columns(gu, 1), *columns(act, 1), cot0, cot2], paired, scratch=grad_scratch, us=0.5,
    )[0]
    mlp_rcv = flip(mlp_oth, "tensor", 1)
    keep_out, send_out = call(
        partial(down_kernel, seqs), "down", after(ids, mlp_oth), [*act, *hid, downs_of(wb), downs_of(wb_oth)],
        [sds((seqs, block, width), F32), sds((seqs, block, width), BF16)],
        us=0.5,
    )
    def own_side(turn):
        mlp_own = call(
            partial(mlp_grads_kernel, seqs, rows), "mlp_grads_own", turn,
            [*nm, *columns(gu, 0), *columns(act, 0), cot0, cot2], apart, scratch=grad_scratch, us=50,
        )
        if stepwise():
            near, far = slice(0, half_dp // 2), slice(half_dp // 2, half_dp)
            crossing_in = [add(mlp_own[1][half], mlp_rcv[1][half]) for half in (far, near)]
            crossing, later = (flip(x, "dp", 1) for x in crossing_in)
            far_sum = add(mlp_own[0][far], mlp_rcv[0][far], crossing)
            mlp_pieces = [ring(far_sum[k], "dp", 2 * (k + half_dp // 2)) for k in range(half_dp - half_dp // 2)]
            rest = mlp_own[0][near], mlp_rcv[0][near], later
        else:
            crossing = mlp_own[0] + mlp_rcv
            crossing_in, mlp_pieces, rest = [crossing], sum_rows_any(crossing), ()
        return crossing_in, crossing, mlp_pieces, rest

    gh, gh_full, gq_own, gq_rcv, gq = ([] for _ in range(5))

    turn = after(ids, keep_out)
    for s in range(seqs):
        got = call(
            hidden_back_kernel, f"hidden_back{s}", turn,
            [gnm[s], gnm_rcv[s], unit[s], inv[s], part(cot0, s), part(cot2, s), gains],
            [sds((block, width), F32), sds((2, block, width), BF16)],
        )
        gh.append(got[0])
        gh_rcv = flip(got[1], "tensor", 1)
        if s == 0:
            crossing_in, crossing, mlp_pieces, rest = own_side(after(ids, gh[0], wa_oth))
        wide = sds((2, block, 3 * qw + 64), BF16)
        got = call(
            attend_back_kernel, f"attend_back{s}", after(ids, *crossing_in) if s == 0 else after(ids, crossing),
            [starts[s : s + 1], qkv[s], mix_t[s], lse[s], got[1], gh_rcv, outs_of(wb)],
            [wide, wide, sds((length, 3 * qw), BF16), sds((length, width), BF16)],
            scratch=[
                pltpu.VMEM((length, qw), BF16), pltpu.VMEM((qw, length), BF16),
                pltpu.VMEM((qw, length), BF16), pltpu.VMEM((qw, length), BF16),
                pltpu.VMEM((8, length), F32), pltpu.VMEM((heads, length, HD), F32),
                pltpu.VMEM((heads, length, HD), F32),
            ],
            us=7,
        )
        gq_own.append(got[0])
        gq_rcv.append(flip(got[1], "tensor", 1))
        gq.append(got[2])
        gh_full.append(got[3])
        turn = after(ids, got[0])
    attn_own = call(
        partial(attn_grads_kernel, seqs, rows), "attn_grads", ids, [*normed, *gq, *gh_full, *mix_n],
        attn_apart, scratch=[pltpu.VMEM((width, 4 * qw), F32)], us=8,
    )
    if stepwise():
        mlp_pieces = sum_ring(add(*together(*rest, attn_own[0])[:3])) + mlp_pieces
        attn_rcv = flip(attn_own[1], "dp", 1)
    both = sds((seqs, block, width), F32), sds((seqs, block, width), BF16)
    keep_in, send_in = call(
        partial(normed_back_kernel, seqs), "normed_back", after(ids, attn_own[0]), [*gq_own, *gq_rcv, wa, wa_oth],
        both, us=20,
    )
    in_rcv = flip(send_in, "tensor", 2)
    out_rcv = flip(after(send_out, gh[-1]), "tensor", 2)
    output = keep_out + out_rcv.astype(F32)

    if stepwise():
        attn_pieces = sum_ring(add(after(attn_own[0], keep_in, *mlp_pieces), attn_rcv))
    else:
        attn_pieces = sum_rows_any(attn_own[0])
    grad_up, grad_down, gain_mlp_part = call(
        partial(finish_mlp_kernel, len(mlp_pieces)), "finish_mlp", after(ids, keep_in), [*mlp_pieces, w_up],
        [sds((rows, ff), F32), sds((ff, rows), F32), sds((rows, 128), F32)],
    )
    input_grad = call(
        partial(input_back_kernel, seqs), "input_back", after(ids, output), [*gh, keep_in, in_rcv, tok0, gains],
        [sds((seqs, block, width), F32)],
        us=3,
    )[0]

    grad_query, grad_key, grad_value, grad_out, gain_attn_part = call(
        partial(finish_attn_kernel, len(attn_pieces)), "finish_attn", after(ids, input_grad, grad_up),
        [*attn_pieces, w_query, w_key, w_value],
        [sds((rows, qw), F32)] * 3 + [sds((qw, rows), F32), sds((rows, 128), F32)],
    )

    gain_parts = jnp.stack([gain_attn_part[:, 0], gain_mlp_part[:, 0]])
    gain_parts = sum([gain_parts] + [flip(gain_parts, "tensor", bits) for bits in (1, 2, 3)])
    return (
        output, input_grad, grad_query, grad_key, grad_value, grad_out, grad_up, grad_down,
        gain_parts[0] / gain_attn.astype(F32), gain_parts[1] / gain_mlp.astype(F32),
    )


def solution(mesh):
    in_specs = (
        P("dp", "tensor", None),
        P("dp", None),
        P("dp", "tensor"),
        P("dp", "tensor"),
        P("dp", "tensor"),
        P("tensor", "dp"),
        P("dp", "tensor"),
        P("tensor", "dp"),
        P("dp"),
        P("dp"),
        P("dp", "tensor", None),
    )
    out_specs = (
        P("dp", "tensor", None),
        P("dp", "tensor", None),
        P("dp", "tensor"),
        P("dp", "tensor"),
        P("dp", "tensor"),
        P("tensor", "dp"),
        P("dp", "tensor"),
        P("tensor", "dp"),
        P("dp"),
        P("dp"),
    )
    return jax.shard_map(body, mesh=mesh, in_specs=in_specs, out_specs=out_specs, check_vma=False)
```

```python
import math
from functools import partial

import jax
import jax.numpy as jnp
import numpy as np
from jax import lax
from jax.experimental import pallas as pl
from jax.experimental.pallas import tpu as pltpu
from jax.sharding import PartitionSpec as P

HD = 64
LANES = 128
DOC_MOST = 512
EPS = 1e-05
NEGATIVE = -1e30
COST = 5e8
SCALE = HD ** (-0.5)
GELU_A = 0.7978845608028654
GELU_B = 0.044715
F32 = jnp.float32
BF16 = jnp.bfloat16


def nn(left, right):
    return lax.dot_general(left, right, (((1,), (0,)), ((), ())), preferred_element_type=F32)


def nt(left, right):
    return lax.dot_general(left, right, (((1,), (1,)), ((), ())), preferred_element_type=F32)


def tn(left, right):
    return lax.dot_general(left, right, (((0,), (0,)), ((), ())), preferred_element_type=F32)


def unit_of(rows):
    center = rows - jnp.mean(rows, axis=-1, keepdims=True)
    spread = jnp.mean(center * center, axis=-1, keepdims=True)
    inverse = lax.rsqrt(spread + EPS)
    return center * inverse, inverse


def norm_back(incoming, unit, inverse, gain):
    scaled = incoming * gain
    return inverse * (
        scaled
        - jnp.mean(scaled, axis=-1, keepdims=True)
        - unit * jnp.mean(scaled * unit, axis=-1, keepdims=True)
    )


def nbytes_of(shapes):
    return sum(math.prod(x.shape) * jnp.dtype(x.dtype).itemsize for x in shapes)


def part(array, index):
    return array, index, jax.eval_shape(lambda x: x[index], array).shape


def call(body, name, ids, ins, outs, scratch=(), us=2.0):
    ins = [x if isinstance(x, tuple) else (x, None, x.shape) for x in ins]
    arrays = []
    for x, _, _ in ins:
        if not any(x is y for y in arrays):
            arrays.append(x)
    place = [next(i for i, y in enumerate(arrays) if y is x) for x, _, _ in ins]
    count, made = len(arrays), len(outs)

    def kernel(ids_ref, *refs):
        sources, targets, own = refs[:count], refs[count : count + made], refs[count + made :]
        loads = []
        for i, (_, index, _) in enumerate(ins):
            source = sources[place[i]]
            loads.append(source if index is None else source.at[index])
        body(ids_ref, *loads, *targets, *own)

    return pl.pallas_call(
        kernel,
        name=name,
        out_shape=tuple(outs),
        in_specs=[pl.BlockSpec(memory_space=pltpu.SMEM)] + [pl.BlockSpec(memory_space=pltpu.VMEM)] * count,
        out_specs=tuple(pl.BlockSpec(memory_space=pltpu.VMEM) for _ in outs),
        scratch_shapes=list(scratch),
        compiler_params=pltpu.CompilerParams(vmem_limit_bytes=nbytes_of(scratch) + (10 << 20)),
        cost_estimate=pl.CostEstimate(flops=int(us * COST), transcendentals=0, bytes_accessed=0),
    )(ids, *arrays)


def sds(shape, dtype):
    return jax.ShapeDtypeStruct(shape, dtype)


def gains_kernel(lane, ids, wa, out):
    out[...] = wa[:, lane : lane + 128].astype(F32).T[64:72, :]


def place_kernel(rows, ids, *refs):
    pieces, out = refs[:-1], refs[-1]
    for k, piece in enumerate(pieces):
        out[pl.ds(pl.multiple_of(ids[1 + k] * rows, 16), rows), :] = piece[...]


def place_chunks_kernel(rows, ids, *refs):
    pieces, out = refs[:-1], refs[-1]
    step = out.shape[2]
    for k, piece in enumerate(pieces):
        here = pl.ds(pl.multiple_of(ids[1 + k] * rows, 16), rows)
        for c in range(out.shape[0]):
            out[c, here, :] = piece[:, c * step : (c + 1) * step]


def place_gains_kernel(rows, lane, ids, *refs):
    out, gains = refs[-2:]
    place_kernel(rows, ids, *refs[:-1])
    gains_kernel(lane, ids, out, gains)


def attend_kernel(
    ids, tok0, tok1, tok2, tok3, wa, gains, start,
    normed_o, q_o, k_o, v_o, q_t_o, k_t_o, mix_t_o, mix_n_o, mix_own_o, mix_oth_o, lse_o, v_t, tok,
):
    t = ids[0]
    heads = mix_t_o.shape[0]
    width = heads * HD
    block = tok0.shape[0]
    gain = gains[0:1, :]
    for j, one in enumerate((tok0, tok1, tok2, tok3)):
        tok[j] = one[...]

    def normalize(j, carry):
        unit, _ = unit_of(tok[j].astype(F32))
        place = pl.multiple_of((t ^ j) * block, block)
        normed_o[pl.ds(place, block), :] = (unit * gain).astype(BF16)
        return carry

    lax.fori_loop(0, 4, normalize, 0)
    count = normed_o.shape[0] // block

    def projections(g, carry):
        here = pl.ds(pl.multiple_of(g * block, block), block)
        got = nn(normed_o[here, :], wa[:, : 3 * width])
        for i, (plain, turned) in enumerate(((q_o, q_t_o), (k_o, k_t_o), (v_o, v_t))):
            one = got[:, i * width : (i + 1) * width]
            if i == 0:
                one = one * SCALE
            other = one.T.astype(BF16)
            one = one.astype(BF16)
            for h in range(heads):
                plain[h, here, :] = one[:, h * HD : (h + 1) * HD]
                turned[h, g] = other[h * HD : (h + 1) * HD, :]
        return carry

    lax.fori_loop(0, count, projections, 0)

    def head(h, carry):
        for g in range(count):
            low = max(0, g - (DOC_MOST + block - 2) // block)
            here = slice(g * block, (g + 1) * block)
            keys = slice(low * block, (g + 1) * block)
            span = (g + 1 - low) * block
            row = lax.broadcasted_iota(jnp.int32, (span, block), 0) + low * block
            column = lax.broadcasted_iota(jnp.int32, (span, block), 1) + g * block
            valid = (row <= column) & (row >= start[0:1, here])
            scores = jnp.where(valid, nn(k_o[h, keys, :], q_t_o[h, g]), NEGATIVE)
            highest = jnp.max(scores, axis=0, keepdims=True)
            weights = jnp.exp(scores - highest)
            total = jnp.sum(weights, axis=0, keepdims=True)
            values = jnp.concatenate([v_t[h, i] for i in range(low, g + 1)], axis=1)
            mix_t_o[h, :, here] = (nn(values, weights.astype(BF16)) / total).astype(BF16)
            lse_o[h, :, here] = highest + jnp.log(total)
        return carry

    lax.fori_loop(0, heads, head, 0)
    for g in range(count):
        here = slice(g * block, (g + 1) * block)
        mixed = jnp.concatenate([mix_t_o[h, :, here] for h in range(heads)], axis=0)
        mix_n_o[here, :] = mixed.astype(F32).T.astype(BF16)
    for j in range(4):
        place = pl.multiple_of((t ^ j) * block, block)
        target = mix_own_o if j % 2 == 0 else mix_oth_o
        target[j // 2] = mix_n_o[pl.ds(place, block), :]


def mlp_kernel(
    ids, tok0, tok2, mix_own, mix_c, wo, wo_oth, mix_y, mix_cy, gains, cot0, cot2, wup, wd, wup_oth, wd_oth,
    unit_o, inv_o, hid_o, nm_o, act_o, gu_o, gnm_o, tok, cot,
):
    gain = gains[1:2, :]
    block = tok0.shape[0]
    qw = mix_own.shape[2]
    chunks = wup.shape[0] // 2
    wo, wo_oth = beside(wo, slice(None)), beside(wo_oth, slice(None))
    tok[0], tok[1] = tok0[...], tok2[...]
    cot[0], cot[1] = cot0[...], cot2[...]

    def half_rows(k, carry):
        here = pl.ds(pl.multiple_of(k * block, block), block)
        hidden = tok[k].astype(F32) + (
            (nt(mix_own[k], wo[:, :qw]) + nt(mix_c[k], wo_oth[:, :qw]))
            + (nt(mix_y[1 - k], wo[:, qw:]) + nt(mix_cy[1 - k], wo_oth[:, qw:]))
        )
        hid_o[k] = hidden
        unit, inverse = unit_of(hidden)
        unit_o[here, :] = unit
        inv_o[here, :] = jnp.broadcast_to(inverse, (block, 128))
        nm_o[here, :] = (unit * gain).astype(BF16)
        back = None
        for base, up_w, down_w in ((0, wup, wd), (chunks, wup_oth, wd_oth)):
            for c in range(chunks):
                up = jnp.concatenate([up_w[2 * c], up_w[2 * c + 1]], axis=1)
                u = nn(nm_o[here, :], up)
                ga = nn(cot[k], jnp.concatenate([down_w[2 * c], down_w[2 * c + 1]], axis=1))
                square = u * u
                th = jnp.tanh(GELU_A * (u + GELU_B * square * u))
                half = 0.5 * (1.0 + th)
                slope = half + 0.5 * u * (1.0 - th * th) * (GELU_A + (3.0 * GELU_A * GELU_B) * square)
                act_o[base + c, here, :] = (u * half).astype(BF16)
                gu = (ga * slope).astype(BF16)
                gu_o[base + c, here, :] = gu
                more = nt(gu, up)
                back = more if back is None else back + more
        gnm_o[k] = back.astype(BF16)
        return carry

    lax.fori_loop(0, 2, half_rows, 0)


def beside(array, here):
    return jnp.concatenate([array[c, here, :] for c in range(array.shape[0])], axis=1)


def down_kernel(seqs, ids, *refs):
    act, hid = refs[:seqs], refs[seqs : 2 * seqs]
    wd, wd_oth, keep_o, send_o = refs[2 * seqs :]
    block = hid[0].shape[1]
    weights = jnp.concatenate([beside(wd, slice(None)), beside(wd_oth, slice(None))], axis=1)
    for s in range(seqs):
        for k in (1, 0):
            got = nt(beside(act[s], slice(k * block, (k + 1) * block)), weights)
            if k == 0:
                keep_o[s] = hid[s][0] + got
            else:
                send_o[s] = got.astype(BF16)


def deal(ids, order, total, rows, cols, outs):
    if len(outs) == 1 and len(outs[0].shape) == 2:
        outs[0][:, cols] = total[...].astype(BF16)
        return
    at = 1 + order * (ids.shape[0] // 3)
    for out in outs:
        lead = out.shape[:-2]
        for k in range(math.prod(lead)):
            start = pl.multiple_of(ids[at] * rows, 8)
            got = total[pl.ds(start, rows), :].astype(BF16)
            if len(lead) == 2:
                out[k // lead[1], k % lead[1], :, cols] = got
            else:
                out[k, :, cols] = got
            at += 1


def deal_chunk(ids, total, rows, at_chunk, outs):
    if len(outs) == 1 and len(outs[0].shape) == 3:
        outs[0][at_chunk] = total[...].astype(BF16)
        return
    at = 1 + ids.shape[0] // 3
    for out in outs:
        lead = out.shape[:-3]
        for k in range(math.prod(lead)):
            start = pl.multiple_of(ids[at] * rows, 8)
            got = total[pl.ds(start, rows), :].astype(BF16)
            if len(lead) == 2:
                out[k // lead[1], k % lead[1], at_chunk] = got
            else:
                out[k, at_chunk] = got
            at += 1


def mlp_grads_kernel(seqs, rows, ids, *refs):
    nm, gu, act = (refs[i * seqs : (i + 1) * seqs] for i in range(3))
    cot0, cot2 = refs[3 * seqs : 3 * seqs + 2]
    outs, total = refs[3 * seqs + 2 : -1], refs[-1]
    block = cot0.shape[1]
    chunks = gu[0].shape[0]
    one, two = slice(0, block), slice(block, 2 * block)

    def chunk(c, carry):
        got = None
        for s in range(seqs):
            more = tn(nm[s][...], gu[s][c])
            got = more if got is None else got + more
        total[...] = got
        deal_chunk(ids, total, rows, c, outs)
        got = None
        for s in range(seqs):
            more = tn(cot0[s], act[s][c, one, :]) + tn(cot2[s], act[s][c, two, :])
            got = more if got is None else got + more
        total[...] = got
        deal_chunk(ids, total, rows, chunks + c, outs)
        return carry

    lax.fori_loop(0, chunks, chunk, 0)


def hidden_back_kernel(ids, gnm_own, gnm_rcv, unit, inv, cot0, cot2, gains, gh_o, ghb_o, cot):
    gain = gains[1:2, :]
    block = cot0.shape[0]
    cot[0], cot[1] = cot0[...], cot2[...]

    def half_rows(k, carry):
        here = pl.ds(pl.multiple_of(k * block, block), block)
        incoming = gnm_own[k].astype(F32) + gnm_rcv[1 - k].astype(F32)
        gh = cot[k].astype(F32) + norm_back(incoming, unit[here, :], inv[here, 0:1], gain)
        gh_o[k] = gh
        ghb_o[k] = gh.astype(BF16)
        return carry

    lax.fori_loop(0, 2, half_rows, 0)


def attend_back_kernel(
    ids, start, q_n, k_n, v_n, q_t, k_t, mix_t, lse, gh_own, gh_rcv, wo, gq_own_o, gq_oth_o, gq_o, gh_o,
    gm_n, gm_t, inner, acc_k, acc_v, gq_n, gk_n, gv_n,
):
    t = ids[0]
    heads, length = q_n.shape[0], q_n.shape[1]
    width = heads * HD
    block = gh_own.shape[1]
    count = length // block
    out_w = beside(wo, slice(None))[:, :width]
    for j in range(4):
        place = pl.multiple_of((t ^ j) * block, block)
        gh_o[pl.ds(place, block), :] = (gh_own if j % 2 == 0 else gh_rcv)[j // 2]
    for g in range(count):
        here = slice(g * block, (g + 1) * block)
        grad_mix = nn(gh_o[here, :], out_w).astype(BF16)
        turned = grad_mix.astype(F32).T
        for h in range(heads):
            lanes = slice(h * HD, (h + 1) * HD)
            gm_n[h, here, :] = grad_mix[:, lanes]
            gm_t[h, g] = turned[lanes, :].astype(BF16)
            both = turned[lanes, :] * mix_t[h, :, here].astype(F32)
            inner[h, :, here] = jnp.sum(both, axis=0, keepdims=True)

    def head(h, carry):
        acc_k[...] = jnp.zeros_like(acc_k)
        acc_v[...] = jnp.zeros_like(acc_v)
        for g in range(count):
            low = max(0, g - (DOC_MOST + block - 2) // block)
            here = slice(g * block, (g + 1) * block)
            keys = slice(low * block, (g + 1) * block)
            span = (g + 1 - low) * block
            row = lax.broadcasted_iota(jnp.int32, (span, block), 0) + low * block
            column = lax.broadcasted_iota(jnp.int32, (span, block), 1) + g * block
            valid = (row <= column) & (row >= start[0:1, here])
            scores = jnp.where(valid, nn(k_n[h, keys, :], q_t[h, g]), NEGATIVE)
            probs = jnp.exp(scores - lse[h, :, here])
            grad_probs = nn(v_n[h, keys, :], gm_t[h, g])
            grad_scores = (probs * (grad_probs - inner[h, :, here])).astype(BF16)
            acc_k[keys, :] += nn(grad_scores, q_n[h, here, :])
            acc_v[keys, :] += nn(probs.astype(BF16), gm_n[h, here, :])
            turned = jnp.concatenate([k_t[h, i] for i in range(low, g + 1)], axis=1)
            gq_n[h, here, :] = (nn(turned, grad_scores) * SCALE).T.astype(BF16)
        gk_n[h] = acc_k[...].astype(BF16)
        gv_n[h] = acc_v[...].astype(BF16)
        return carry

    lax.fori_loop(0, heads, head, 0)
    for i, part_n in enumerate((gq_n, gk_n, gv_n)):
        for h in range(heads):
            gq_o[:, i * width + h * HD : i * width + (h + 1) * HD] = part_n[h]
    for j in range(4):
        place = pl.multiple_of((t ^ j) * block, block)
        target = gq_own_o if j % 2 == 0 else gq_oth_o
        target[j // 2, :, : 3 * width] = gq_o[pl.ds(place, block), :]


def attn_grads_kernel(seqs, rows, ids, *refs):
    normed, gq, gh, mix = (refs[i * seqs : (i + 1) * seqs] for i in range(4))
    outs, total = refs[4 * seqs : -1], refs[-1]
    wide = gq[0].shape[1]
    step = 256

    def chunk(c, carry):
        here = pl.ds(pl.multiple_of(c * step, step), step)
        for cols, left, right in ((slice(0, wide), normed, gq), (slice(wide, None), gh, mix)):
            got = None
            for s in range(seqs):
                more = tn(left[s][:, here], right[s][...])
                got = more if got is None else got + more
            total[here, cols] = got
        return carry

    lax.fori_loop(0, total.shape[0] // step, chunk, 0)
    deal(ids, 1, total, rows, slice(None), outs)


def normed_back_kernel(seqs, ids, *refs):
    gq_own, gq_rcv = refs[:seqs], refs[seqs : 2 * seqs]
    wa_own, wa_oth, keep_o, send_o = refs[2 * seqs :]
    width = gq_own[0].shape[2] // 128 * 128 - 64
    for k in (1, 0):
        for s in range(seqs):
            own, rcv = gq_own[s][k, :, :width], gq_rcv[s][k, :, :width]
            got = nt(own, wa_own[:, :width]) + nt(rcv, wa_oth[:, :width])
            if k == 0:
                keep_o[s] = got
            else:
                send_o[s] = got.astype(BF16)


def finish_attn_kernel(count, ids, *refs):
    pieces, weights, outs = refs[:count], refs[count : count + 3], refs[count + 3 :]
    total = pieces[0][...].astype(F32)
    for piece in pieces[1:]:
        total = total + piece[...].astype(F32)
    width = outs[0].shape[1]
    gain = None
    for i in range(3):
        grad = total[:, i * width : (i + 1) * width]
        outs[i][...] = grad
        line = jnp.sum(grad * weights[i][...].astype(F32), axis=1, keepdims=True)
        gain = line if gain is None else gain + line
    outs[3][...] = total[:, 3 * width :].T
    outs[4][...] = jnp.broadcast_to(gain, outs[4].shape)


def finish_mlp_kernel(count, ids, *refs):
    pieces, weight, outs = refs[:count], refs[count], refs[count + 1 :]
    total = pieces[0][...].astype(F32)
    for piece in pieces[1:]:
        total = total + piece[...].astype(F32)
    if len(total.shape) == 3:
        total = jnp.concatenate([total[c] for c in range(total.shape[0])], axis=1)
    width = outs[0].shape[1]
    outs[0][...] = total[:, :width]
    outs[1][...] = total[:, width:].T
    gain = jnp.sum(total[:, :width] * weight[...].astype(F32), axis=1, keepdims=True)
    outs[2][...] = jnp.broadcast_to(gain, outs[2].shape)


def input_back_kernel(seqs, ids, *refs):
    gh = refs[:seqs]
    keep, rcv, tok0, gains, out = refs[seqs:]
    for s in range(seqs):
        unit, inverse = unit_of(tok0[s].astype(F32))
        incoming = keep[s] + rcv[s].astype(F32)
        out[s] = gh[s][0] + norm_back(incoming, unit, inverse, gains[0:1, :])


def flip(array, axis, bit):
    size = lax.axis_size(axis)
    return lax.ppermute(array, axis, [(i, i ^ bit) for i in range(size)])


def ring(array, axis, step):
    size = lax.axis_size(axis)
    return lax.ppermute(array, axis, [(i, (i + step) % size) for i in range(size)])


def after(value, *others):
    return lax.optimization_barrier((value, *others))[0]


def stepwise():
    return lax.axis_size("dp") == 8


def together(*values):
    return lax.optimization_barrier(values)


def places():
    size, wide = lax.axis_size("dp"), lax.axis_size("tensor")
    table = np.zeros((size * wide, 1 + 3 * size), np.int32)
    for me in range(size):
        half = range(size // 2)
        for low, line in (
            (0, [(me - 2 * k) % size for k in half]),
            (1, [(me + 2 * k) % size for k in half]),
            (2, [me % 2 + 2 * k for k in half]),
        ):
            for t in range(wide):
                row = table[me * wide + t]
                row[0] = t
                row[1 + low * size : 1 + (low + 1) * size] = line + [p ^ 1 for p in line]
    return lax.dynamic_index_in_dim(jnp.asarray(table), lax.axis_index(("dp", "tensor")), 0, keepdims=False)


def add(*blocks):
    return sum(block.astype(F32) for block in blocks).astype(BF16)


def sum_far(total):
    size = lax.axis_size("dp")
    groups = [[2 * k + low for k in range(size // 2)] for low in range(2)]
    got = lax.all_to_all(total, "dp", split_axis=0, concat_axis=0, tiled=True, axis_index_groups=groups)
    return [got[k] for k in range(size // 2)]


def sum_ring(total):
    return [total[0]] + [ring(total[r], "dp", 2 * r) for r in range(1, total.shape[0])]


def sum_rows_any(grads):
    size = lax.axis_size("dp")
    blocks = grads.reshape(size, -1, grads.shape[1])
    arrived = lax.all_to_all(blocks, "dp", split_axis=0, concat_axis=0, tiled=True)
    return [arrived.astype(F32).sum(axis=0)]


def body(
    tokens, segment_ids, w_query, w_key, w_value, w_out, w_up, w_down, gain_attn, gain_mlp, cotangent
):
    seqs, block, width = tokens.shape
    length = segment_ids.shape[1]
    qw = w_query.shape[1]
    ff = w_up.shape[1]
    rows = w_query.shape[0]
    size = lax.axis_size("dp")
    heads = qw // HD
    ids = places()
    act_rows = 2 * block

    gain_pair = jnp.stack([gain_attn, gain_mlp], axis=1)
    pack_a = jnp.concatenate(
        [w_query, w_key, w_value, jnp.pad(gain_pair, ((0, 0), (0, 62)))], axis=1
    )
    lane = 3 * qw - 64
    shape_a, shape_g = sds((width, 3 * qw + 64), BF16), sds((8, width), F32)
    out_turned = w_out.T
    tok0, cot0 = tokens, cotangent
    if stepwise():
        tok2, tok1 = flip(tok0, "tensor", 2), flip(tok0, "tensor", 1)
        a_p, a_m, a_x0 = ring(pack_a, "dp", 2), ring(pack_a, "dp", -2), flip(pack_a, "dp", 1)
        a_p, a_m, a_x0, tok1 = together(a_p, a_m, a_x0, tok1)
        out_y = flip(after(out_turned, ids, tok1), "tensor", 2)
        a_2, a_xp, a_xm = ring(a_p, "dp", 2), flip(a_p, "dp", 1), flip(a_m, "dp", 1)
        a_2, a_xp, a_xm, tok2, out_y = together(a_2, a_xp, a_xm, tok2, out_y)
        pack_b = jnp.concatenate([out_turned, out_y, w_up, w_down.T], axis=1)
        a_x2, tok3, b_p = flip(a_2, "dp", 1), flip(tok2, "tensor", 1), ring(pack_b, "dp", 2)
        cot2 = flip(after(cot0, tok2), "tensor", 2)
        a_x2, b_p, tok3 = together(a_x2, b_p, tok3)
        b_2, b_m, b_x0 = ring(b_p, "dp", 2), ring(after(pack_b, b_p), "dp", -2), flip(after(pack_b, b_p), "dp", 1)
        wa, gains = call(
            partial(place_gains_kernel, rows, lane), "place_a", ids,
            [pack_a, a_p, a_2, a_m, a_x0, a_xp, a_x2, a_xm], [shape_a, shape_g],
        )
        b_xp = flip(after(b_p, wa), "dp", 1)
        start_turn = after(ids, wa)
    else:
        out_y = flip(out_turned, "tensor", 2)
        pack_b = jnp.concatenate([out_turned, out_y, w_up, w_down.T], axis=1)
        tok1, tok2, cot2 = flip(tok0, "tensor", 1), flip(tok0, "tensor", 2), flip(cot0, "tensor", 2)
        tok3 = flip(tok2, "tensor", 1)
        wa = lax.all_gather(pack_a, "dp", axis=0, tiled=True)
        gains = call(partial(gains_kernel, lane), "gains", ids, [wa], [shape_g])[0]
        wb = lax.all_gather(pack_b, "dp", axis=0, tiled=True)
        wb = jnp.moveaxis(wb.reshape(width, -1, LANES), 1, 0)
        start_turn = ids

    def cut(array, low, count):
        return part(array, (slice(None), pl.ds(low, count)))

    out_chunks, ff_chunks = 2 * qw // LANES, ff // LANES

    def outs_of(array):
        return part(array, slice(0, out_chunks))

    def ups_of(array):
        return part(array, slice(out_chunks, out_chunks + ff_chunks))

    def downs_of(array):
        return part(array, slice(out_chunks + ff_chunks, out_chunks + 2 * ff_chunks))

    heads_n, heads_t = sds((heads, length, HD), BF16), sds((heads, length // block, HD, block), BF16)
    chunks = ff // 256
    starts = jnp.sum(
        (segment_ids[:, None, :] < segment_ids[:, :, None]).astype(jnp.int32), axis=-1
    )

    normed, qkv, mix_n, mix_own, mix_c, mix_y, mix_cy = ([] for _ in range(7))
    turn = start_turn
    for s in range(seqs):
        got = call(
            attend_kernel, f"attend{s}", turn,
            [*(part(x, s) for x in (tok0, tok1, tok2, tok3)), wa, gains, starts[s : s + 1]],
            [
                sds((length, width), BF16), heads_n, heads_n, heads_n, heads_t, heads_t,
                sds((heads, HD, length), BF16), sds((length, qw), BF16),
                sds((2, block, qw), BF16), sds((2, block, qw), BF16), sds((heads, 1, length), F32),
            ],
            scratch=[
                pltpu.VMEM((heads, length // block, HD, block), BF16), pltpu.VMEM((4, block, width), BF16),
            ],
            us=11,
        )
        normed.append(got[0])
        qkv.append([*got[1:7], got[10]])
        mix_n.append(got[7])
        mix_own.append(got[8])
        own, oth = together(mix_own[s], got[9], *mix_y, *mix_c, *mix_cy)[:2]
        mix_y.append(flip(own, "tensor", 2))
        mix_c.append(flip(oth, "tensor", 1))
        mix_cy.append(flip(oth, "tensor", 3))
        turn = after(ids, mix_own[s])
        if s == 0 and stepwise():
            b_2, b_m, b_x0, b_xp = together(b_2, b_m, b_x0, b_xp, cot2, mix_own[0])[:4]
            b_x2, b_xm = flip(b_2, "dp", 1), flip(b_m, "dp", 1)
            turn = after(ids, b_2)
    if stepwise():
        wb = call(
            partial(place_chunks_kernel, rows), "place_b", after(ids, mix_own[-1], mix_y[0], mix_c[0], mix_cy[0]),
            [pack_b, b_p, b_2, b_m, b_x0, b_xp, b_x2, b_xm],
            [sds((2 * (qw + ff) // LANES, width, LANES), BF16)],
        )[0]
    wb_oth = flip(wb, "tensor", 1)

    unit, inv, hid, nm, act, gu, gnm, gnm_rcv = ([] for _ in range(8))
    turn = ids
    for s in range(seqs):
        got = call(
            mlp_kernel, f"mlp{s}", turn,
            [
                part(tok0, s), part(tok2, s), mix_own[s], mix_c[s], outs_of(wb), outs_of(wb_oth), mix_y[s], mix_cy[s],
                gains, part(cot0, s), part(cot2, s), ups_of(wb), downs_of(wb), ups_of(wb_oth), downs_of(wb_oth),
            ],
            [
                sds((act_rows, width), F32), sds((act_rows, 128), F32), sds((2, block, width), F32),
                sds((act_rows, width), BF16), *[sds((2 * chunks, act_rows, 256), BF16)] * 2,
                sds((2, block, width), BF16),
            ],
            scratch=[pltpu.VMEM((2, block, width), BF16)] * 2,
            us=9,
        )
        for target, value in zip((unit, inv, hid, nm, act, gu, gnm), got):
            target.append(value)
        gnm_rcv.append(flip(after(gnm[s], mix_y[-1], mix_c[-1], mix_cy[-1]), "tensor", 2))
        if s == 0:
            wa_oth = flip(after(wa, gnm[0]), "tensor", 1)
        turn = after(ids, gnm[s])

    half_dp = size // 2
    if stepwise():
        apart = [sds((half_dp, 2 * chunks, rows, 256), BF16)] * 2
        paired = [sds((2, half_dp, 2 * chunks, rows, 256), BF16)]
        attn_apart = [sds((half_dp, rows, 4 * qw), BF16)] * 2
    else:
        apart = paired = [sds((2 * chunks, width, 256), BF16)]
        attn_apart = [sds((width, 4 * qw), BF16)]
    grad_scratch = [pltpu.VMEM((width, 256), F32)]

    def columns(arrays, h):
        return [part(x, slice(h * chunks, (h + 1) * chunks)) for x in arrays]

    mlp_oth = call(
        partial(mlp_grads_kernel, seqs, rows), "mlp_grads_oth", after(ids, gnm[-1]),
        [*nm, *columns(gu, 1), *columns(act, 1), cot0, cot2], paired, scratch=grad_scratch, us=0.5,
    )[0]
    mlp_rcv = flip(mlp_oth, "tensor", 1)
    keep_out, send_out = call(
        partial(down_kernel, seqs), "down", after(ids, mlp_oth), [*act, *hid, downs_of(wb), downs_of(wb_oth)],
        [sds((seqs, block, width), F32), sds((seqs, block, width), BF16)],
        us=0.5,
    )
    def own_side(turn):
        mlp_own = call(
            partial(mlp_grads_kernel, seqs, rows), "mlp_grads_own", turn,
            [*nm, *columns(gu, 0), *columns(act, 0), cot0, cot2], apart, scratch=grad_scratch, us=50,
        )
        if stepwise():
            near, far = slice(0, half_dp // 2), slice(half_dp // 2, half_dp)
            crossing_in = [add(mlp_own[1][half], mlp_rcv[1][half]) for half in (far, near)]
            crossing, later = (flip(x, "dp", 1) for x in crossing_in)
            far_sum = add(mlp_own[0][far], mlp_rcv[0][far], crossing)
            mlp_pieces = [ring(far_sum[k], "dp", 2 * (k + half_dp // 2)) for k in range(half_dp - half_dp // 2)]
            rest = mlp_own[0][near], mlp_rcv[0][near], later
        else:
            crossing = jnp.moveaxis(mlp_own[0] + mlp_rcv, 0, 1).reshape(width, 2 * ff)
            crossing_in, mlp_pieces, rest = [crossing], sum_rows_any(crossing), ()
        return crossing_in, crossing, mlp_pieces, rest

    gh, gh_full, gq_own, gq_rcv, gq = ([] for _ in range(5))

    turn = after(ids, keep_out)
    for s in range(seqs):
        got = call(
            hidden_back_kernel, f"hidden_back{s}", turn,
            [gnm[s], gnm_rcv[s], unit[s], inv[s], part(cot0, s), part(cot2, s), gains],
            [sds((2, block, width), F32), sds((2, block, width), BF16)],
            scratch=[pltpu.VMEM((2, block, width), BF16)],
        )
        gh.append(got[0])
        gh_rcv = flip(got[1], "tensor", 1)
        if s == 0:
            crossing_in, crossing, mlp_pieces, rest = own_side(after(ids, gh[0], wa_oth))
        wide = sds((2, block, 3 * qw + 64), BF16)
        got = call(
            attend_back_kernel, f"attend_back{s}", after(ids, *crossing_in) if s == 0 else after(ids, crossing),
            [starts[s : s + 1], *qkv[s], got[1], gh_rcv, outs_of(wb)],
            [wide, wide, sds((length, 3 * qw), BF16), sds((length, width), BF16)],
            scratch=[
                pltpu.VMEM((heads, length, HD), BF16), pltpu.VMEM((heads, length // block, HD, block), BF16),
                pltpu.VMEM((heads, 1, length), F32), pltpu.VMEM((length, HD), F32), pltpu.VMEM((length, HD), F32),
                *[pltpu.VMEM((heads, length, HD), BF16)] * 3,
            ],
            us=7,
        )
        gq_own.append(got[0])
        gq_rcv.append(flip(got[1], "tensor", 1))
        gq.append(got[2])
        gh_full.append(got[3])
        turn = after(ids, got[0])
    attn_own = call(
        partial(attn_grads_kernel, seqs, rows), "attn_grads", ids, [*normed, *gq, *gh_full, *mix_n],
        attn_apart, scratch=[pltpu.VMEM((width, 4 * qw), F32)], us=8,
    )
    if stepwise():
        mlp_pieces = sum_ring(add(*together(*rest, attn_own[0])[:3])) + mlp_pieces
        attn_rcv = flip(attn_own[1], "dp", 1)
    both = sds((seqs, block, width), F32), sds((seqs, block, width), BF16)
    keep_in, send_in = call(
        partial(normed_back_kernel, seqs), "normed_back", after(ids, attn_own[0]), [*gq_own, *gq_rcv, wa, wa_oth],
        both, us=20,
    )
    in_rcv = flip(send_in, "tensor", 2)
    out_rcv = flip(after(send_out, gh[-1]), "tensor", 2)
    output = keep_out + out_rcv.astype(F32)

    if stepwise():
        attn_pieces = sum_ring(add(after(attn_own[0], keep_in, *mlp_pieces), attn_rcv))
    else:
        attn_pieces = sum_rows_any(attn_own[0])
    grad_up, grad_down, gain_mlp_part = call(
        partial(finish_mlp_kernel, len(mlp_pieces)), "finish_mlp", after(ids, keep_in), [*mlp_pieces, w_up],
        [sds((rows, ff), F32), sds((ff, rows), F32), sds((rows, 128), F32)],
    )
    input_grad = call(
        partial(input_back_kernel, seqs), "input_back", after(ids, output), [*gh, keep_in, in_rcv, tok0, gains],
        [sds((seqs, block, width), F32)],
        us=3,
    )[0]

    grad_query, grad_key, grad_value, grad_out, gain_attn_part = call(
        partial(finish_attn_kernel, len(attn_pieces)), "finish_attn", after(ids, input_grad, grad_up),
        [*attn_pieces, w_query, w_key, w_value],
        [sds((rows, qw), F32)] * 3 + [sds((qw, rows), F32), sds((rows, 128), F32)],
    )

    gain_parts = jnp.stack([gain_attn_part[:, 0], gain_mlp_part[:, 0]])
    gain_parts = sum([gain_parts] + [flip(gain_parts, "tensor", bits) for bits in (1, 2, 3)])
    return (
        output, input_grad, grad_query, grad_key, grad_value, grad_out, grad_up, grad_down,
        gain_parts[0] / gain_attn.astype(F32), gain_parts[1] / gain_mlp.astype(F32),
    )


def solution(mesh):
    in_specs = (
        P("dp", "tensor", None),
        P("dp", None),
        P("dp", "tensor"),
        P("dp", "tensor"),
        P("dp", "tensor"),
        P("tensor", "dp"),
        P("dp", "tensor"),
        P("tensor", "dp"),
        P("dp"),
        P("dp"),
        P("dp", "tensor", None),
    )
    out_specs = (
        P("dp", "tensor", None),
        P("dp", "tensor", None),
        P("dp", "tensor"),
        P("dp", "tensor"),
        P("dp", "tensor"),
        P("tensor", "dp"),
        P("dp", "tensor"),
        P("tensor", "dp"),
        P("dp"),
        P("dp"),
    )
    return jax.shard_map(body, mesh=mesh, in_specs=in_specs, out_specs=out_specs, check_vma=False)
```

```python
import math
from functools import partial

import jax
import jax.numpy as jnp
import numpy as np
from jax import lax
from jax.experimental import pallas as pl
from jax.experimental.pallas import tpu as pltpu
from jax.sharding import PartitionSpec as P

HD = 64
LANES = 128
DOC_MOST = 512
EPS = 1e-05
NEGATIVE = -1e30
COST = 5e8
SCALE = HD ** (-0.5)
GELU_A = 0.7978845608028654
GELU_B = 0.044715
F32 = jnp.float32
BF16 = jnp.bfloat16


def nn(left, right):
    return lax.dot_general(left, right, (((1,), (0,)), ((), ())), preferred_element_type=F32)


def nt(left, right):
    return lax.dot_general(left, right, (((1,), (1,)), ((), ())), preferred_element_type=F32)


def tn(left, right):
    return lax.dot_general(left, right, (((0,), (0,)), ((), ())), preferred_element_type=F32)


def unit_of(rows):
    center = rows - jnp.mean(rows, axis=-1, keepdims=True)
    spread = jnp.mean(center * center, axis=-1, keepdims=True)
    inverse = lax.rsqrt(spread + EPS)
    return center * inverse, inverse


def norm_back(incoming, unit, inverse, gain):
    scaled = incoming * gain
    return inverse * (
        scaled
        - jnp.mean(scaled, axis=-1, keepdims=True)
        - unit * jnp.mean(scaled * unit, axis=-1, keepdims=True)
    )


def nbytes_of(shapes):
    return sum(math.prod(x.shape) * jnp.dtype(x.dtype).itemsize for x in shapes)


def part(array, index):
    return array, index, jax.eval_shape(lambda x: x[index], array).shape


def call(body, name, ids, ins, outs, scratch=(), us=2.0):
    ins = [x if isinstance(x, tuple) else (x, None, x.shape) for x in ins]
    arrays = []
    for x, _, _ in ins:
        if not any(x is y for y in arrays):
            arrays.append(x)
    place = [next(i for i, y in enumerate(arrays) if y is x) for x, _, _ in ins]
    count, made = len(arrays), len(outs)

    def kernel(ids_ref, *refs):
        sources, targets, own = refs[:count], refs[count : count + made], refs[count + made :]
        loads = []
        for i, (_, index, _) in enumerate(ins):
            source = sources[place[i]]
            loads.append(source if index is None else source.at[index])
        body(ids_ref, *loads, *targets, *own)

    return pl.pallas_call(
        kernel,
        name=name,
        out_shape=tuple(outs),
        in_specs=[pl.BlockSpec(memory_space=pltpu.SMEM)] + [pl.BlockSpec(memory_space=pltpu.VMEM)] * count,
        out_specs=tuple(pl.BlockSpec(memory_space=pltpu.VMEM) for _ in outs),
        scratch_shapes=list(scratch),
        compiler_params=pltpu.CompilerParams(vmem_limit_bytes=nbytes_of(scratch) + (10 << 20)),
        cost_estimate=pl.CostEstimate(flops=int(us * COST), transcendentals=0, bytes_accessed=0),
    )(ids, *arrays)


def sds(shape, dtype):
    return jax.ShapeDtypeStruct(shape, dtype)


def gains_kernel(lane, ids, wa, out):
    out[...] = wa[:, lane : lane + 128].astype(F32).T[64:72, :]


def place_kernel(rows, ids, *refs):
    pieces, out = refs[:-1], refs[-1]
    for k, piece in enumerate(pieces):
        out[pl.ds(pl.multiple_of(ids[1 + k] * rows, 16), rows), :] = piece[...]


def place_chunks_kernel(rows, ids, *refs):
    pieces, out = refs[:-1], refs[-1]
    step = out.shape[2]
    for k, piece in enumerate(pieces):
        here = pl.ds(pl.multiple_of(ids[1 + k] * rows, 16), rows)
        for c in range(out.shape[0]):
            out[c, here, :] = piece[:, c * step : (c + 1) * step]


def place_gains_kernel(rows, lane, ids, *refs):
    out, gains = refs[-2:]
    place_kernel(rows, ids, *refs[:-1])
    gains_kernel(lane, ids, out, gains)


def attend_kernel(
    ids, tok0, tok1, tok2, tok3, wa, gains, start,
    normed_o, q_o, k_o, v_o, q_t_o, k_t_o, mix_t_o, mix_n_o, mix_own_o, mix_oth_o, lse_o, v_t, tok,
):
    t = ids[0]
    heads = mix_t_o.shape[0]
    width = heads * HD
    block = tok0.shape[0]
    gain = gains[0:1, :]
    for j, one in enumerate((tok0, tok1, tok2, tok3)):
        tok[j] = one[...]

    def normalize(j, carry):
        unit, _ = unit_of(tok[j].astype(F32))
        place = pl.multiple_of((t ^ j) * block, block)
        normed_o[pl.ds(place, block), :] = (unit * gain).astype(BF16)
        return carry

    lax.fori_loop(0, 4, normalize, 0)
    count = normed_o.shape[0] // block

    def projections(g, carry):
        here = pl.ds(pl.multiple_of(g * block, block), block)
        got = nn(normed_o[here, :], wa[:, : 3 * width])
        for i, (plain, turned) in enumerate(((q_o, q_t_o), (k_o, k_t_o), (v_o, v_t))):
            one = got[:, i * width : (i + 1) * width]
            if i == 0:
                one = one * SCALE
            other = one.T.astype(BF16)
            one = one.astype(BF16)
            for h in range(heads):
                plain[h, here, :] = one[:, h * HD : (h + 1) * HD]
                turned[h, g] = other[h * HD : (h + 1) * HD, :]
        return carry

    lax.fori_loop(0, count, projections, 0)

    def head(h, carry):
        for g in range(count):
            low = max(0, g - (DOC_MOST + block - 2) // block)
            here = slice(g * block, (g + 1) * block)
            keys = slice(low * block, (g + 1) * block)
            span = (g + 1 - low) * block
            row = lax.broadcasted_iota(jnp.int32, (span, block), 0) + low * block
            column = lax.broadcasted_iota(jnp.int32, (span, block), 1) + g * block
            valid = (row <= column) & (row >= start[0:1, here])
            scores = jnp.where(valid, nn(k_o[h, keys, :], q_t_o[h, g]), NEGATIVE)
            highest = jnp.max(scores, axis=0, keepdims=True)
            weights = jnp.exp(scores - highest)
            total = jnp.sum(weights, axis=0, keepdims=True)
            values = jnp.concatenate([v_t[h, i] for i in range(low, g + 1)], axis=1)
            mix_t_o[h, :, here] = (nn(values, weights.astype(BF16)) / total).astype(BF16)
            lse_o[h, :, here] = highest + jnp.log(total)
        return carry

    lax.fori_loop(0, heads, head, 0)
    for g in range(count):
        here = slice(g * block, (g + 1) * block)
        mixed = jnp.concatenate([mix_t_o[h, :, here] for h in range(heads)], axis=0)
        mix_n_o[here, :] = mixed.astype(F32).T.astype(BF16)
    for j in range(4):
        place = pl.multiple_of((t ^ j) * block, block)
        target = mix_own_o if j % 2 == 0 else mix_oth_o
        target[j // 2] = mix_n_o[pl.ds(place, block), :]


def mlp_kernel(
    ids, tok0, tok2, mix_own, mix_c, wo, wo_oth, mix_y, mix_cy, gains, cot0, cot2, wup, wd, wup_oth, wd_oth,
    unit_o, inv_o, hid_o, nm_o, act_o, gu_o, gnm_o, tok, cot,
):
    gain = gains[1:2, :]
    block = tok0.shape[0]
    qw = mix_own.shape[2]
    chunks = wup.shape[0] // 2
    wo, wo_oth = beside(wo, slice(None)), beside(wo_oth, slice(None))
    tok[0], tok[1] = tok0[...], tok2[...]
    cot[0], cot[1] = cot0[...], cot2[...]

    def half_rows(k, carry):
        here = pl.ds(pl.multiple_of(k * block, block), block)
        hidden = tok[k].astype(F32) + (
            (nt(mix_own[k], wo[:, :qw]) + nt(mix_c[k], wo_oth[:, :qw]))
            + (nt(mix_y[1 - k], wo[:, qw:]) + nt(mix_cy[1 - k], wo_oth[:, qw:]))
        )
        hid_o[k] = hidden
        unit, inverse = unit_of(hidden)
        unit_o[here, :] = unit
        inv_o[here, :] = jnp.broadcast_to(inverse, (block, 128))
        nm_o[here, :] = (unit * gain).astype(BF16)
        back = None
        for base, up_w, down_w in ((0, wup, wd), (chunks, wup_oth, wd_oth)):
            for c in range(chunks):
                up = jnp.concatenate([up_w[2 * c], up_w[2 * c + 1]], axis=1)
                u = nn(nm_o[here, :], up)
                ga = nn(cot[k], jnp.concatenate([down_w[2 * c], down_w[2 * c + 1]], axis=1))
                square = u * u
                th = jnp.tanh(GELU_A * (u + GELU_B * square * u))
                half = 0.5 * (1.0 + th)
                slope = half + 0.5 * u * (1.0 - th * th) * (GELU_A + (3.0 * GELU_A * GELU_B) * square)
                act_o[base + c, here, :] = (u * half).astype(BF16)
                gu = (ga * slope).astype(BF16)
                gu_o[base + c, here, :] = gu
                more = nt(gu, up)
                back = more if back is None else back + more
        gnm_o[k] = back.astype(BF16)
        return carry

    lax.fori_loop(0, 2, half_rows, 0)


def beside(array, here):
    return jnp.concatenate([array[c, here, :] for c in range(array.shape[0])], axis=1)


def down_kernel(seqs, ids, *refs):
    act, hid = refs[:seqs], refs[seqs : 2 * seqs]
    wd, wd_oth, keep_o, send_o = refs[2 * seqs :]
    block = hid[0].shape[1]
    weights = jnp.concatenate([beside(wd, slice(None)), beside(wd_oth, slice(None))], axis=1)
    for s in range(seqs):
        for k in (1, 0):
            got = nt(beside(act[s], slice(k * block, (k + 1) * block)), weights)
            if k == 0:
                keep_o[s] = hid[s][0] + got
            else:
                send_o[s] = got.astype(BF16)


def deal(ids, order, total, rows, cols, outs):
    if len(outs) == 1 and len(outs[0].shape) == 2:
        outs[0][:, cols] = total[...].astype(BF16)
        return
    at = 1 + order * (ids.shape[0] // 3)
    for out in outs:
        lead = out.shape[:-2]
        for k in range(math.prod(lead)):
            start = pl.multiple_of(ids[at] * rows, 8)
            got = total[pl.ds(start, rows), :].astype(BF16)
            if len(lead) == 2:
                out[k // lead[1], k % lead[1], :, cols] = got
            else:
                out[k, :, cols] = got
            at += 1


def deal_chunk(ids, total, rows, at_chunk, outs):
    if len(outs) == 1 and len(outs[0].shape) == 3:
        outs[0][at_chunk] = total[...].astype(BF16)
        return
    at = 1 + ids.shape[0] // 3
    for out in outs:
        lead = out.shape[:-3]
        for k in range(math.prod(lead)):
            start = pl.multiple_of(ids[at] * rows, 8)
            got = total[pl.ds(start, rows), :].astype(BF16)
            if len(lead) == 2:
                out[k // lead[1], k % lead[1], at_chunk] = got
            else:
                out[k, at_chunk] = got
            at += 1


def mlp_grads_kernel(seqs, rows, ids, *refs):
    nm, gu, act = (refs[i * seqs : (i + 1) * seqs] for i in range(3))
    cot0, cot2 = refs[3 * seqs : 3 * seqs + 2]
    outs, total = refs[3 * seqs + 2 : -1], refs[-1]
    block = cot0.shape[1]
    chunks = gu[0].shape[0]
    one, two = slice(0, block), slice(block, 2 * block)

    def chunk(c, carry):
        got = None
        for s in range(seqs):
            more = tn(nm[s][...], gu[s][c])
            got = more if got is None else got + more
        total[...] = got
        deal_chunk(ids, total, rows, c, outs)
        got = None
        for s in range(seqs):
            more = tn(cot0[s], act[s][c, one, :]) + tn(cot2[s], act[s][c, two, :])
            got = more if got is None else got + more
        total[...] = got
        deal_chunk(ids, total, rows, chunks + c, outs)
        return carry

    lax.fori_loop(0, chunks, chunk, 0)


def hidden_back_kernel(ids, gnm_own, gnm_rcv, unit, inv, cot0, cot2, gains, gh_o, ghb_o, cot):
    gain = gains[1:2, :]
    block = cot0.shape[0]
    cot[0], cot[1] = cot0[...], cot2[...]

    def half_rows(k, carry):
        here = pl.ds(pl.multiple_of(k * block, block), block)
        incoming = gnm_own[k].astype(F32) + gnm_rcv[1 - k].astype(F32)
        gh = cot[k].astype(F32) + norm_back(incoming, unit[here, :], inv[here, 0:1], gain)
        gh_o[k] = gh
        ghb_o[k] = gh.astype(BF16)
        return carry

    lax.fori_loop(0, 2, half_rows, 0)


def attend_back_kernel(
    ids, start, q_n, k_n, v_n, q_t, k_t, mix_t, lse, gh_own, gh_rcv, wo, gq_own_o, gq_oth_o, gq_o, gh_o,
    gm_n, gm_t, inner, acc_k, acc_v, gq_n, gk_n, gv_n,
):
    t = ids[0]
    heads, length = q_n.shape[0], q_n.shape[1]
    width = heads * HD
    block = gh_own.shape[1]
    count = length // block
    out_w = beside(wo, slice(None))[:, :width]
    for j in range(4):
        place = pl.multiple_of((t ^ j) * block, block)
        gh_o[pl.ds(place, block), :] = (gh_own if j % 2 == 0 else gh_rcv)[j // 2]
    for g in range(count):
        here = slice(g * block, (g + 1) * block)
        grad_mix = nn(gh_o[here, :], out_w).astype(BF16)
        turned = grad_mix.astype(F32).T
        for h in range(heads):
            lanes = slice(h * HD, (h + 1) * HD)
            gm_n[h, here, :] = grad_mix[:, lanes]
            gm_t[h, g] = turned[lanes, :].astype(BF16)
            both = turned[lanes, :] * mix_t[h, :, here].astype(F32)
            inner[h, :, here] = jnp.sum(both, axis=0, keepdims=True)

    def head(h, carry):
        acc_k[...] = jnp.zeros_like(acc_k)
        acc_v[...] = jnp.zeros_like(acc_v)
        for g in range(count):
            low = max(0, g - (DOC_MOST + block - 2) // block)
            here = slice(g * block, (g + 1) * block)
            keys = slice(low * block, (g + 1) * block)
            span = (g + 1 - low) * block
            row = lax.broadcasted_iota(jnp.int32, (span, block), 0) + low * block
            column = lax.broadcasted_iota(jnp.int32, (span, block), 1) + g * block
            valid = (row <= column) & (row >= start[0:1, here])
            scores = jnp.where(valid, nn(k_n[h, keys, :], q_t[h, g]), NEGATIVE)
            probs = jnp.exp(scores - lse[h, :, here])
            grad_probs = nn(v_n[h, keys, :], gm_t[h, g])
            grad_scores = (probs * (grad_probs - inner[h, :, here])).astype(BF16)
            acc_k[keys, :] += nn(grad_scores, q_n[h, here, :])
            acc_v[keys, :] += nn(probs.astype(BF16), gm_n[h, here, :])
            turned = jnp.concatenate([k_t[h, i] for i in range(low, g + 1)], axis=1)
            gq_n[h, here, :] = (nn(turned, grad_scores) * SCALE).T.astype(BF16)
        gk_n[h] = acc_k[...].astype(BF16)
        gv_n[h] = acc_v[...].astype(BF16)
        return carry

    lax.fori_loop(0, heads, head, 0)
    for i, part_n in enumerate((gq_n, gk_n, gv_n)):
        for h in range(heads):
            gq_o[:, i * width + h * HD : i * width + (h + 1) * HD] = part_n[h]
    for j in range(4):
        place = pl.multiple_of((t ^ j) * block, block)
        target = gq_own_o if j % 2 == 0 else gq_oth_o
        target[j // 2, :, : 3 * width] = gq_o[pl.ds(place, block), :]


def attn_grads_kernel(seqs, rows, ids, *refs):
    normed, gq, gh, mix = (refs[i * seqs : (i + 1) * seqs] for i in range(4))
    outs, total = refs[4 * seqs : -1], refs[-1]
    wide = gq[0].shape[1]
    step = 256

    def chunk(c, carry):
        here = pl.ds(pl.multiple_of(c * step, step), step)
        for cols, left, right in ((slice(0, wide), normed, gq), (slice(wide, None), gh, mix)):
            got = None
            for s in range(seqs):
                more = tn(left[s][:, here], right[s][...])
                got = more if got is None else got + more
            total[here, cols] = got
        return carry

    lax.fori_loop(0, total.shape[0] // step, chunk, 0)
    deal(ids, 1, total, rows, slice(None), outs)


def normed_back_kernel(seqs, ids, *refs):
    gq_own, gq_rcv = refs[:seqs], refs[seqs : 2 * seqs]
    wa_own, wa_oth, keep_o, send_o = refs[2 * seqs :]
    width = gq_own[0].shape[2] // 128 * 128 - 64
    for k in (1, 0):
        for s in range(seqs):
            own, rcv = gq_own[s][k, :, :width], gq_rcv[s][k, :, :width]
            got = nt(own, wa_own[:, :width]) + nt(rcv, wa_oth[:, :width])
            if k == 0:
                keep_o[s] = got
            else:
                send_o[s] = got.astype(BF16)


def finish_attn_kernel(count, ids, *refs):
    pieces, weights, outs = refs[:count], refs[count : count + 3], refs[count + 3 :]
    total = pieces[0][...].astype(F32)
    for piece in pieces[1:]:
        total = total + piece[...].astype(F32)
    width = outs[0].shape[1]
    gain = None
    for i in range(3):
        grad = total[:, i * width : (i + 1) * width]
        outs[i][...] = grad
        line = jnp.sum(grad * weights[i][...].astype(F32), axis=1, keepdims=True)
        gain = line if gain is None else gain + line
    outs[3][...] = total[:, 3 * width :].T
    outs[4][...] = jnp.broadcast_to(gain, outs[4].shape)


def finish_mlp_kernel(count, ids, *refs):
    pieces, weight, outs = refs[:count], refs[count], refs[count + 1 :]
    total = pieces[0][...].astype(F32)
    for piece in pieces[1:]:
        total = total + piece[...].astype(F32)
    if len(total.shape) == 3:
        total = jnp.concatenate([total[c] for c in range(total.shape[0])], axis=1)
    width = outs[0].shape[1]
    outs[0][...] = total[:, :width]
    outs[1][...] = total[:, width:].T
    gain = jnp.sum(total[:, :width] * weight[...].astype(F32), axis=1, keepdims=True)
    outs[2][...] = jnp.broadcast_to(gain, outs[2].shape)


def input_back_kernel(seqs, ids, *refs):
    gh = refs[:seqs]
    keep, rcv, tok0, gains, out = refs[seqs:]
    for s in range(seqs):
        unit, inverse = unit_of(tok0[s].astype(F32))
        incoming = keep[s] + rcv[s].astype(F32)
        out[s] = gh[s][0] + norm_back(incoming, unit, inverse, gains[0:1, :])


def flip(array, axis, bit):
    size = lax.axis_size(axis)
    return lax.ppermute(array, axis, [(i, i ^ bit) for i in range(size)])


def ring(array, axis, step):
    size = lax.axis_size(axis)
    return lax.ppermute(array, axis, [(i, (i + step) % size) for i in range(size)])


def after(value, *others):
    return lax.optimization_barrier((value, *others))[0]


def stepwise():
    return lax.axis_size("dp") == 8


def together(*values):
    return lax.optimization_barrier(values)


def places():
    size, wide = lax.axis_size("dp"), lax.axis_size("tensor")
    table = np.zeros((size * wide, 1 + 3 * size), np.int32)
    for me in range(size):
        half = range(size // 2)
        for low, line in (
            (0, [(me - 2 * k) % size for k in half]),
            (1, [(me + 2 * k) % size for k in half]),
            (2, [me % 2 + 2 * k for k in half]),
        ):
            for t in range(wide):
                row = table[me * wide + t]
                row[0] = t
                row[1 + low * size : 1 + (low + 1) * size] = line + [p ^ 1 for p in line]
    return lax.dynamic_index_in_dim(jnp.asarray(table), lax.axis_index(("dp", "tensor")), 0, keepdims=False)


def add(*blocks):
    return sum(block.astype(F32) for block in blocks).astype(BF16)


def sum_far(total):
    size = lax.axis_size("dp")
    groups = [[2 * k + low for k in range(size // 2)] for low in range(2)]
    got = lax.all_to_all(total, "dp", split_axis=0, concat_axis=0, tiled=True, axis_index_groups=groups)
    return [got[k] for k in range(size // 2)]


def sum_ring(total):
    return [total[0]] + [ring(total[r], "dp", 2 * r) for r in range(1, total.shape[0])]


def sum_rows_any(grads):
    size = lax.axis_size("dp")
    blocks = grads.reshape(size, -1, grads.shape[1])
    arrived = lax.all_to_all(blocks, "dp", split_axis=0, concat_axis=0, tiled=True)
    return [arrived.astype(F32).sum(axis=0)]


def body(
    tokens, segment_ids, w_query, w_key, w_value, w_out, w_up, w_down, gain_attn, gain_mlp, cotangent
):
    seqs, block, width = tokens.shape
    length = segment_ids.shape[1]
    qw = w_query.shape[1]
    ff = w_up.shape[1]
    rows = w_query.shape[0]
    size = lax.axis_size("dp")
    heads = qw // HD
    ids = places()
    act_rows = 2 * block

    gain_pair = jnp.stack([gain_attn, gain_mlp], axis=1)
    pack_a = jnp.concatenate(
        [w_query, w_key, w_value, jnp.pad(gain_pair, ((0, 0), (0, 62)))], axis=1
    )
    lane = 3 * qw - 64
    shape_a, shape_g = sds((width, 3 * qw + 64), BF16), sds((8, width), F32)
    out_turned = w_out.T
    tok0, cot0 = tokens, cotangent
    starts = jnp.sum(
        (segment_ids[:, None, :] < segment_ids[:, :, None]).astype(jnp.int32), axis=-1
    )
    if stepwise():
        out_y, tok1 = flip(after(out_turned, ids), "tensor", 2), flip(tok0, "tensor", 1)
        a_p, a_m, a_x0 = ring(pack_a, "dp", 2), ring(pack_a, "dp", -2), flip(pack_a, "dp", 1)
        tok2 = flip(after(tok0, out_y), "tensor", 2)
        pack_b = jnp.concatenate([out_turned, out_y, w_up, w_down.T], axis=1)
        a_p, a_m, a_x0, tok1, pack_b, starts = together(a_p, a_m, a_x0, tok1, pack_b, starts)
        a_2, a_xp, a_xm, b_p = ring(a_p, "dp", 2), flip(a_p, "dp", 1), flip(a_m, "dp", 1), ring(pack_b, "dp", 2)
        a_2, a_xp, a_xm, tok2, b_p = together(a_2, a_xp, a_xm, tok2, b_p)
        a_x2, tok3 = flip(a_2, "dp", 1), flip(tok2, "tensor", 1)
        cot2 = flip(after(cot0, tok2), "tensor", 2)
        a_x2, tok3 = together(a_x2, tok3)
        b_2, b_m, b_x0 = ring(b_p, "dp", 2), ring(after(pack_b, a_x2), "dp", -2), flip(after(pack_b, b_p), "dp", 1)
        wa, gains = call(
            partial(place_gains_kernel, rows, lane), "place_a", ids,
            [pack_a, a_p, a_2, a_m, a_x0, a_xp, a_x2, a_xm], [shape_a, shape_g],
        )
        b_xp = flip(after(b_p, wa), "dp", 1)
        start_turn = after(ids, wa)
    else:
        out_y = flip(out_turned, "tensor", 2)
        pack_b = jnp.concatenate([out_turned, out_y, w_up, w_down.T], axis=1)
        tok1, tok2, cot2 = flip(tok0, "tensor", 1), flip(tok0, "tensor", 2), flip(cot0, "tensor", 2)
        tok3 = flip(tok2, "tensor", 1)
        wa = lax.all_gather(pack_a, "dp", axis=0, tiled=True)
        gains = call(partial(gains_kernel, lane), "gains", ids, [wa], [shape_g])[0]
        wb = lax.all_gather(pack_b, "dp", axis=0, tiled=True)
        wb = jnp.moveaxis(wb.reshape(width, -1, LANES), 1, 0)
        start_turn = ids

    def cut(array, low, count):
        return part(array, (slice(None), pl.ds(low, count)))

    out_chunks, ff_chunks = 2 * qw // LANES, ff // LANES

    def outs_of(array):
        return part(array, slice(0, out_chunks))

    def ups_of(array):
        return part(array, slice(out_chunks, out_chunks + ff_chunks))

    def downs_of(array):
        return part(array, slice(out_chunks + ff_chunks, out_chunks + 2 * ff_chunks))

    heads_n, heads_t = sds((heads, length, HD), BF16), sds((heads, length // block, HD, block), BF16)
    chunks = ff // 256
    normed, qkv, mix_n, mix_own, mix_c, mix_y, mix_cy = ([] for _ in range(7))
    turn = start_turn
    for s in range(seqs):
        got = call(
            attend_kernel, f"attend{s}", turn,
            [*(part(x, s) for x in (tok0, tok1, tok2, tok3)), wa, gains, starts[s : s + 1]],
            [
                sds((length, width), BF16), heads_n, heads_n, heads_n, heads_t, heads_t,
                sds((heads, HD, length), BF16), sds((length, qw), BF16),
                sds((2, block, qw), BF16), sds((2, block, qw), BF16), sds((heads, 1, length), F32),
            ],
            scratch=[
                pltpu.VMEM((heads, length // block, HD, block), BF16), pltpu.VMEM((4, block, width), BF16),
            ],
            us=11,
        )
        normed.append(got[0])
        qkv.append([*got[1:7], got[10]])
        mix_n.append(got[7])
        mix_own.append(got[8])
        own, oth = together(mix_own[s], got[9], *mix_y, *mix_c, *mix_cy)[:2]
        mix_y.append(flip(own, "tensor", 2))
        mix_c.append(flip(oth, "tensor", 1))
        mix_cy.append(flip(oth, "tensor", 3))
        turn = after(ids, mix_own[s])
        if s == 0 and stepwise():
            b_2, b_m, b_x0, b_xp = together(b_2, b_m, b_x0, b_xp, cot2, mix_own[0])[:4]
            b_x2, b_xm = flip(b_2, "dp", 1), flip(b_m, "dp", 1)
            turn = after(ids, b_2)
    if stepwise():
        wb = call(
            partial(place_chunks_kernel, rows), "place_b", after(ids, mix_own[-1], mix_y[0], mix_c[0], mix_cy[0]),
            [pack_b, b_p, b_2, b_m, b_x0, b_xp, b_x2, b_xm],
            [sds((2 * (qw + ff) // LANES, width, LANES), BF16)],
        )[0]
    wb_oth = flip(wb, "tensor", 1)

    unit, inv, hid, nm, act, gu, gnm, gnm_rcv = ([] for _ in range(8))
    turn = ids
    for s in range(seqs):
        got = call(
            mlp_kernel, f"mlp{s}", turn,
            [
                part(tok0, s), part(tok2, s), mix_own[s], mix_c[s], outs_of(wb), outs_of(wb_oth), mix_y[s], mix_cy[s],
                gains, part(cot0, s), part(cot2, s), ups_of(wb), downs_of(wb), ups_of(wb_oth), downs_of(wb_oth),
            ],
            [
                sds((act_rows, width), F32), sds((act_rows, 128), F32), sds((2, block, width), F32),
                sds((act_rows, width), BF16), *[sds((2 * chunks, act_rows, 256), BF16)] * 2,
                sds((2, block, width), BF16),
            ],
            scratch=[pltpu.VMEM((2, block, width), BF16)] * 2,
            us=9,
        )
        for target, value in zip((unit, inv, hid, nm, act, gu, gnm), got):
            target.append(value)
        gnm_rcv.append(flip(after(gnm[s], mix_y[-1], mix_c[-1], mix_cy[-1]), "tensor", 2))
        if s == 0:
            wa_oth = flip(after(wa, gnm[0]), "tensor", 1)
        turn = after(ids, gnm[s])

    half_dp = size // 2
    if stepwise():
        apart = [sds((half_dp, 2 * chunks, rows, 256), BF16)] * 2
        paired = [sds((2, half_dp, 2 * chunks, rows, 256), BF16)]
        attn_apart = [sds((half_dp, rows, 4 * qw), BF16)] * 2
    else:
        apart = paired = [sds((2 * chunks, width, 256), BF16)]
        attn_apart = [sds((width, 4 * qw), BF16)]
    grad_scratch = [pltpu.VMEM((width, 256), F32)]

    def columns(arrays, h):
        return [part(x, slice(h * chunks, (h + 1) * chunks)) for x in arrays]

    mlp_oth = call(
        partial(mlp_grads_kernel, seqs, rows), "mlp_grads_oth", after(ids, gnm[-1]),
        [*nm, *columns(gu, 1), *columns(act, 1), cot0, cot2], paired, scratch=grad_scratch, us=0.5,
    )[0]
    mlp_rcv = flip(mlp_oth, "tensor", 1)
    keep_out, send_out = call(
        partial(down_kernel, seqs), "down", after(ids, mlp_oth), [*act, *hid, downs_of(wb), downs_of(wb_oth)],
        [sds((seqs, block, width), F32), sds((seqs, block, width), BF16)],
        us=0.5,
    )
    def own_side(turn):
        mlp_own = call(
            partial(mlp_grads_kernel, seqs, rows), "mlp_grads_own", turn,
            [*nm, *columns(gu, 0), *columns(act, 0), cot0, cot2], apart, scratch=grad_scratch, us=50,
        )
        if stepwise():
            near, far = slice(0, half_dp // 2), slice(half_dp // 2, half_dp)
            crossing_in = [add(mlp_own[1][half], mlp_rcv[1][half]) for half in (far, near)]
            crossing, later = (flip(x, "dp", 1) for x in crossing_in)
            far_sum = add(mlp_own[0][far], mlp_rcv[0][far], crossing)
            mlp_pieces = [ring(far_sum[k], "dp", 2 * (k + half_dp // 2)) for k in range(half_dp - half_dp // 2)]
            rest = mlp_own[0][near], mlp_rcv[0][near], later
        else:
            crossing = jnp.moveaxis(mlp_own[0] + mlp_rcv, 0, 1).reshape(width, 2 * ff)
            crossing_in, mlp_pieces, rest = [crossing], sum_rows_any(crossing), ()
        return crossing_in, crossing, mlp_pieces, rest

    gh, gh_full, gq_own, gq_rcv, gq = ([] for _ in range(5))

    turn = after(ids, keep_out)
    for s in range(seqs):
        got = call(
            hidden_back_kernel, f"hidden_back{s}", turn,
            [gnm[s], gnm_rcv[s], unit[s], inv[s], part(cot0, s), part(cot2, s), gains],
            [sds((2, block, width), F32), sds((2, block, width), BF16)],
            scratch=[pltpu.VMEM((2, block, width), BF16)],
        )
        gh.append(got[0])
        gh_rcv = flip(got[1], "tensor", 1)
        if s == 0:
            crossing_in, crossing, mlp_pieces, rest = own_side(after(ids, gh[0], wa_oth))
        wide = sds((2, block, 3 * qw + 64), BF16)
        got = call(
            attend_back_kernel, f"attend_back{s}", after(ids, *crossing_in) if s == 0 else after(ids, crossing),
            [starts[s : s + 1], *qkv[s], got[1], gh_rcv, outs_of(wb)],
            [wide, wide, sds((length, 3 * qw), BF16), sds((length, width), BF16)],
            scratch=[
                pltpu.VMEM((heads, length, HD), BF16), pltpu.VMEM((heads, length // block, HD, block), BF16),
                pltpu.VMEM((heads, 1, length), F32), pltpu.VMEM((length, HD), F32), pltpu.VMEM((length, HD), F32),
                *[pltpu.VMEM((heads, length, HD), BF16)] * 3,
            ],
            us=7,
        )
        gq_own.append(got[0])
        gq_rcv.append(flip(got[1], "tensor", 1))
        gq.append(got[2])
        gh_full.append(got[3])
        turn = after(ids, got[0])
    attn_own = call(
        partial(attn_grads_kernel, seqs, rows), "attn_grads", ids, [*normed, *gq, *gh_full, *mix_n],
        attn_apart, scratch=[pltpu.VMEM((width, 4 * qw), F32)], us=8,
    )
    if stepwise():
        near_sum = add(*together(*rest, attn_own[0])[:3])
        attn_rcv = flip(attn_own[1], "dp", 1)
    both = sds((seqs, block, width), F32), sds((seqs, block, width), BF16)
    keep_in, send_in = call(
        partial(normed_back_kernel, seqs), "normed_back", after(ids, attn_own[0]), [*gq_own, *gq_rcv, wa, wa_oth],
        both, us=20,
    )
    in_rcv = flip(send_in, "tensor", 2)
    if stepwise():
        mlp_pieces = sum_ring(after(near_sum, keep_in)) + mlp_pieces
    out_rcv = flip(after(send_out, gh[-1]), "tensor", 2)
    output = keep_out + out_rcv.astype(F32)

    if stepwise():
        attn_pieces = sum_ring(add(after(attn_own[0], keep_in, *mlp_pieces), attn_rcv))
    else:
        attn_pieces = sum_rows_any(attn_own[0])
    grad_up, grad_down, gain_mlp_part = call(
        partial(finish_mlp_kernel, len(mlp_pieces)), "finish_mlp", after(ids, keep_in), [*mlp_pieces, w_up],
        [sds((rows, ff), F32), sds((ff, rows), F32), sds((rows, 128), F32)],
    )
    input_grad = call(
        partial(input_back_kernel, seqs), "input_back", after(ids, output), [*gh, keep_in, in_rcv, tok0, gains],
        [sds((seqs, block, width), F32)],
        us=3,
    )[0]

    grad_query, grad_key, grad_value, grad_out, gain_attn_part = call(
        partial(finish_attn_kernel, len(attn_pieces)), "finish_attn", after(ids, input_grad, grad_up),
        [*attn_pieces, w_query, w_key, w_value],
        [sds((rows, qw), F32)] * 3 + [sds((qw, rows), F32), sds((rows, 128), F32)],
    )

    gain_parts = jnp.stack([gain_attn_part[:, 0], gain_mlp_part[:, 0]])
    gain_parts = sum([gain_parts] + [flip(gain_parts, "tensor", bits) for bits in (1, 2, 3)])
    return (
        output, input_grad, grad_query, grad_key, grad_value, grad_out, grad_up, grad_down,
        gain_parts[0] / gain_attn.astype(F32), gain_parts[1] / gain_mlp.astype(F32),
    )


def solution(mesh):
    in_specs = (
        P("dp", "tensor", None),
        P("dp", None),
        P("dp", "tensor"),
        P("dp", "tensor"),
        P("dp", "tensor"),
        P("tensor", "dp"),
        P("dp", "tensor"),
        P("tensor", "dp"),
        P("dp"),
        P("dp"),
        P("dp", "tensor", None),
    )
    out_specs = (
        P("dp", "tensor", None),
        P("dp", "tensor", None),
        P("dp", "tensor"),
        P("dp", "tensor"),
        P("dp", "tensor"),
        P("tensor", "dp"),
        P("dp", "tensor"),
        P("tensor", "dp"),
        P("dp"),
        P("dp"),
    )
    return jax.shard_map(body, mesh=mesh, in_specs=in_specs, out_specs=out_specs, check_vma=False)
```

```python
import math
from functools import partial

import jax
import jax.numpy as jnp
import numpy as np
from jax import lax
from jax.experimental import pallas as pl
from jax.experimental.pallas import tpu as pltpu
from jax.sharding import PartitionSpec as P

HD = 64
LANES = 128
DOC_MOST = 512
EPS = 1e-05
NEGATIVE = -1e30
COST = 5e8
SCALE = HD ** (-0.5)
GELU_A = 0.7978845608028654
GELU_B = 0.044715
F32 = jnp.float32
BF16 = jnp.bfloat16


def nn(left, right):
    return lax.dot_general(left, right, (((1,), (0,)), ((), ())), preferred_element_type=F32)


def nt(left, right):
    return lax.dot_general(left, right, (((1,), (1,)), ((), ())), preferred_element_type=F32)


def tn(left, right):
    return lax.dot_general(left, right, (((0,), (0,)), ((), ())), preferred_element_type=F32)


def unit_of(rows):
    center = rows - jnp.mean(rows, axis=-1, keepdims=True)
    spread = jnp.mean(center * center, axis=-1, keepdims=True)
    inverse = lax.rsqrt(spread + EPS)
    return center * inverse, inverse


def norm_back(incoming, unit, inverse, gain):
    scaled = incoming * gain
    return inverse * (
        scaled
        - jnp.mean(scaled, axis=-1, keepdims=True)
        - unit * jnp.mean(scaled * unit, axis=-1, keepdims=True)
    )


def nbytes_of(shapes):
    return sum(math.prod(x.shape) * jnp.dtype(x.dtype).itemsize for x in shapes)


def part(array, index):
    return array, index, jax.eval_shape(lambda x: x[index], array).shape


def call(body, name, ids, ins, outs, scratch=(), us=2.0):
    ins = [x if isinstance(x, tuple) else (x, None, x.shape) for x in ins]
    arrays = []
    for x, _, _ in ins:
        if not any(x is y for y in arrays):
            arrays.append(x)
    place = [next(i for i, y in enumerate(arrays) if y is x) for x, _, _ in ins]
    count, made = len(arrays), len(outs)

    def kernel(ids_ref, *refs):
        sources, targets, own = refs[:count], refs[count : count + made], refs[count + made :]
        loads = []
        for i, (_, index, _) in enumerate(ins):
            source = sources[place[i]]
            loads.append(source if index is None else source.at[index])
        body(ids_ref, *loads, *targets, *own)

    return pl.pallas_call(
        kernel,
        name=name,
        out_shape=tuple(outs),
        in_specs=[pl.BlockSpec(memory_space=pltpu.SMEM)] + [pl.BlockSpec(memory_space=pltpu.VMEM)] * count,
        out_specs=tuple(pl.BlockSpec(memory_space=pltpu.VMEM) for _ in outs),
        scratch_shapes=list(scratch),
        compiler_params=pltpu.CompilerParams(vmem_limit_bytes=nbytes_of(scratch) + (10 << 20)),
        cost_estimate=pl.CostEstimate(flops=int(us * COST), transcendentals=0, bytes_accessed=0),
    )(ids, *arrays)


def sds(shape, dtype):
    return jax.ShapeDtypeStruct(shape, dtype)


def gains_kernel(lane, ids, wa, out):
    out[...] = wa[:, lane : lane + 128].astype(F32).T[64:72, :]


def place_kernel(rows, ids, *refs):
    pieces, out = refs[:-1], refs[-1]
    for k, piece in enumerate(pieces):
        out[pl.ds(pl.multiple_of(ids[1 + k] * rows, 16), rows), :] = piece[...]


def place_chunks_kernel(rows, ids, *refs):
    pieces, out = refs[:-1], refs[-1]
    step = out.shape[2]
    for k, piece in enumerate(pieces):
        here = pl.ds(pl.multiple_of(ids[1 + k] * rows, 16), rows)
        for c in range(out.shape[0]):
            out[c, here, :] = piece[:, c * step : (c + 1) * step]


def place_gains_kernel(rows, lane, ids, *refs):
    out, gains = refs[-2:]
    place_kernel(rows, ids, *refs[:-1])
    gains_kernel(lane, ids, out, gains)


def attend_kernel(
    ids, tok0, tok1, tok2, tok3, wa, gains, start,
    normed_o, q_o, k_o, v_o, q_t_o, k_t_o, mix_t_o, mix_n_o, mix_own_o, mix_oth_o, lse_o, v_t, tok,
):
    t = ids[0]
    heads = mix_t_o.shape[0]
    width = heads * HD
    block = tok0.shape[0]
    gain = gains[0:1, :]
    for j, one in enumerate((tok0, tok1, tok2, tok3)):
        tok[j] = one[...]

    def normalize(j, carry):
        unit, _ = unit_of(tok[j].astype(F32))
        place = pl.multiple_of((t ^ j) * block, block)
        normed_o[pl.ds(place, block), :] = (unit * gain).astype(BF16)
        return carry

    lax.fori_loop(0, 4, normalize, 0)
    count = normed_o.shape[0] // block

    def projections(g, carry):
        here = pl.ds(pl.multiple_of(g * block, block), block)
        got = nn(normed_o[here, :], wa[:, : 3 * width])
        for i, (plain, turned) in enumerate(((q_o, q_t_o), (k_o, k_t_o), (v_o, v_t))):
            one = got[:, i * width : (i + 1) * width]
            if i == 0:
                one = one * SCALE
            other = one.T.astype(BF16)
            one = one.astype(BF16)
            for h in range(heads):
                plain[h, here, :] = one[:, h * HD : (h + 1) * HD]
                turned[h, g] = other[h * HD : (h + 1) * HD, :]
        return carry

    lax.fori_loop(0, count, projections, 0)

    def head(h, carry):
        for g in range(count):
            low = max(0, g - (DOC_MOST + block - 2) // block)
            here = slice(g * block, (g + 1) * block)
            keys = slice(low * block, (g + 1) * block)
            span = (g + 1 - low) * block
            row = lax.broadcasted_iota(jnp.int32, (span, block), 0) + low * block
            column = lax.broadcasted_iota(jnp.int32, (span, block), 1) + g * block
            valid = (row <= column) & (row >= start[0:1, here])
            scores = jnp.where(valid, nn(k_o[h, keys, :], q_t_o[h, g]), NEGATIVE)
            highest = jnp.max(scores, axis=0, keepdims=True)
            weights = jnp.exp(scores - highest)
            total = jnp.sum(weights, axis=0, keepdims=True)
            values = jnp.concatenate([v_t[h, i] for i in range(low, g + 1)], axis=1)
            mix_t_o[h, :, here] = (nn(values, weights.astype(BF16)) / total).astype(BF16)
            lse_o[h, :, here] = highest + jnp.log(total)
        return carry

    lax.fori_loop(0, heads, head, 0)
    for g in range(count):
        here = slice(g * block, (g + 1) * block)
        mixed = jnp.concatenate([mix_t_o[h, :, here] for h in range(heads)], axis=0)
        mix_n_o[here, :] = mixed.astype(F32).T.astype(BF16)
    for j in range(4):
        place = pl.multiple_of((t ^ j) * block, block)
        target = mix_own_o if j % 2 == 0 else mix_oth_o
        target[j // 2] = mix_n_o[pl.ds(place, block), :]


def mlp_kernel(
    ids, tok0, tok2, mix_own, mix_c, wo, wo_oth, mix_y, mix_cy, gains, cot0, cot2, wup, wd, wup_oth, wd_oth,
    unit_o, inv_o, hid_o, nm_o, act_o, gu_o, gnm_o, tok, cot,
):
    gain = gains[1:2, :]
    block = tok0.shape[0]
    qw = mix_own.shape[2]
    chunks = wup.shape[0] // 2
    wo, wo_oth = beside(wo, slice(None)), beside(wo_oth, slice(None))
    tok[0], tok[1] = tok0[...], tok2[...]
    cot[0], cot[1] = cot0[...], cot2[...]

    def half_rows(k, carry):
        here = pl.ds(pl.multiple_of(k * block, block), block)
        hidden = tok[k].astype(F32) + (
            (nt(mix_own[k], wo[:, :qw]) + nt(mix_c[k], wo_oth[:, :qw]))
            + (nt(mix_y[1 - k], wo[:, qw:]) + nt(mix_cy[1 - k], wo_oth[:, qw:]))
        )
        hid_o[k] = hidden
        unit, inverse = unit_of(hidden)
        unit_o[here, :] = unit
        inv_o[here, :] = jnp.broadcast_to(inverse, (block, 128))
        nm_o[here, :] = (unit * gain).astype(BF16)
        back = None
        for base, up_w, down_w in ((0, wup, wd), (chunks, wup_oth, wd_oth)):
            for c in range(chunks):
                up = jnp.concatenate([up_w[2 * c], up_w[2 * c + 1]], axis=1)
                u = nn(nm_o[here, :], up)
                ga = nn(cot[k], jnp.concatenate([down_w[2 * c], down_w[2 * c + 1]], axis=1))
                square = u * u
                th = jnp.tanh(GELU_A * (u + GELU_B * square * u))
                half = 0.5 * (1.0 + th)
                slope = half + 0.5 * u * (1.0 - th * th) * (GELU_A + (3.0 * GELU_A * GELU_B) * square)
                act_o[base + c, here, :] = (u * half).astype(BF16)
                gu = (ga * slope).astype(BF16)
                gu_o[base + c, here, :] = gu
                more = nt(gu, up)
                back = more if back is None else back + more
        gnm_o[k] = back.astype(BF16)
        return carry

    lax.fori_loop(0, 2, half_rows, 0)


def beside(array, here):
    return jnp.concatenate([array[c, here, :] for c in range(array.shape[0])], axis=1)


def down_kernel(seqs, ids, *refs):
    act, hid = refs[:seqs], refs[seqs : 2 * seqs]
    wd, wd_oth, keep_o, send_o = refs[2 * seqs :]
    block = hid[0].shape[1]
    weights = jnp.concatenate([beside(wd, slice(None)), beside(wd_oth, slice(None))], axis=1)
    for s in range(seqs):
        for k in (1, 0):
            got = nt(beside(act[s], slice(k * block, (k + 1) * block)), weights)
            if k == 0:
                keep_o[s] = hid[s][0] + got
            else:
                send_o[s] = got.astype(BF16)


def deal(ids, order, total, rows, cols, outs):
    if len(outs) == 1 and len(outs[0].shape) == 2:
        outs[0][:, cols] = total[...].astype(BF16)
        return
    at = 1 + order * (ids.shape[0] // 3)
    for out in outs:
        lead = out.shape[:-2]
        for k in range(math.prod(lead)):
            start = pl.multiple_of(ids[at] * rows, 8)
            got = total[pl.ds(start, rows), :].astype(BF16)
            if len(lead) == 2:
                out[k // lead[1], k % lead[1], :, cols] = got
            else:
                out[k, :, cols] = got
            at += 1


def deal_chunk(ids, total, rows, at_chunk, outs):
    if len(outs) == 1 and len(outs[0].shape) == 3:
        outs[0][at_chunk] = total[...].astype(BF16)
        return
    at = 1 + ids.shape[0] // 3
    for out in outs:
        lead = out.shape[:-3]
        for k in range(math.prod(lead)):
            start = pl.multiple_of(ids[at] * rows, 8)
            got = total[pl.ds(start, rows), :].astype(BF16)
            if len(lead) == 2:
                out[k // lead[1], k % lead[1], at_chunk] = got
            else:
                out[k, at_chunk] = got
            at += 1


def mlp_grads_kernel(seqs, rows, ids, *refs):
    nm, gu, act = (refs[i * seqs : (i + 1) * seqs] for i in range(3))
    cot0, cot2 = refs[3 * seqs : 3 * seqs + 2]
    outs, total = refs[3 * seqs + 2 : -1], refs[-1]
    block = cot0.shape[1]
    chunks = gu[0].shape[0]
    one, two = slice(0, block), slice(block, 2 * block)

    def chunk(c, carry):
        got = None
        for s in range(seqs):
            more = tn(nm[s][...], gu[s][c])
            got = more if got is None else got + more
        total[...] = got
        deal_chunk(ids, total, rows, c, outs)
        got = None
        for s in range(seqs):
            more = tn(cot0[s], act[s][c, one, :]) + tn(cot2[s], act[s][c, two, :])
            got = more if got is None else got + more
        total[...] = got
        deal_chunk(ids, total, rows, chunks + c, outs)
        return carry

    lax.fori_loop(0, chunks, chunk, 0)


def hidden_back_kernel(ids, gnm_own, gnm_rcv, unit, inv, cot0, cot2, gains, gh_o, ghb_o, cot):
    gain = gains[1:2, :]
    block = cot0.shape[0]
    cot[0], cot[1] = cot0[...], cot2[...]

    def half_rows(k, carry):
        here = pl.ds(pl.multiple_of(k * block, block), block)
        incoming = gnm_own[k].astype(F32) + gnm_rcv[1 - k].astype(F32)
        gh = cot[k].astype(F32) + norm_back(incoming, unit[here, :], inv[here, 0:1], gain)
        gh_o[k] = gh
        ghb_o[k] = gh.astype(BF16)
        return carry

    lax.fori_loop(0, 2, half_rows, 0)


def attend_back_kernel(
    ids, start, q_n, k_n, v_n, q_t, k_t, mix_t, lse, gh_own, gh_rcv, wo, gq_own_o, gq_oth_o, gq_o, gh_o,
    gm_n, gm_t, inner, acc_k, acc_v, gq_n, gk_n, gv_n,
):
    t = ids[0]
    heads, length = q_n.shape[0], q_n.shape[1]
    width = heads * HD
    block = gh_own.shape[1]
    count = length // block
    out_w = beside(wo, slice(None))[:, :width]
    for j in range(4):
        place = pl.multiple_of((t ^ j) * block, block)
        gh_o[pl.ds(place, block), :] = (gh_own if j % 2 == 0 else gh_rcv)[j // 2]
    for g in range(count):
        here = slice(g * block, (g + 1) * block)
        grad_mix = nn(gh_o[here, :], out_w).astype(BF16)
        turned = grad_mix.astype(F32).T
        for h in range(heads):
            lanes = slice(h * HD, (h + 1) * HD)
            gm_n[h, here, :] = grad_mix[:, lanes]
            gm_t[h, g] = turned[lanes, :].astype(BF16)
            both = turned[lanes, :] * mix_t[h, :, here].astype(F32)
            inner[h, :, here] = jnp.sum(both, axis=0, keepdims=True)

    def head(h, carry):
        acc_k[...] = jnp.zeros_like(acc_k)
        acc_v[...] = jnp.zeros_like(acc_v)
        for g in range(count):
            low = max(0, g - (DOC_MOST + block - 2) // block)
            here = slice(g * block, (g + 1) * block)
            keys = slice(low * block, (g + 1) * block)
            span = (g + 1 - low) * block
            row = lax.broadcasted_iota(jnp.int32, (span, block), 0) + low * block
            column = lax.broadcasted_iota(jnp.int32, (span, block), 1) + g * block
            valid = (row <= column) & (row >= start[0:1, here])
            scores = jnp.where(valid, nn(k_n[h, keys, :], q_t[h, g]), NEGATIVE)
            probs = jnp.exp(scores - lse[h, :, here])
            grad_probs = nn(v_n[h, keys, :], gm_t[h, g])
            grad_scores = (probs * (grad_probs - inner[h, :, here])).astype(BF16)
            acc_k[keys, :] += nn(grad_scores, q_n[h, here, :])
            acc_v[keys, :] += nn(probs.astype(BF16), gm_n[h, here, :])
            turned = jnp.concatenate([k_t[h, i] for i in range(low, g + 1)], axis=1)
            gq_n[h, here, :] = (nn(turned, grad_scores) * SCALE).T.astype(BF16)
        gk_n[h] = acc_k[...].astype(BF16)
        gv_n[h] = acc_v[...].astype(BF16)
        return carry

    lax.fori_loop(0, heads, head, 0)
    for i, part_n in enumerate((gq_n, gk_n, gv_n)):
        for h in range(heads):
            gq_o[:, i * width + h * HD : i * width + (h + 1) * HD] = part_n[h]
    for j in range(4):
        place = pl.multiple_of((t ^ j) * block, block)
        target = gq_own_o if j % 2 == 0 else gq_oth_o
        target[j // 2, :, : 3 * width] = gq_o[pl.ds(place, block), :]


def attn_grads_kernel(seqs, rows, ids, *refs):
    normed, gq, gh, mix = (refs[i * seqs : (i + 1) * seqs] for i in range(4))
    outs, total = refs[4 * seqs : -1], refs[-1]
    wide = gq[0].shape[1]
    step = 256

    def chunk(c, carry):
        here = pl.ds(pl.multiple_of(c * step, step), step)
        for cols, left, right in ((slice(0, wide), normed, gq), (slice(wide, None), gh, mix)):
            got = None
            for s in range(seqs):
                more = tn(left[s][:, here], right[s][...])
                got = more if got is None else got + more
            total[here, cols] = got
        return carry

    lax.fori_loop(0, total.shape[0] // step, chunk, 0)
    deal(ids, 1, total, rows, slice(None), outs)


def normed_back_kernel(seqs, ids, *refs):
    gq_own, gq_rcv = refs[:seqs], refs[seqs : 2 * seqs]
    wa_own, wa_oth, keep_o, send_o = refs[2 * seqs :]
    width = gq_own[0].shape[2] // 128 * 128 - 64
    for k in (1, 0):
        for s in range(seqs):
            own, rcv = gq_own[s][k, :, :width], gq_rcv[s][k, :, :width]
            got = nt(own, wa_own[:, :width]) + nt(rcv, wa_oth[:, :width])
            if k == 0:
                keep_o[s] = got
            else:
                send_o[s] = got.astype(BF16)


def finish_attn_kernel(count, ids, *refs):
    pieces, weights, outs = refs[:count], refs[count : count + 3], refs[count + 3 :]
    total = pieces[0][...].astype(F32)
    for piece in pieces[1:]:
        total = total + piece[...].astype(F32)
    width = outs[0].shape[1]
    gain = None
    for i in range(3):
        grad = total[:, i * width : (i + 1) * width]
        outs[i][...] = grad
        line = jnp.sum(grad * weights[i][...].astype(F32), axis=1, keepdims=True)
        gain = line if gain is None else gain + line
    outs[3][...] = total[:, 3 * width :].T
    outs[4][...] = jnp.broadcast_to(gain, outs[4].shape)


def finish_mlp_kernel(count, ids, *refs):
    pieces, weight, outs = refs[:count], refs[count], refs[count + 1 :]
    total = pieces[0][...].astype(F32)
    for piece in pieces[1:]:
        total = total + piece[...].astype(F32)
    if len(total.shape) == 3:
        total = jnp.concatenate([total[c] for c in range(total.shape[0])], axis=1)
    width = outs[0].shape[1]
    outs[0][...] = total[:, :width]
    outs[1][...] = total[:, width:].T
    gain = jnp.sum(total[:, :width] * weight[...].astype(F32), axis=1, keepdims=True)
    outs[2][...] = jnp.broadcast_to(gain, outs[2].shape)


def input_back_kernel(seqs, ids, *refs):
    gh = refs[:seqs]
    keep, rcv, tok0, gains, out = refs[seqs:]
    for s in range(seqs):
        unit, inverse = unit_of(tok0[s].astype(F32))
        incoming = keep[s] + rcv[s].astype(F32)
        out[s] = gh[s][0] + norm_back(incoming, unit, inverse, gains[0:1, :])


def flip(array, axis, bit):
    size = lax.axis_size(axis)
    return lax.ppermute(array, axis, [(i, i ^ bit) for i in range(size)])


def ring(array, axis, step):
    size = lax.axis_size(axis)
    return lax.ppermute(array, axis, [(i, (i + step) % size) for i in range(size)])


def after(value, *others):
    return lax.optimization_barrier((value, *others))[0]


def stepwise():
    return lax.axis_size("dp") == 8


def together(*values):
    return lax.optimization_barrier(values)


def places():
    size, wide = lax.axis_size("dp"), lax.axis_size("tensor")
    table = np.zeros((size * wide, 1 + 3 * size), np.int32)
    for me in range(size):
        half = range(size // 2)
        for low, line in (
            (0, [(me - 2 * k) % size for k in half]),
            (1, [(me + 2 * k) % size for k in half]),
            (2, [me % 2 + 2 * k for k in half]),
        ):
            for t in range(wide):
                row = table[me * wide + t]
                row[0] = t
                row[1 + low * size : 1 + (low + 1) * size] = line + [p ^ 1 for p in line]
    return lax.dynamic_index_in_dim(jnp.asarray(table), lax.axis_index(("dp", "tensor")), 0, keepdims=False)


def add(*blocks):
    return sum(block.astype(F32) for block in blocks).astype(BF16)


def sum_far(total):
    size = lax.axis_size("dp")
    groups = [[2 * k + low for k in range(size // 2)] for low in range(2)]
    got = lax.all_to_all(total, "dp", split_axis=0, concat_axis=0, tiled=True, axis_index_groups=groups)
    return [got[k] for k in range(size // 2)]


def sum_ring(total):
    return [total[0]] + [ring(total[r], "dp", 2 * r) for r in range(1, total.shape[0])]


def sum_rows_any(grads):
    size = lax.axis_size("dp")
    blocks = grads.reshape(size, -1, grads.shape[1])
    arrived = lax.all_to_all(blocks, "dp", split_axis=0, concat_axis=0, tiled=True)
    return [arrived.astype(F32).sum(axis=0)]


def body(
    tokens, segment_ids, w_query, w_key, w_value, w_out, w_up, w_down, gain_attn, gain_mlp, cotangent
):
    seqs, block, width = tokens.shape
    length = segment_ids.shape[1]
    qw = w_query.shape[1]
    ff = w_up.shape[1]
    rows = w_query.shape[0]
    size = lax.axis_size("dp")
    heads = qw // HD
    ids = places()
    act_rows = 2 * block

    gain_pair = jnp.stack([gain_attn, gain_mlp], axis=1)
    pack_a = jnp.concatenate(
        [w_query, w_key, w_value, jnp.pad(gain_pair, ((0, 0), (0, 62)))], axis=1
    )
    lane = 3 * qw - 64
    shape_a, shape_g = sds((width, 3 * qw + 64), BF16), sds((8, width), F32)
    out_turned = w_out.T
    tok0, cot0 = tokens, cotangent
    starts = jnp.sum(
        (segment_ids[:, None, :] < segment_ids[:, :, None]).astype(jnp.int32), axis=-1
    )
    if stepwise():
        out_y, tok1 = flip(after(out_turned, ids), "tensor", 2), flip(tok0, "tensor", 1)
        a_p, a_m, a_x0 = ring(pack_a, "dp", 2), ring(pack_a, "dp", -2), flip(pack_a, "dp", 1)
        tok2 = flip(after(tok0, out_y), "tensor", 2)
        pack_b = jnp.concatenate([out_turned, out_y, w_up, w_down.T], axis=1)
        a_p, a_m, a_x0, tok1, pack_b, starts = together(a_p, a_m, a_x0, tok1, pack_b, starts)
        a_2, a_xp, a_xm, b_p = ring(a_p, "dp", 2), flip(a_p, "dp", 1), flip(a_m, "dp", 1), ring(pack_b, "dp", 2)
        a_2, a_xp, a_xm, tok2, b_p = together(a_2, a_xp, a_xm, tok2, b_p)
        a_x2, tok3 = flip(a_2, "dp", 1), flip(tok2, "tensor", 1)
        cot2 = flip(after(cot0, tok2), "tensor", 2)
        a_x2, tok3 = together(a_x2, tok3)
        b_2, b_m, b_x0 = ring(b_p, "dp", 2), ring(after(pack_b, a_x2), "dp", -2), flip(after(pack_b, b_p), "dp", 1)
        wa, gains = call(
            partial(place_gains_kernel, rows, lane), "place_a", ids,
            [pack_a, a_p, a_2, a_m, a_x0, a_xp, a_x2, a_xm], [shape_a, shape_g],
        )
        b_xp = flip(after(b_p, wa), "dp", 1)
        start_turn = after(ids, wa)
    else:
        out_y = flip(out_turned, "tensor", 2)
        pack_b = jnp.concatenate([out_turned, out_y, w_up, w_down.T], axis=1)
        tok1, tok2, cot2 = flip(tok0, "tensor", 1), flip(tok0, "tensor", 2), flip(cot0, "tensor", 2)
        tok3 = flip(tok2, "tensor", 1)
        wa = lax.all_gather(pack_a, "dp", axis=0, tiled=True)
        gains = call(partial(gains_kernel, lane), "gains", ids, [wa], [shape_g])[0]
        wb = lax.all_gather(pack_b, "dp", axis=0, tiled=True)
        wb = jnp.moveaxis(wb.reshape(width, -1, LANES), 1, 0)
        start_turn = ids

    def cut(array, low, count):
        return part(array, (slice(None), pl.ds(low, count)))

    out_chunks, ff_chunks = 2 * qw // LANES, ff // LANES

    def outs_of(array):
        return part(array, slice(0, out_chunks))

    def ups_of(array):
        return part(array, slice(out_chunks, out_chunks + ff_chunks))

    def downs_of(array):
        return part(array, slice(out_chunks + ff_chunks, out_chunks + 2 * ff_chunks))

    heads_n, heads_t = sds((heads, length, HD), BF16), sds((heads, length // block, HD, block), BF16)
    chunks = ff // 256
    normed, qkv, mix_n, mix_own, mix_c, mix_y, mix_cy = ([] for _ in range(7))
    turn = start_turn
    for s in range(seqs):
        got = call(
            attend_kernel, f"attend{s}", turn,
            [*(part(x, s) for x in (tok0, tok1, tok2, tok3)), wa, gains, starts[s : s + 1]],
            [
                sds((length, width), BF16), heads_n, heads_n, heads_n, heads_t, heads_t,
                sds((heads, HD, length), BF16), sds((length, qw), BF16),
                sds((2, block, qw), BF16), sds((2, block, qw), BF16), sds((heads, 1, length), F32),
            ],
            scratch=[
                pltpu.VMEM((heads, length // block, HD, block), BF16), pltpu.VMEM((4, block, width), BF16),
            ],
            us=11,
        )
        normed.append(got[0])
        qkv.append([*got[1:7], got[10]])
        mix_n.append(got[7])
        mix_own.append(got[8])
        own, oth = together(mix_own[s], got[9], *mix_y, *mix_c, *mix_cy)[:2]
        mix_y.append(flip(own, "tensor", 2))
        mix_c.append(flip(oth, "tensor", 1))
        mix_cy.append(flip(oth, "tensor", 3))
        turn = after(ids, mix_own[s])
        if s == 0 and stepwise():
            b_2, b_m, b_x0, b_xp = together(b_2, b_m, b_x0, b_xp, cot2, mix_own[0])[:4]
            b_x2, b_xm = flip(b_2, "dp", 1), ring(b_x0, "dp", -2)
            turn = after(ids, b_2)
    if stepwise():
        wb = call(
            partial(place_chunks_kernel, rows), "place_b", after(ids, mix_own[-1], mix_y[0], mix_c[0], mix_cy[0]),
            [pack_b, b_p, b_2, b_m, b_x0, b_xp, b_x2, b_xm],
            [sds((2 * (qw + ff) // LANES, width, LANES), BF16)],
        )[0]
    wb_oth = flip(wb, "tensor", 1)

    unit, inv, hid, nm, act, gu, gnm, gnm_rcv = ([] for _ in range(8))
    turn = ids
    for s in range(seqs):
        got = call(
            mlp_kernel, f"mlp{s}", turn,
            [
                part(tok0, s), part(tok2, s), mix_own[s], mix_c[s], outs_of(wb), outs_of(wb_oth), mix_y[s], mix_cy[s],
                gains, part(cot0, s), part(cot2, s), ups_of(wb), downs_of(wb), ups_of(wb_oth), downs_of(wb_oth),
            ],
            [
                sds((act_rows, width), F32), sds((act_rows, 128), F32), sds((2, block, width), F32),
                sds((act_rows, width), BF16), *[sds((2 * chunks, act_rows, 256), BF16)] * 2,
                sds((2, block, width), BF16),
            ],
            scratch=[pltpu.VMEM((2, block, width), BF16)] * 2,
            us=9,
        )
        for target, value in zip((unit, inv, hid, nm, act, gu, gnm), got):
            target.append(value)
        gnm_rcv.append(flip(after(gnm[s], mix_y[-1], mix_c[-1], mix_cy[-1]), "tensor", 2))
        if s == 0:
            wa_oth = flip(after(wa, gnm[0]), "tensor", 1)
        turn = after(ids, gnm[s])

    half_dp = size // 2
    if stepwise():
        apart = [sds((half_dp, 2 * chunks, rows, 256), BF16)] * 2
        paired = [sds((2, half_dp, 2 * chunks, rows, 256), BF16)]
        attn_apart = [sds((half_dp, rows, 4 * qw), BF16)] * 2
    else:
        apart = paired = [sds((2 * chunks, width, 256), BF16)]
        attn_apart = [sds((width, 4 * qw), BF16)]
    grad_scratch = [pltpu.VMEM((width, 256), F32)]

    def columns(arrays, h):
        return [part(x, slice(h * chunks, (h + 1) * chunks)) for x in arrays]

    mlp_oth = call(
        partial(mlp_grads_kernel, seqs, rows), "mlp_grads_oth", after(ids, gnm[-1]),
        [*nm, *columns(gu, 1), *columns(act, 1), cot0, cot2], paired, scratch=grad_scratch, us=0.5,
    )[0]
    mlp_rcv = flip(mlp_oth, "tensor", 1)
    keep_out, send_out = call(
        partial(down_kernel, seqs), "down", after(ids, mlp_oth), [*act, *hid, downs_of(wb), downs_of(wb_oth)],
        [sds((seqs, block, width), F32), sds((seqs, block, width), BF16)],
        us=0.5,
    )
    def own_side(turn):
        mlp_own = call(
            partial(mlp_grads_kernel, seqs, rows), "mlp_grads_own", turn,
            [*nm, *columns(gu, 0), *columns(act, 0), cot0, cot2], apart, scratch=grad_scratch, us=50,
        )
        if stepwise():
            near, far = slice(0, half_dp // 2), slice(half_dp // 2, half_dp)
            crossing_in = [add(mlp_own[1][half], mlp_rcv[1][half]) for half in (far, near)]
            crossing, later = (flip(x, "dp", 1) for x in crossing_in)
            far_sum = add(mlp_own[0][far], mlp_rcv[0][far], crossing)
            mlp_pieces = [ring(far_sum[k], "dp", 2 * (k + half_dp // 2)) for k in range(half_dp - half_dp // 2)]
            rest = mlp_own[0][near], mlp_rcv[0][near], later
        else:
            crossing = jnp.moveaxis(mlp_own[0] + mlp_rcv, 0, 1).reshape(width, 2 * ff)
            crossing_in, mlp_pieces, rest = [crossing], sum_rows_any(crossing), ()
        return crossing_in, crossing, mlp_pieces, rest

    gh, gh_full, gq_own, gq_rcv, gq = ([] for _ in range(5))

    turn = after(ids, keep_out)
    for s in range(seqs):
        got = call(
            hidden_back_kernel, f"hidden_back{s}", turn,
            [gnm[s], gnm_rcv[s], unit[s], inv[s], part(cot0, s), part(cot2, s), gains],
            [sds((2, block, width), F32), sds((2, block, width), BF16)],
            scratch=[pltpu.VMEM((2, block, width), BF16)],
        )
        gh.append(got[0])
        gh_rcv = flip(got[1], "tensor", 1)
        if s == 0:
            crossing_in, crossing, mlp_pieces, rest = own_side(after(ids, gh[0], wa_oth))
        wide = sds((2, block, 3 * qw + 64), BF16)
        got = call(
            attend_back_kernel, f"attend_back{s}", after(ids, *crossing_in) if s == 0 else after(ids, crossing),
            [starts[s : s + 1], *qkv[s], got[1], gh_rcv, outs_of(wb)],
            [wide, wide, sds((length, 3 * qw), BF16), sds((length, width), BF16)],
            scratch=[
                pltpu.VMEM((heads, length, HD), BF16), pltpu.VMEM((heads, length // block, HD, block), BF16),
                pltpu.VMEM((heads, 1, length), F32), pltpu.VMEM((length, HD), F32), pltpu.VMEM((length, HD), F32),
                *[pltpu.VMEM((heads, length, HD), BF16)] * 3,
            ],
            us=7,
        )
        gq_own.append(got[0])
        gq_rcv.append(flip(got[1], "tensor", 1))
        gq.append(got[2])
        gh_full.append(got[3])
        turn = after(ids, got[0])
    attn_own = call(
        partial(attn_grads_kernel, seqs, rows), "attn_grads", ids, [*normed, *gq, *gh_full, *mix_n],
        attn_apart, scratch=[pltpu.VMEM((width, 4 * qw), F32)], us=8,
    )
    if stepwise():
        near_sum = add(*together(*rest, attn_own[0])[:3])
        attn_rcv = flip(attn_own[1], "dp", 1)
    both = sds((seqs, block, width), F32), sds((seqs, block, width), BF16)
    keep_in, send_in = call(
        partial(normed_back_kernel, seqs), "normed_back", after(ids, attn_own[0]), [*gq_own, *gq_rcv, wa, wa_oth],
        both, us=20,
    )
    in_rcv = flip(send_in, "tensor", 2)
    if stepwise():
        mlp_pieces = sum_ring(after(near_sum, keep_in)) + mlp_pieces
    out_rcv = flip(after(send_out, gh[-1]), "tensor", 2)
    output = keep_out + out_rcv.astype(F32)

    if stepwise():
        attn_pieces = sum_ring(add(after(attn_own[0], keep_in, *mlp_pieces), attn_rcv))
    else:
        attn_pieces = sum_rows_any(attn_own[0])
    grad_up, grad_down, gain_mlp_part = call(
        partial(finish_mlp_kernel, len(mlp_pieces)), "finish_mlp", after(ids, keep_in), [*mlp_pieces, w_up],
        [sds((rows, ff), F32), sds((ff, rows), F32), sds((rows, 128), F32)],
    )
    input_grad = call(
        partial(input_back_kernel, seqs), "input_back", after(ids, output), [*gh, keep_in, in_rcv, tok0, gains],
        [sds((seqs, block, width), F32)],
        us=3,
    )[0]

    grad_query, grad_key, grad_value, grad_out, gain_attn_part = call(
        partial(finish_attn_kernel, len(attn_pieces)), "finish_attn", after(ids, input_grad, grad_up),
        [*attn_pieces, w_query, w_key, w_value],
        [sds((rows, qw), F32)] * 3 + [sds((qw, rows), F32), sds((rows, 128), F32)],
    )

    gain_parts = jnp.stack([gain_attn_part[:, 0], gain_mlp_part[:, 0]])
    gain_parts = sum([gain_parts] + [flip(gain_parts, "tensor", bits) for bits in (1, 2, 3)])
    return (
        output, input_grad, grad_query, grad_key, grad_value, grad_out, grad_up, grad_down,
        gain_parts[0] / gain_attn.astype(F32), gain_parts[1] / gain_mlp.astype(F32),
    )


def solution(mesh):
    in_specs = (
        P("dp", "tensor", None),
        P("dp", None),
        P("dp", "tensor"),
        P("dp", "tensor"),
        P("dp", "tensor"),
        P("tensor", "dp"),
        P("dp", "tensor"),
        P("tensor", "dp"),
        P("dp"),
        P("dp"),
        P("dp", "tensor", None),
    )
    out_specs = (
        P("dp", "tensor", None),
        P("dp", "tensor", None),
        P("dp", "tensor"),
        P("dp", "tensor"),
        P("dp", "tensor"),
        P("tensor", "dp"),
        P("dp", "tensor"),
        P("tensor", "dp"),
        P("dp"),
        P("dp"),
    )
    return jax.shard_map(body, mesh=mesh, in_specs=in_specs, out_specs=out_specs, check_vma=False)
```
